32 devices in a mesh: shard: 4 (over z), context: 2 (over y), tensor: 4 (over x, core).
Axes of the slice: x: 2, y: 2, z: 4, core: 2. Of those that a mesh axis runs over, the one named last changes fastest.
Arguments:
- tokens: bfloat16 [16, 1024, 1024], P('shard', 'context'), may hold values from -6 to 6
- cotangent: bfloat16 [16, 1024, 1024], P('shard', 'context'), may hold values from -6 to 6
- adapter_index: int32 [16], P('shard'), may hold values from 0 to 7, as said below
- ln1_gain: float32 [1024], replicated, may hold values from 0.5 to 1.5
- ln1_bias: float32 [1024], replicated, may hold values from -1.5 to 1.5
- ln2_gain: float32 [1024], replicated, may hold values from 0.5 to 1.5
- ln2_bias: float32 [1024], replicated, may hold values from -1.5 to 1.5
- layer_scale: float32 [2, 1024], replicated, may hold values from 0.4 to 1.2
- w_qkv: bfloat16 [1024, 3, 1024], P(('shard', 'context'), None, 'tensor'), may hold values from -0.1875 to 0.1875
- w_proj: bfloat16 [1024, 1024], P(('shard', 'context'), 'tensor'), may hold values from -0.5 to 0.5
- w_fc1: bfloat16 [1024, 4096], P(('shard', 'context'), 'tensor'), may hold values from -0.1875 to 0.1875
- w_fc2: bfloat16 [1024, 4096], P(('shard', 'context'), 'tensor'), may hold values from -0.09375 to 0.09375
- down_in: bfloat16 [8, 4, 1024, 16], replicated, may hold values from -0.1875 to 0.1875
- qkv_up: bfloat16 [8, 3, 16, 1024], P(None, None, None, 'tensor'), may hold values from -1.5 to 1.5
- fc1_up: bfloat16 [8, 16, 4096], P(None, None, 'tensor'), may hold values from -1.5 to 1.5
- proj_down: bfloat16 [8, 1024, 16], P(None, 'tensor'), may hold values from -0.5 to 0.5
- fc2_down: bfloat16 [8, 4096, 16], P(None, 'tensor'), may hold values from -0.09375 to 0.09375
- out_up: bfloat16 [8, 2, 16, 1024], replicated, may hold values from -1.5 to 1.5
Outputs:
- result: bfloat16 [16, 1024, 1024], P('shard', 'context')
- input_grad: float32 [16, 1024, 1024], P('shard', 'context')
- down_in_grad: float32 [8, 4, 1024, 16], replicated
- qkv_up_grad: float32 [8, 3, 16, 1024], P(None, None, None, 'tensor')
- fc1_up_grad: float32 [8, 16, 4096], P(None, None, 'tensor')
- proj_down_grad: float32 [8, 1024, 16], P(None, 'tensor')
- fc2_down_grad: float32 [8, 4096, 16], P(None, 'tensor')
- out_up_grad: float32 [8, 2, 16, 1024], replicated
The draws below stay inside these ranges and needn't reach their ends.
Inputs may be any that keep to these rules, and one draw needn't show every extreme that they name: `adapter_index`: every adapter index is used by exactly 2 images.
All inputs are finite; a program needn't handle non-finite values.
Results may differ from the reference program's by a relative error of at most 0.015.
The reference program's roundings to bfloat16 on the way count: a program that leaves them out, or rounds other values in their place, can miss the bound.
Values may be sent and summed in bfloat16 or wider, within the bound.
No kernel may reach another device: no remote copies, remote signals or barrier semaphores. Data moves between devices by JAX's collectives and lax.ppermute only.
A program may use at most 256 MiB of HBM per device.

```python
import math
import jax
import jax.numpy as jnp
from jax import lax

D = 1024
HEADS = 16
HEAD_DIM = 64
FF = 4096
RANK = 16
ADAPTERS = 8
LENGTH = 1024
IMAGES = 16


def draw_adapter_index(key, part):
    repeated = jnp.arange(IMAGES, dtype=jnp.int32) % ADAPTERS
    return jax.random.permutation(jax.random.fold_in(key, 5), repeated)


def block_levels(rng, shape, cuts, least, high):
    def one(position, parts):
        heights = jax.random.uniform(jax.random.fold_in(jax.random.fold_in(rng, 6), position), (parts,), jnp.float32, least / len(cuts), high / len(cuts))
        return jnp.repeat(jnp.exp(heights), shape[position] // parts).reshape((-1,) + (1,) * (len(shape) - position - 1))

    loudness = one(*cuts[0])
    for cut in cuts[1:]:
        loudness = loudness * one(*cut)
    return loudness


def noise(stream_key, shape, deviation, most, pieces=(), kind=jnp.bfloat16):
    values = deviation * jax.random.normal(stream_key, shape, jnp.float32)
    if pieces:
        values = values * block_levels(stream_key, shape, pieces, -0.22, 0.18)
    return jnp.clip(values, -most, most).astype(kind)


def setup_inputs(seed: int = 0) -> dict:
    keys = jax.random.split(jax.random.key(seed), 19)
    return {
        "tokens": noise(keys[0], (IMAGES, LENGTH, D), 1.0, 6.0, ((0, 4), (1, 2))),
        "cotangent": noise(keys[1], (IMAGES, LENGTH, D), 1.0, 6.0, ((0, 4), (1, 2))),
        "adapter_index": draw_adapter_index(jax.random.fold_in(keys[18], 71), 0),
        "ln1_gain": jnp.clip(1.0 + 0.1 * jax.random.normal(keys[3], (D,), jnp.float32), 0.5, 1.5),
        "ln1_bias": noise(keys[4], (D,), 0.3, 1.5, (), jnp.float32),
        "ln2_gain": jnp.clip(1.0 + 0.1 * jax.random.normal(keys[5], (D,), jnp.float32), 0.5, 1.5),
        "ln2_bias": noise(keys[6], (D,), 0.3, 1.5, (), jnp.float32),
        "layer_scale": jnp.clip(jax.random.uniform(keys[7], (2, D), jnp.float32, 0.4, 1.2), 0.4, 1.2),
        "w_qkv": noise(keys[8], (D, 3, D), D ** -0.5, 0.1875, ((0, 8), (2, 4))),
        "w_proj": noise(keys[9], (D, D), (D // 8) ** -0.5, 0.5, ((0, 8), (1, 4))),
        "w_fc1": noise(keys[10], (D, FF), D ** -0.5, 0.1875, ((0, 8), (1, 4))),
        "w_fc2": noise(keys[11], (D, FF), FF ** -0.5, 0.09375, ((0, 8), (1, 4))),
        "down_in": noise(keys[12], (ADAPTERS, 4, D, RANK), D ** -0.5, 0.1875),
        "qkv_up": noise(keys[13], (ADAPTERS, 3, RANK, D), RANK ** -0.5, 1.5, ((3, 4),)),
        "fc1_up": noise(keys[14], (ADAPTERS, RANK, FF), RANK ** -0.5, 1.5, ((2, 4),)),
        "proj_down": noise(keys[15], (ADAPTERS, D, RANK), (D // 8) ** -0.5, 0.5, ((1, 4),)),
        "fc2_down": noise(keys[16], (ADAPTERS, FF, RANK), FF ** -0.5, 0.09375, ((1, 4),)),
        "out_up": noise(keys[17], (ADAPTERS, 2, RANK, D), RANK ** -0.5, 1.5),
    }


@jax.custom_vjp
def low(v):
    return lax.optimization_barrier(v.astype(jnp.bfloat16)).astype(jnp.float32)

@jax.custom_vjp
def low_back(v):
    return v

def low_keep(v):
    return (low(v), None)

def low_pass(kept, grad):
    return (grad,)

def back_keep(v):
    return (v, None)

def back_low(kept, grad):
    return (low(grad),)
low.defvjp(low_keep, low_pass)
low_back.defvjp(back_keep, back_low)
HIGHEST = lax.Precision.HIGHEST
eps_norm = 1e-06

def rounded_both(values):
    return low_back(low(values))

def layer_norm(values, norm_gain, norm_shift):
    centre = values - lax.optimization_barrier(jnp.mean(values, axis=-1, keepdims=True))
    spread = lax.optimization_barrier(jnp.mean(centre * centre, axis=-1, keepdims=True))
    return centre * lax.rsqrt(spread + eps_norm) * norm_gain + norm_shift

def one_image(picture, down_in, qkv_up, fc1_up, proj_down, fc2_down, out_up, adapter_id, frozen):
    ln1_gain, ln1_bias, ln2_gain, ln2_bias, layer_scale, w_qkv, w_proj, w_fc1, w_fc2 = frozen
    chosen_down = down_in[adapter_id]
    chosen_out = out_up[adapter_id]
    normed = low(layer_norm(picture, ln1_gain, ln1_bias))
    rank_qkv = rounded_both(jnp.einsum('ld,kdr->klr', normed, chosen_down[:3], precision=HIGHEST))
    projected = jnp.einsum('ld,dkc->klc', normed, w_qkv, precision=HIGHEST)
    projected = rounded_both(projected + jnp.einsum('klr,krc->klc', rank_qkv, qkv_up[adapter_id], precision=HIGHEST))
    queries = projected[0].reshape(LENGTH, HEADS, HEAD_DIM)
    key_heads = projected[1].reshape(LENGTH, HEADS, HEAD_DIM)
    value_heads = projected[2].reshape(LENGTH, HEADS, HEAD_DIM)
    scores = low_back(jnp.einsum('qhe,khe->hqk', queries, key_heads, precision=HIGHEST) * (1.0 / math.sqrt(HEAD_DIM)))
    probabilities = low(jax.nn.softmax(scores, axis=-1))
    mixed_heads = jnp.einsum('hqk,khe->qhe', probabilities, value_heads, precision=HIGHEST).reshape(LENGTH, D)
    mixed_heads = rounded_both(mixed_heads)
    proj_rank = rounded_both(jnp.dot(mixed_heads, proj_down[adapter_id], precision=HIGHEST))
    attn_out = low_back(jnp.dot(mixed_heads, w_proj.T, precision=HIGHEST) + jnp.dot(proj_rank, chosen_out[0], precision=HIGHEST))
    hidden_one = picture + layer_scale[0] * attn_out
    normed_two = low(layer_norm(hidden_one, ln2_gain, ln2_bias))
    fc1_rank = rounded_both(jnp.dot(normed_two, chosen_down[3], precision=HIGHEST))
    preact = low_back(jnp.dot(normed_two, w_fc1, precision=HIGHEST) + jnp.dot(fc1_rank, fc1_up[adapter_id], precision=HIGHEST))
    activation = low(jax.nn.gelu(preact, approximate=False))
    fc2_rank = rounded_both(jnp.dot(activation, fc2_down[adapter_id], precision=HIGHEST))
    branch = low_back(jnp.dot(activation, w_fc2.T, precision=HIGHEST) + jnp.dot(fc2_rank, chosen_out[1], precision=HIGHEST))
    return hidden_one + layer_scale[1] * branch

def reference(tokens, cotangent, adapter_index, ln1_gain, ln1_bias, ln2_gain, ln2_bias, layer_scale, w_qkv, w_proj, w_fc1, w_fc2, down_in, qkv_up, fc1_up, proj_down, fc2_down, out_up):
    frozen = tuple((array.astype(jnp.float32) for array in (ln1_gain, ln1_bias, ln2_gain, ln2_bias, layer_scale, w_qkv, w_proj, w_fc1, w_fc2)))
    adapters = tuple((array.astype(jnp.float32) for array in (down_in, qkv_up, fc1_up, proj_down, fc2_down, out_up)))
    starting = tuple((jnp.zeros(array.shape, jnp.float32) for array in adapters))

    def image_step(totals, current):
        picture, upstream, adapter_id = current

        def forward(picture_f, *adapter_f):
            return one_image(picture_f, *adapter_f, adapter_id, frozen)
        output, pullback = jax.vjp(forward, picture.astype(jnp.float32), *adapters)
        gradients = pullback(upstream.astype(jnp.float32))
        totals = tuple((running + added for running, added in zip(totals, gradients[1:])))
        return (totals, (output.astype(jnp.bfloat16), gradients[0]))
    totals, (result, input_grad) = lax.scan(image_step, starting, (tokens, cotangent, adapter_index))
    return (result, input_grad, totals[0], totals[1], totals[2], totals[3], totals[4], totals[5])
```

```python
import functools
import math

import jax
import jax.numpy as jnp
from jax import lax
from jax.experimental import pallas as pl
from jax.experimental.pallas import tpu as pltpu
from jax.sharding import PartitionSpec as P

HEAD_DIM = 64
PAIR = 2 * HEAD_DIM
EPS = 1e-06
LOG2E = math.log2(math.e)
SCORE = 1.0 / math.sqrt(HEAD_DIM)
F32 = jnp.float32
BF16 = jnp.bfloat16
NT = (((1,), (1,)), ((), ()))
TN = (((0,), (0,)), ((), ()))


def dot(a, b):
    return jnp.dot(a, b, preferred_element_type=F32)


def dot_nt(a, b):
    return lax.dot_general(a, b, NT, preferred_element_type=F32)


def dot_tn(a, b):
    return lax.dot_general(a, b, TN, preferred_element_type=F32)


def head_masks(rows):
    lane = lax.broadcasted_iota(jnp.int32, (rows, PAIR), 1)
    return lane < HEAD_DIM


def attend_kernel(block, x_ref, o_ref, lse_ref):
    rows = x_ref.shape[0]
    keys = x_ref[:, PAIR : 2 * PAIR]
    values = jnp.concatenate(
        [x_ref[:, 2 * PAIR : 3 * PAIR], jnp.ones((rows, PAIR), BF16)], axis=1
    )
    first = head_masks(block)

    def step(i, carry):
        at = pl.ds(pl.multiple_of(i * block, block), block)
        q = x_ref[at, :PAIR]
        outs = []
        logs = []
        for head in range(2):
            mine = first if head == 0 else jnp.logical_not(first)
            s = dot_nt(jnp.where(mine, q, jnp.zeros_like(q)), keys)
            peak = jnp.max(s, axis=1, keepdims=True)
            e = jnp.exp2((s - peak) * (SCORE * LOG2E))
            acc = dot(e.astype(BF16), values)
            total = acc[:, PAIR:]
            outs.append(acc[:, :PAIR] / total)
            logs.append(peak * (SCORE * LOG2E) + jnp.log2(total))
        o_ref[at, :] = jnp.where(first, outs[0], outs[1]).astype(BF16)
        lane = lax.broadcasted_iota(jnp.int32, (block, PAIR), 1)
        both = jnp.where(lane == 0, logs[0], logs[1])
        lse_ref[0, :, at] = jnp.transpose(both)[:8]
        return carry

    lax.fori_loop(0, rows // block, step, 0)


def attend(qkv):
    rows, width = qkv.shape
    pairs = width // (3 * PAIR)
    block = min(256, rows)
    return pl.pallas_call(
        functools.partial(attend_kernel, block),
        grid=(pairs,),
        in_specs=[pl.BlockSpec((rows, 3 * PAIR), lambda p: (0, p))],
        out_specs=[
            pl.BlockSpec((rows, PAIR), lambda p: (0, p)),
            pl.BlockSpec((1, 8, rows), lambda p: (p, 0, 0)),
        ],
        out_shape=[
            jax.ShapeDtypeStruct((rows, pairs * PAIR), BF16),
            jax.ShapeDtypeStruct((pairs, 8, rows), F32),
        ],
        cost_estimate=pl.CostEstimate(
            flops=pairs * 2 * rows * rows * 256 * 4,
            bytes_accessed=rows * pairs * PAIR * 8,
            transcendentals=pairs * 2 * rows * rows,
        ),
        name="attend",
    )(qkv)


def attend_back_kernel(block, x_ref, go_ref, o_ref, lse_ref, g_ref, gq_ref, d_ref):
    rows = x_ref.shape[0]
    first = head_masks(block)
    prod = o_ref[...].astype(F32) * go_ref[...].astype(F32)
    lane8 = lax.broadcasted_iota(jnp.int32, (8, PAIR), 1) // HEAD_DIM
    row8 = lax.broadcasted_iota(jnp.int32, (8, PAIR), 0)
    d_ref[...] = lax.dot_general(
        (lane8 == row8).astype(F32),
        prod,
        NT,
        preferred_element_type=F32,
        precision=lax.Precision.HIGHEST,
    )
    gq_ref[...] = jnp.zeros_like(gq_ref)

    def step(i, carry):
        at = pl.ds(pl.multiple_of(i * block, block), block)
        k = x_ref[at, PAIR : 2 * PAIR]
        v = x_ref[at, 2 * PAIR : 3 * PAIR]
        q = x_ref[:, :PAIR]
        go = go_ref[...]
        gks = []
        gvs = []
        gq = None
        for head in range(2):
            mine = first if head == 0 else jnp.logical_not(first)
            k_own = jnp.where(mine, k, jnp.zeros_like(k))
            v_own = jnp.where(mine, v, jnp.zeros_like(v))
            s = dot_nt(k_own, q)
            gp = dot_nt(v_own, go)
            p = jnp.exp2(s * (SCORE * LOG2E) - lse_ref[0, head : head + 1, :])
            gs = (p * (gp - d_ref[head : head + 1, :])).astype(BF16)
            gks.append(dot(gs, q))
            gvs.append(dot(p.astype(BF16), go))
            part = dot(jnp.transpose(k_own), gs)
            gq = part if gq is None else gq + part
        gq_ref[...] += gq
        g_ref[at, PAIR : 2 * PAIR] = (jnp.where(first, gks[0], gks[1]) * SCORE).astype(BF16)
        g_ref[at, 2 * PAIR : 3 * PAIR] = jnp.where(first, gvs[0], gvs[1]).astype(BF16)
        return carry

    lax.fori_loop(0, rows // block, step, 0)
    g_ref[:, :PAIR] = (jnp.transpose(gq_ref[...]) * SCORE).astype(BF16)


def attend_back(qkv, go, o, lse):
    rows, width = qkv.shape
    pairs = width // (3 * PAIR)
    block = min(256, rows)
    return pl.pallas_call(
        functools.partial(attend_back_kernel, block),
        grid=(pairs,),
        in_specs=[
            pl.BlockSpec((rows, 3 * PAIR), lambda p: (0, p)),
            pl.BlockSpec((rows, PAIR), lambda p: (0, p)),
            pl.BlockSpec((rows, PAIR), lambda p: (0, p)),
            pl.BlockSpec((1, 8, rows), lambda p: (p, 0, 0)),
        ],
        out_specs=pl.BlockSpec((rows, 3 * PAIR), lambda p: (0, p)),
        out_shape=jax.ShapeDtypeStruct((rows, width), BF16),
        scratch_shapes=[pltpu.VMEM((PAIR, rows), F32), pltpu.VMEM((8, rows), F32)],
        cost_estimate=pl.CostEstimate(
            flops=pairs * 2 * rows * rows * 256 * 10,
            bytes_accessed=rows * pairs * PAIR * 16,
            transcendentals=pairs * 2 * rows * rows,
        ),
        name="attend_back",
    )(qkv, go, o, lse)


def mlp_kernel(
    block,
    n_ref,
    gb_ref,
    f_ref,
    gm_ref,
    ft_ref,
    gmt_ref,
    w1_ref,
    w2_ref,
    u1_ref,
    d2_ref,
    branch_ref,
    gn_ref,
    m_ref,
    gf_ref,
    gf1_ref,
    gf2_ref,
):
    rows = n_ref.shape[0]

    @pl.when(pl.program_id(0) == 0)
    def _():
        branch_ref[...] = jnp.zeros_like(branch_ref)
        gn_ref[...] = jnp.zeros_like(gn_ref)
        m_ref[...] = jnp.zeros_like(m_ref)
        gf_ref[...] = jnp.zeros_like(gf_ref)

    gf1_ref[...] = jnp.zeros_like(gf1_ref)
    gf2_ref[...] = jnp.zeros_like(gf2_ref)

    def step(i, carry):
        at = pl.ds(pl.multiple_of(i * block, block), block)
        w1 = w1_ref[...]
        w2 = w2_ref[...]
        u1 = u1_ref[...]
        d2 = d2_ref[...]
        z = dot(n_ref[at, :], w1) + dot(f_ref[at, :], u1)
        cdf = 0.5 * (1.0 + lax.erf(z * (1.0 / math.sqrt(2.0))))
        a = (z * cdf).astype(BF16)
        slope = cdf + z * (jnp.exp2(z * z * (-0.5 * LOG2E)) * (1.0 / math.sqrt(2.0 * math.pi)))
        ga = dot(gb_ref[at, :], w2) + dot(gm_ref[at, :], d2)
        gz = (ga * slope).astype(BF16)
        branch_ref[at, :] += dot_nt(a, w2)
        m_ref[at, :] += dot_nt(a, d2)
        gn_ref[at, :] += dot_nt(gz, w1)
        gf_ref[at, :] += dot_nt(gz, u1)
        gf1_ref[...] += dot(ft_ref[:, at], gz)
        gf2_ref[...] += dot(gmt_ref[:, at], a)
        return carry

    lax.fori_loop(0, rows // block, step, 0)


def mlp(n, gb, f, gm, w1, w2, u1, d2):
    rows, model = n.shape
    hidden = w1.shape[1]
    rank = f.shape[1]
    chunk = min(512, hidden)
    block = min(256, rows)
    whole = lambda shape: pl.BlockSpec(shape, lambda j: (0, 0))
    part = lambda depth: pl.BlockSpec((depth, chunk), lambda j: (0, j))
    return pl.pallas_call(
        functools.partial(mlp_kernel, block),
        grid=(hidden // chunk,),
        in_specs=[
            whole((rows, model)),
            whole((rows, model)),
            whole((rows, rank)),
            whole((rows, rank)),
            whole((rank, rows)),
            whole((rank, rows)),
            part(model),
            part(model),
            part(rank),
            part(rank),
        ],
        out_specs=[
            whole((rows, model)),
            whole((rows, model)),
            whole((rows, rank)),
            whole((rows, rank)),
            part(rank),
            part(rank),
        ],
        out_shape=[
            jax.ShapeDtypeStruct((rows, model), F32),
            jax.ShapeDtypeStruct((rows, model), F32),
            jax.ShapeDtypeStruct((rows, rank), F32),
            jax.ShapeDtypeStruct((rows, rank), F32),
            jax.ShapeDtypeStruct((rank, hidden), F32),
            jax.ShapeDtypeStruct((rank, hidden), F32),
        ],
        cost_estimate=pl.CostEstimate(
            flops=12 * rows * model * hidden,
            bytes_accessed=4 * model * hidden + 12 * rows * model,
            transcendentals=2 * rows * hidden,
        ),
        name="mlp",
    )(n, gb, f, gm, f.T, gm.T, w1, w2, u1, d2)


def normalize(values, gain, shift):
    centre = values - jnp.mean(values, axis=-1, keepdims=True)
    inverse = lax.rsqrt(jnp.mean(centre * centre, axis=-1, keepdims=True) + EPS)
    unit = centre * inverse
    return unit * gain + shift, unit, inverse


def norm_back(grad, unit, inverse, gain):
    scaled = grad * gain
    centred = scaled - jnp.mean(scaled, axis=-1, keepdims=True)
    return inverse * (centred - unit * jnp.mean(scaled * unit, axis=-1, keepdims=True))


def per_device(
    sizes,
    tokens,
    cotangent,
    adapter_index,
    ln1_gain,
    ln1_bias,
    ln2_gain,
    ln2_bias,
    layer_scale,
    w_qkv,
    w_proj,
    w_fc1,
    w_fc2,
    down_in,
    qkv_up,
    fc1_up,
    proj_down,
    fc2_down,
    out_up,
):
    shards, contexts, tensors = sizes
    half = contexts // 2
    sides = tensors // 2
    images, rows, model = tokens.shape
    rank = down_in.shape[-1]
    depth = w_fc1.shape[0]
    width = w_proj.shape[1]
    hidden = w_fc1.shape[1]
    pairs = width // PAIR
    adapters = down_in.shape[0]
    shard = lax.axis_index("shard")
    context = lax.axis_index("context")
    tensor = lax.axis_index("tensor")
    side, core = tensor // 2, tensor % 2
    high = context // half

    ring = {
        "shard": [(i, (i + 1) % shards) for i in range(shards)],
        "context": [(i, (i + 1) % contexts) for i in range(contexts)],
        "tensor": [(i, (i + 2) % tensors) for i in range(tensors)],
    }
    count = {"shard": shards, "context": contexts, "tensor": sides}
    twin = [(i, i ^ 1) for i in range(tensors)]

    def hop(value, axis):
        return lax.ppermute(value, axis, ring[axis])

    def swap(value):
        return lax.ppermute(value, "tensor", twin)

    def around(value, axis):
        out = [value]
        for _ in range(count[axis] - 1):
            out.append(hop(out[-1], axis))
        return out

    to_owner = []
    to_home = []
    to_home_far = {far: [] for far in range(sides)}
    for c in range(contexts):
        for s in range(sides):
            for k in range(2):
                here = c * tensors + 2 * s + k
                source = 2 * (c % half) + k
                to_owner.append((source * tensors + 2 * s + c // half, here))
                for far in range(sides):
                    there = (s + far) % sides
                    to_home_far[far].append((here, source * tensors + 2 * there + c // half))
    plane = ("context", "tensor")

    def block_of(array, index):
        return lax.dynamic_index_in_dim(array, index, 0, keepdims=False)

    x_own = lax.ppermute(block_of(tokens, tensor), plane, to_owner)
    gy_own = lax.ppermute(block_of(cotangent, tensor), plane, to_owner)

    attn_own = jnp.concatenate(
        [w_qkv[:, j, p * PAIR : (p + 1) * PAIR] for p in range(pairs) for j in range(3)] + [w_proj],
        axis=1,
    )

    def gather_mid(value, first, last):
        parts = jnp.concatenate(around(value, first), axis=0)
        out = {}
        for i, item in enumerate(around(parts, "shard")):
            for j, got in enumerate(around(item, last)):
                for k in range(count[first]):
                    piece = got[k * depth : (k + 1) * depth]
                    far, near = (k, j) if first == "tensor" else (j, k)
                    out[(i, near, far)] = piece
        return out

    def gather_flat(value):
        line = around(value, "shard")
        out = {}
        middle = max(shards // 2, 1)
        for start, stop, first, last in (
            (0, middle, "tensor", "context"),
            (middle, shards, "context", "tensor"),
        ):
            if start == stop:
                continue
            parts = jnp.concatenate(line[start:stop], axis=0)
            for a, item in enumerate(around(parts, first)):
                for b, got in enumerate(around(item, last)):
                    far, near = (a, b) if first == "tensor" else (b, a)
                    for i in range(start, stop):
                        k = i - start
                        out[(i, near, far)] = got[k * depth : (k + 1) * depth]
        return out

    def gather_plain(value):
        whole = lax.all_gather(value, ("shard", "context"), axis=0, tiled=True)
        return around(whole, "tensor")

    ringed = shards * contexts * sides <= 16

    def stack(parts):
        return [
            jnp.concatenate(
                [parts[(i, j, far)] for i in range(shards) for j in range(contexts)], axis=0
            )
            for far in range(sides)
        ]

    if ringed:
        attn_parts = stack(gather_flat(attn_own))
        fc1_parts = stack(gather_mid(w_fc1, "tensor", "context"))
        fc2_parts = stack(gather_mid(w_fc2, "context", "tensor"))
        order = [
            ((shard - i) % shards) * contexts + (context - j) % contexts
            for i in range(shards)
            for j in range(contexts)
        ]
        back = [
            ((shard - b // contexts) % shards) * contexts + (context - b % contexts) % contexts
            for b in range(shards * contexts)
        ]
    else:
        attn_parts = gather_plain(attn_own)
        fc1_parts = gather_plain(w_fc1)
        fc2_parts = gather_plain(w_fc2)
        order = back = None

    def reorder(array, blocks):
        if blocks is None:
            return array
        axis = array.ndim - 1
        return jnp.concatenate(
            [lax.dynamic_slice_in_dim(array, b * depth, depth, axis) for b in blocks], axis=axis
        )

    shuffle = lambda array: reorder(array, order)
    restore = lambda array: reorder(array, back)

    def adapter_of(far):
        return block_of(adapter_index, 2 * ((side + far) % sides) + high)

    def up_pack(index):
        up = block_of(qkv_up, index)
        return jnp.concatenate(
            [up[0], up[1], up[2], block_of(fc1_up, index)]
            + [block_of(proj_down, index).T, block_of(fc2_down, index).T],
            axis=1,
        )

    packs = [up_pack(adapter_of(0))]
    for far in range(1, sides):
        send = [(i, (i + 2 * far) % tensors) for i in range(tensors)]
        packs.append(lax.ppermute(up_pack(adapter_of(far)), "tensor", send))
    mine = adapter_of(0)
    down = block_of(down_in, mine)
    down_t = shuffle(jnp.transpose(down, (0, 2, 1)).reshape(4 * rank, model))
    out_t = shuffle(block_of(out_up, mine))

    zero = jnp.zeros((rank, PAIR), BF16)

    def spread(pack):
        lines = []
        for j in range(3):
            cells = []
            for p in range(pairs):
                start = j * width + p * PAIR
                for k in range(3):
                    cells.append(pack[:, start : start + PAIR] if k == j else zero)
            lines.append(jnp.concatenate(cells, axis=1))
        return jnp.concatenate(lines, axis=0)

    qkv_lift = jnp.concatenate([spread(pack) for pack in packs], axis=1)
    base = 3 * width
    fc1_lift = jnp.concatenate([pack[:, base : base + hidden] for pack in packs], axis=1)
    base += hidden
    proj_t = jnp.concatenate([pack[:, base : base + width] for pack in packs], axis=1)
    base += width
    fc2_t = jnp.concatenate([pack[:, base : base + hidden] for pack in packs], axis=1)

    gain_one, bias_one = shuffle(ln1_gain), shuffle(ln1_bias)
    gain_two, bias_two = shuffle(ln2_gain), shuffle(ln2_bias)
    scale = shuffle(layer_scale)

    x_own = shuffle(x_own)
    x_all = jnp.concatenate([x_own, swap(x_own)], axis=0).astype(F32)
    normed, unit_one, inverse_one = normalize(x_all, gain_one, bias_one)
    n1 = normed.astype(BF16)
    u = dot_nt(n1, down_t[: 3 * rank]).astype(BF16)
    w_in = jnp.concatenate([part[:, : 3 * width] for part in attn_parts], axis=1)
    w_out = jnp.concatenate([part[:, 3 * width :] for part in attn_parts], axis=1)
    qkv = (dot(n1, w_in) + dot(u, qkv_lift)).astype(BF16)

    groups = [[h * half + i for i in range(half)] for h in range(2)]

    def to_heads(array, cell):
        if half == 1:
            return array
        cells = array.reshape(array.shape[0], -1, cell)
        moved = lax.all_to_all(
            cells, "context", 1, 0, axis_index_groups=groups, tiled=True
        )
        return moved.reshape(moved.shape[0], -1)

    def to_rows(array, cell):
        if half == 1:
            return array
        cells = array.reshape(array.shape[0], -1, cell)
        moved = lax.all_to_all(
            cells, "context", 0, 1, axis_index_groups=groups, tiled=True
        )
        return moved.reshape(moved.shape[0], -1)

    qkv_heads = to_heads(qkv, 3 * PAIR)
    o_heads, lse = attend(qkv_heads)
    o = to_rows(o_heads, PAIR)
    attn_part = dot_nt(o, w_out)
    c_part = dot_nt(o, proj_t)
    c_own = (c_part[:rows] + swap(c_part[rows:])).astype(BF16)
    attn_out = attn_part[:rows] + swap(attn_part[rows:]) + dot(c_own, out_t[0])
    h = x_all[:rows] + scale[0] * attn_out
    normed, unit_two, inverse_two = normalize(h, gain_two, bias_two)
    n2_own = normed.astype(BF16)
    n2 = jnp.concatenate([n2_own, swap(n2_own)], axis=0)
    f = dot_nt(n2, down_t[3 * rank :]).astype(BF16)

    gy_own = shuffle(gy_own)
    gy_all = jnp.concatenate([gy_own, swap(gy_own)], axis=0)
    gb = (gy_all.astype(F32) * scale[1]).astype(BF16)
    gm = dot_nt(gb, out_t[1]).astype(BF16)

    branch_part, gn2_part, m_part, gf_part, g_fc1, g_fc2 = mlp(
        n2,
        gb,
        f,
        gm,
        jnp.concatenate(fc1_parts, axis=1),
        jnp.concatenate(fc2_parts, axis=1),
        fc1_lift,
        fc2_t,
    )
    m_own = (m_part[:rows] + swap(m_part[rows:])).astype(BF16)
    branch_far = swap(branch_part[rows:].astype(BF16)).astype(F32)
    branch = branch_part[:rows] + branch_far + dot(m_own, out_t[1])
    result_own = (h + scale[1] * branch).astype(BF16)
    g_out1 = dot_tn(m_own, gb[:rows])

    gf_own = (gf_part[:rows] + swap(gf_part[rows:])).astype(BF16)
    gn2 = gn2_part[:rows] + swap(gn2_part[rows:]) + dot(gf_own, down_t[3 * rank :])
    g_down3 = dot_tn(gf_own, n2_own)
    gh = gy_own.astype(F32) + norm_back(gn2, unit_two, inverse_two, gain_two)
    gattn_own = (scale[0] * gh).astype(BF16)
    gattn = jnp.concatenate([gattn_own, swap(gattn_own)], axis=0)
    gc = dot_nt(gattn, out_t[0]).astype(BF16)
    g_out0 = dot_tn(c_own, gattn_own)
    go = (dot(gattn, w_out) + dot(gc, proj_t)).astype(BF16)
    g_proj = dot_tn(gc, o)
    g = to_rows(attend_back(qkv_heads, to_heads(go, PAIR), o_heads, lse), 3 * PAIR)

    gu_part = dot_nt(g, qkv_lift)
    gu_own = (gu_part[:rows] + swap(gu_part[rows:])).astype(BF16)
    gn1_part = dot_nt(g, w_in)
    gn1 = gn1_part[:rows] + swap(gn1_part[rows:]) + dot(gu_own, down_t[: 3 * rank])
    g_up = dot_tn(u, g)
    g_down = dot_tn(gu_own, n1[:rows])
    input_own = gh + norm_back(gn1, unit_one[:rows], inverse_one[:rows], gain_one)

    def send_home(block):
        near = []
        for far in range(sides):
            got = lax.ppermute(block, plane, to_home_far[far])
            near += [got, swap(got)]
        return near

    def place(near, kind):
        out = jnp.zeros((images, rows, model), kind)
        for far in range(sides):
            for flip in range(2):
                where = 2 * ((side - far) % sides) + (core ^ flip)
                piece = near[2 * far + flip].astype(kind)[None]
                out = lax.dynamic_update_slice(out, piece, (where, 0, 0))
        return out

    result = place(send_home(restore(result_own)), BF16)
    input_grad = place(send_home(restore(input_own.astype(BF16))), F32)

    def slice_grads(far):
        cells = []
        for j in range(3):
            for p in range(pairs):
                start = ((far * pairs + p) * 3 + j) * PAIR
                cells.append(g_up[j * rank : (j + 1) * rank, start : start + PAIR])
        cells.append(g_fc1[:, far * hidden : (far + 1) * hidden])
        cells.append(g_proj[:, far * width : (far + 1) * width])
        cells.append(g_fc2[:, far * hidden : (far + 1) * hidden])
        return jnp.concatenate(cells, axis=1)

    shared = jnp.concatenate(
        [g_down.reshape(3, rank, model), g_down3[None], g_out0[None], g_out1[None]], axis=0
    )
    shared = restore(shared)
    both = shared + swap(shared)
    cut = model // 2
    own_half = lax.dynamic_slice_in_dim(both, core * cut, cut, 2)
    own_half = jnp.concatenate([own_half[j] for j in range(6)], axis=1)

    owners = jnp.stack([adapter_of(0)])
    gathered = [jnp.concatenate([slice_grads(0), own_half], axis=1).astype(BF16)]
    marks = [adapter_of(0)]
    for far in range(1, sides):
        send = [(i, (i - 2 * far) % tensors) for i in range(tensors)]
        pack = jnp.concatenate([slice_grads(far), own_half], axis=1).astype(BF16)
        gathered.append(lax.ppermute(pack, "tensor", send))
        marks.append(adapter_of(far))
    block = jnp.stack(gathered)
    mark = jnp.stack(marks)
    lane = jnp.arange(adapters, dtype=jnp.int32)
    pick = (mark[:, None] == lane[None, :]).astype(F32)
    if half > 1:
        steps = [[h * half + i for i in range(half)] for h in range(2)]
        block = lax.psum(block.astype(F32), "context", axis_index_groups=steps).astype(BF16)
        across = [(i, (i + half) % contexts) for i in range(contexts)]
    else:
        across = ring["context"]
    block = jnp.concatenate([block, lax.ppermute(block, "context", across)], axis=0)
    pick = jnp.concatenate([pick, lax.ppermute(pick, "context", across)], axis=0)
    blocks = around(block, "shard")
    picks = around(pick, "shard")
    all_blocks = jnp.concatenate(blocks, axis=0)
    all_picks = jnp.concatenate(picks, axis=0).astype(BF16)
    flat = all_blocks.reshape(all_blocks.shape[0], -1)
    totals = lax.dot_general(all_picks, flat, TN, preferred_element_type=F32)
    totals = totals.reshape(adapters, rank, -1)

    base = 3 * width
    qkv_grad = totals[:, :, :base].reshape(adapters, rank, 3, width)
    qkv_grad = jnp.transpose(qkv_grad, (0, 2, 1, 3))
    fc1_grad = totals[:, :, base : base + hidden]
    base += hidden
    proj_grad = jnp.transpose(totals[:, :, base : base + width], (0, 2, 1))
    base += width
    fc2_grad = jnp.transpose(totals[:, :, base : base + hidden], (0, 2, 1))
    base += hidden
    halves = totals[:, :, base:].reshape(adapters, rank, 6, cut)
    other = swap(halves)
    low = jnp.where(core == 0, halves, other)
    top = jnp.where(core == 0, other, halves)
    shared = jnp.transpose(jnp.concatenate([low, top], axis=3), (0, 2, 1, 3))
    down_grad = jnp.transpose(shared[:, :4], (0, 1, 3, 2))
    out_grad = shared[:, 4:]
    return (
        result,
        input_grad,
        down_grad,
        qkv_grad,
        fc1_grad,
        proj_grad,
        fc2_grad,
        out_grad,
    )


def solution(mesh):
    sizes = (mesh.shape["shard"], mesh.shape["context"], mesh.shape["tensor"])
    placed = (
        P("shard", "context", None),
        P("shard", "context", None),
        P("shard"),
        P(),
        P(),
        P(),
        P(),
        P(),
        P(("shard", "context"), None, "tensor"),
        P(("shard", "context"), "tensor"),
        P(("shard", "context"), "tensor"),
        P(("shard", "context"), "tensor"),
        P(),
        P(None, None, None, "tensor"),
        P(None, None, "tensor"),
        P(None, "tensor", None),
        P(None, "tensor", None),
        P(),
    )
    return jax.shard_map(
        functools.partial(per_device, sizes),
        mesh=mesh,
        in_specs=placed,
        out_specs=(
            P("shard", "context", None),
            P("shard", "context", None),
            P(),
            P(None, None, None, "tensor"),
            P(None, None, "tensor"),
            P(None, "tensor", None),
            P(None, "tensor", None),
            P(),
        ),
        check_vma=False,
    )
```

```python
import functools
import math

import jax
import jax.numpy as jnp
import numpy as np
from jax import lax
from jax.experimental import pallas as pl
from jax.experimental.pallas import tpu as pltpu
from jax.sharding import PartitionSpec as P

HEAD_DIM = 64
PAIR = 2 * HEAD_DIM
EPS = 1e-06
LOG2E = math.log2(math.e)
SCORE = 1.0 / math.sqrt(HEAD_DIM)
F32 = jnp.float32
BF16 = jnp.bfloat16
NT = (((1,), (1,)), ((), ()))
TN = (((0,), (0,)), ((), ()))


def dot(a, b):
    return jnp.dot(a, b, preferred_element_type=F32)


def dot_nt(a, b):
    return lax.dot_general(a, b, NT, preferred_element_type=F32)


def dot_tn(a, b):
    return lax.dot_general(a, b, TN, preferred_element_type=F32)


def head_masks(rows):
    lane = lax.broadcasted_iota(jnp.int32, (rows, PAIR), 1)
    return lane < HEAD_DIM


def attend_kernel(block, q_ref, k_ref, v_ref, _, o_ref, lse_ref):
    rows = q_ref.shape[0]
    keys = k_ref[...]
    values = jnp.concatenate([v_ref[...], jnp.ones((rows, PAIR), BF16)], axis=1)
    first = head_masks(block)

    def step(i, carry):
        at = pl.ds(pl.multiple_of(i * block, block), block)
        q = q_ref[at, :]
        outs = []
        logs = []
        for head in range(2):
            mine = first if head == 0 else jnp.logical_not(first)
            s = dot_nt(jnp.where(mine, q, jnp.zeros_like(q)), keys)
            peak = jnp.max(s, axis=1, keepdims=True)
            e = jnp.exp2((s - peak) * (SCORE * LOG2E))
            acc = dot(e.astype(BF16), values)
            total = acc[:, PAIR:]
            outs.append(acc[:, :PAIR] / total)
            logs.append(peak * (SCORE * LOG2E) + jnp.log2(total))
        o_ref[at, :] = jnp.where(first, outs[0], outs[1]).astype(BF16)
        lane = lax.broadcasted_iota(jnp.int32, (block, PAIR), 1)
        both = jnp.where(lane == 0, logs[0], logs[1])
        lse_ref[0, :, at] = jnp.transpose(both)[:8]
        return carry

    lax.fori_loop(0, rows // block, step, 0)


def thirds(rows, group, near):
    return [
        pl.BlockSpec((rows, PAIR), lambda p, j=j: (0, (group * 3 + j) * near + p))
        for j in range(3)
    ]


def attend(qkv, group, near, o):
    rows, width = qkv.shape
    pairs = width // (3 * PAIR)
    block = min(256, rows)
    anywhere = pl.BlockSpec(memory_space=pl.ANY)
    operands = [qkv, qkv, qkv, qkv if o is None else o]
    return pl.pallas_call(
        functools.partial(attend_kernel, block),
        grid=(near,),
        in_specs=thirds(rows, group, near) + [anywhere],
        out_specs=[
            pl.BlockSpec((rows, PAIR), lambda p: (0, group * near + p)),
            pl.BlockSpec((1, 8, rows), lambda p: (p, 0, 0)),
        ],
        out_shape=[
            jax.ShapeDtypeStruct((rows, pairs * PAIR), BF16),
            jax.ShapeDtypeStruct((near, 8, rows), F32),
        ],
        input_output_aliases={} if o is None else {3: 0},
        cost_estimate=pl.CostEstimate(
            flops=near * 2 * rows * rows * 256 * 4,
            bytes_accessed=rows * near * PAIR * 8,
            transcendentals=near * 2 * rows * rows,
        ),
        name="attend",
    )(*operands)


def attend_back_kernel(
    block, near, q_ref, k_ref, v_ref, go_ref, o_ref, lse_ref, _, g_ref, gq_ref, d_ref
):
    rows = q_ref.shape[0]
    pair = pl.program_id(0)
    lanes = [pl.ds(pl.multiple_of((j * near + pair) * PAIR, PAIR), PAIR) for j in range(3)]
    first = head_masks(block)
    prod = o_ref[...].astype(F32) * go_ref[...].astype(F32)
    lane8 = lax.broadcasted_iota(jnp.int32, (8, PAIR), 1) // HEAD_DIM
    row8 = lax.broadcasted_iota(jnp.int32, (8, PAIR), 0)
    d_ref[...] = lax.dot_general(
        (lane8 == row8).astype(F32),
        prod,
        NT,
        preferred_element_type=F32,
        precision=lax.Precision.HIGHEST,
    )
    gq_ref[...] = jnp.zeros_like(gq_ref)

    def step(i, carry):
        at = pl.ds(pl.multiple_of(i * block, block), block)
        k = k_ref[at, :]
        v = v_ref[at, :]
        q = q_ref[...]
        go = go_ref[...]
        gks = []
        gvs = []
        gq = None
        for head in range(2):
            mine = first if head == 0 else jnp.logical_not(first)
            k_own = jnp.where(mine, k, jnp.zeros_like(k))
            v_own = jnp.where(mine, v, jnp.zeros_like(v))
            s = dot_nt(k_own, q)
            gp = dot_nt(v_own, go)
            p = jnp.exp2(s * (SCORE * LOG2E) - lse_ref[0, head : head + 1, :])
            gs = (p * (gp - d_ref[head : head + 1, :])).astype(BF16)
            gks.append(dot(gs, q))
            gvs.append(dot(p.astype(BF16), go))
            part = dot(jnp.transpose(k_own), gs)
            gq = part if gq is None else gq + part
        gq_ref[...] += gq
        g_ref[at, lanes[1]] = (jnp.where(first, gks[0], gks[1]) * SCORE).astype(BF16)
        g_ref[at, lanes[2]] = jnp.where(first, gvs[0], gvs[1]).astype(BF16)
        return carry

    lax.fori_loop(0, rows // block, step, 0)
    g_ref[:, lanes[0]] = (jnp.transpose(gq_ref[...]) * SCORE).astype(BF16)


def attend_back(qkv, go, o, lse, group, near, g):
    rows, width = qkv.shape
    block = min(256, rows)
    mine = pl.BlockSpec((rows, PAIR), lambda p: (0, group * near + p))
    anywhere = pl.BlockSpec(memory_space=pl.ANY)
    operands = [qkv, qkv, qkv, go, o, lse, qkv if g is None else g]
    return pl.pallas_call(
        functools.partial(attend_back_kernel, block, near),
        grid=(near,),
        in_specs=thirds(rows, group, near)
        + [mine, mine, pl.BlockSpec((1, 8, rows), lambda p: (p, 0, 0)), anywhere],
        out_specs=pl.BlockSpec((rows, 3 * near * PAIR), lambda p: (0, group)),
        out_shape=jax.ShapeDtypeStruct((rows, width), BF16),
        scratch_shapes=[pltpu.VMEM((PAIR, rows), F32), pltpu.VMEM((8, rows), F32)],
        input_output_aliases={} if g is None else {6: 0},
        cost_estimate=pl.CostEstimate(
            flops=near * 2 * rows * rows * 256 * 10,
            bytes_accessed=rows * near * PAIR * 16,
            transcendentals=near * 2 * rows * rows,
        ),
        name="attend_back",
    )(*operands)


def mlp_kernel(
    block,
    own,
    moves,
    pieces,
    place_ref,
    n_ref,
    gb_ref,
    f_ref,
    gm_ref,
    ft_ref,
    gmt_ref,
    u1_ref,
    d2_ref,
    *refs,
):
    parts = refs[:pieces]
    outs, scratch = refs[pieces : pieces + 8], refs[pieces + 8 :]
    branch_own, branch_far, gn_own, gn_far, rank_own, rank_far, gf1_ref, gf2_ref = outs
    w1_all, w2_all, branch_ref, gn_ref, m_ref, gf_ref, sems = scratch
    rows = n_ref.shape[0]
    chunk = u1_ref.shape[1]
    at_chunk = pl.ds(pl.multiple_of(pl.program_id(0) * chunk, chunk), chunk)

    @pl.when(pl.program_id(0) == 0)
    def _():
        copies = []
        for k, (part, start, depth, which) in enumerate(moves):
            width = parts[part].shape[1]
            down = pl.ds(pl.multiple_of(place_ref[0, k] * depth, depth), depth)
            along = pl.ds(pl.multiple_of(place_ref[1, k] * width, width), width)
            copies.append(
                pltpu.make_async_copy(
                    parts[part].at[pl.ds(start, depth), :],
                    (w1_all, w2_all)[which].at[down, along],
                    sems.at[k],
                )
            )
        for copy in copies:
            copy.start()
        branch_ref[...] = jnp.zeros_like(branch_ref)
        gn_ref[...] = jnp.zeros_like(gn_ref)
        m_ref[...] = jnp.zeros_like(m_ref)
        gf_ref[...] = jnp.zeros_like(gf_ref)
        for copy in copies:
            copy.wait()

    gf1_ref[...] = jnp.zeros_like(gf1_ref)
    gf2_ref[...] = jnp.zeros_like(gf2_ref)

    def step(i, carry):
        at = pl.ds(pl.multiple_of(i * block, block), block)
        w1 = w1_all[:, at_chunk]
        w2 = w2_all[:, at_chunk]
        u1 = u1_ref[...]
        d2 = d2_ref[...]
        z = dot(n_ref[at, :], w1) + dot(f_ref[at, :], u1)
        cdf = 0.5 * (1.0 + lax.erf(z * (1.0 / math.sqrt(2.0))))
        a = (z * cdf).astype(BF16)
        slope = cdf + z * (jnp.exp2(z * z * (-0.5 * LOG2E)) * (1.0 / math.sqrt(2.0 * math.pi)))
        ga = dot(gb_ref[at, :], w2) + dot(gm_ref[at, :], d2)
        gz = (ga * slope).astype(BF16)
        branch_ref[at, :] += dot_nt(a, w2)
        m_ref[at, :] += dot_nt(a, d2)
        gn_ref[at, :] += dot_nt(gz, w1)
        gf_ref[at, :] += dot_nt(gz, u1)
        gf1_ref[...] += dot(ft_ref[:, at], gz)
        gf2_ref[...] += dot(gmt_ref[:, at], a)
        return carry

    lax.fori_loop(0, rows // block, step, 0)

    @pl.when(pl.program_id(0) == pl.num_programs(0) - 1)
    def _():
        branch_own[...] = branch_ref[:own, :]
        branch_far[...] = branch_ref[own:, :].astype(BF16)
        gn_own[...] = gn_ref[:own, :]
        gn_far[...] = gn_ref[own:, :]
        rank_own[...] = jnp.concatenate([m_ref[:own, :], gf_ref[:own, :]], axis=1)
        rank_far[...] = jnp.concatenate([m_ref[own:, :], gf_ref[own:, :]], axis=1)


def mlp(n, gb, f, gm, parts, moves, place, u1, d2, own):
    rows, model = n.shape
    hidden = u1.shape[1]
    rank = f.shape[1]
    chunk = min(512, hidden)
    block = min(256, rows)
    whole = lambda shape: pl.BlockSpec(shape, lambda j, place: (0, 0))
    part = lambda depth: pl.BlockSpec((depth, chunk), lambda j, place: (0, j))
    far = rows - own
    shapes = [
        ((own, model), F32),
        ((far, model), BF16),
        ((own, model), F32),
        ((far, model), F32),
        ((own, 2 * rank), F32),
        ((far, 2 * rank), F32),
    ]
    return pl.pallas_call(
        functools.partial(mlp_kernel, block, own, moves, len(parts)),
        grid_spec=pltpu.PrefetchScalarGridSpec(
            num_scalar_prefetch=1,
            grid=(hidden // chunk,),
            in_specs=[
                whole((rows, model)),
                whole((rows, model)),
                whole((rows, rank)),
                whole((rows, rank)),
                whole((rank, rows)),
                whole((rank, rows)),
                part(rank),
                part(rank),
            ]
            + [pl.BlockSpec(memory_space=pl.ANY)] * len(parts),
            out_specs=[whole(shape) for shape, _ in shapes] + [part(rank), part(rank)],
            scratch_shapes=[
                pltpu.VMEM((model, hidden), BF16),
                pltpu.VMEM((model, hidden), BF16),
                pltpu.VMEM((rows, model), F32),
                pltpu.VMEM((rows, model), F32),
                pltpu.VMEM((rows, rank), F32),
                pltpu.VMEM((rows, rank), F32),
                pltpu.SemaphoreType.DMA((len(moves),)),
            ],
        ),
        out_shape=[jax.ShapeDtypeStruct(*shape) for shape in shapes]
        + [jax.ShapeDtypeStruct((rank, hidden), F32)] * 2,
        cost_estimate=pl.CostEstimate(
            flops=12 * rows * model * hidden,
            bytes_accessed=4 * model * hidden + 12 * rows * model,
            transcendentals=2 * rows * hidden,
        ),
        name="mlp",
    )(place, n, gb, f, gm, f.T, gm.T, u1, d2, *parts)


def assemble_kernel(moves, pieces, place_ref, *refs):
    parts, outs, sems = refs[:pieces], refs[pieces:-1], refs[-1]
    copies = []
    for k, (part, start, depth) in enumerate(moves):
        column = 0
        for j, out in enumerate(outs):
            width = out.shape[1] // 2
            down = pl.ds(pl.multiple_of(place_ref[0, k] * depth, depth), depth)
            along = pl.ds(pl.multiple_of(place_ref[1, k] * width, width), width)
            copies.append(
                pltpu.make_async_copy(
                    parts[part].at[pl.ds(start, depth), pl.ds(column, width)],
                    out.at[down, along],
                    sems.at[k, j],
                )
            )
            column += width
    for copy in copies:
        copy.start()
    for copy in copies:
        copy.wait()


def assemble(parts, moves, place, rows, widths):
    anywhere = pl.BlockSpec(memory_space=pl.ANY)
    return pl.pallas_call(
        functools.partial(assemble_kernel, moves, len(parts)),
        grid_spec=pltpu.PrefetchScalarGridSpec(
            num_scalar_prefetch=1,
            grid=(1,),
            in_specs=[anywhere] * len(parts),
            out_specs=[
                pl.BlockSpec((rows, 2 * width), lambda i, place: (0, 0)) for width in widths
            ],
            scratch_shapes=[pltpu.SemaphoreType.DMA((len(moves), len(widths)))],
        ),
        out_shape=[jax.ShapeDtypeStruct((rows, 2 * width), BF16) for width in widths],
        name="assemble",
    )(place, *parts)


def totals_kernel(blocks, widths, *refs):
    sources, outs = refs[:blocks], refs[blocks:]
    for out in outs:
        out[...] = jnp.zeros_like(out)
    total = sum(widths)
    for source in sources:
        for k in range(source.shape[0]):
            owner = jnp.max(source[k, :, total:].astype(F32)).astype(jnp.int32)
            column = 0
            for out, width in zip(outs, widths):
                out[owner] += source[k, :, column : column + width].astype(F32)
                column += width


def totals(blocks, widths, adapters):
    rank = blocks[0].shape[1]
    return pl.pallas_call(
        functools.partial(totals_kernel, len(blocks), widths),
        out_shape=[jax.ShapeDtypeStruct((adapters, rank, width), F32) for width in widths],
        name="totals",
    )(*blocks)


def spread_kernel(order, core_ref, *refs):
    halves, target = refs[:-1], refs[-1]
    cut = target.shape[3] // 2
    first = core_ref[0] == 0
    for j, (pair, k) in enumerate(order):
        own = halves[2 * pair][:, :, k * cut : (k + 1) * cut]
        other = halves[2 * pair + 1][:, :, k * cut : (k + 1) * cut]
        target[:, j, :, :cut] = jnp.where(first, own, other)
        target[:, j, :, cut:] = jnp.where(first, other, own)


def spread(core, halves, order, cut):
    adapters, rank, _ = halves[0].shape
    return pl.pallas_call(
        functools.partial(spread_kernel, order),
        in_specs=[pl.BlockSpec(memory_space=pltpu.SMEM)]
        + [pl.BlockSpec(memory_space=pltpu.VMEM)] * len(halves),
        out_shape=jax.ShapeDtypeStruct((adapters, len(order), rank, 2 * cut), F32),
        name="spread",
    )(jnp.reshape(core, (1,)), *halves)


def settle_kernel(where_ref, *refs):
    parts, out = refs[:-1], refs[-1]
    for k, part in enumerate(parts):

        @pl.when(pl.program_id(0) == k)
        def _():
            out[0] = part[...].astype(out.dtype)


def settle(parts, where, kind):
    rows, model = parts[0].shape
    return pl.pallas_call(
        settle_kernel,
        grid_spec=pltpu.PrefetchScalarGridSpec(
            num_scalar_prefetch=1,
            grid=(len(parts),),
            in_specs=[pl.BlockSpec((rows, model), lambda k, where: (0, 0))] * len(parts),
            out_specs=pl.BlockSpec((1, rows, model), lambda k, where: (where[k], 0, 0)),
        ),
        out_shape=jax.ShapeDtypeStruct((len(parts), rows, model), kind),
        name="settle",
    )(where, *parts)


def normalize(values, gain, shift):
    centre = values - jnp.mean(values, axis=-1, keepdims=True)
    inverse = lax.rsqrt(jnp.mean(centre * centre, axis=-1, keepdims=True) + EPS)
    unit = centre * inverse
    return unit * gain + shift, unit, inverse


def norm_back(grad, unit, inverse, gain):
    scaled = grad * gain
    centred = scaled - jnp.mean(scaled, axis=-1, keepdims=True)
    return inverse * (centred - unit * jnp.mean(scaled * unit, axis=-1, keepdims=True))


def per_device(
    sizes,
    tokens,
    cotangent,
    adapter_index,
    ln1_gain,
    ln1_bias,
    ln2_gain,
    ln2_bias,
    layer_scale,
    w_qkv,
    w_proj,
    w_fc1,
    w_fc2,
    down_in,
    qkv_up,
    fc1_up,
    proj_down,
    fc2_down,
    out_up,
):
    shards, contexts, tensors = sizes
    half = contexts // 2
    sides = tensors // 2
    images, rows, model = tokens.shape
    rank = down_in.shape[-1]
    depth = w_fc1.shape[0]
    width = w_proj.shape[1]
    hidden = w_fc1.shape[1]
    pairs = width // PAIR
    adapters = down_in.shape[0]
    shard = lax.axis_index("shard")
    context = lax.axis_index("context")
    tensor = lax.axis_index("tensor")
    side, core = tensor // 2, tensor % 2
    high = context // half

    ring = {
        "shard": [(i, (i + 1) % shards) for i in range(shards)],
        "context": [(i, (i + 1) % contexts) for i in range(contexts)],
        "tensor": [(i, (i + 2) % tensors) for i in range(tensors)],
    }
    count = {"shard": shards, "context": contexts, "tensor": sides}
    twin = [(i, i ^ 1) for i in range(tensors)]
    plane = ("context", "tensor")

    def hop(value, axis):
        return lax.ppermute(value, axis, ring[axis])

    def swap(value):
        return lax.ppermute(value, "tensor", twin)

    def around(value, axis):
        out = [value]
        for _ in range(count[axis] - 1):
            out.append(hop(out[-1], axis))
        return out

    def fence(*values):
        return lax.optimization_barrier(values)

    to_owner = []
    to_home = {far: [] for far in range(sides)}
    for c in range(contexts):
        for s in range(sides):
            for k in range(2):
                here = c * tensors + 2 * s + k
                source = 2 * (c % half) + k
                to_owner.append((source * tensors + 2 * s + c // half, here))
                for far in range(sides):
                    there = (s + far) % sides
                    to_home[far].append((here, source * tensors + 2 * there + c // half))

    ringed = contexts == 2 and sides == 2
    cross = {0: [], 1: []}
    if ringed:
        for c in range(2):
            for s in range(2):
                for k in range(2):
                    here = c * tensors + 2 * s + k
                    along = c * tensors + 2 * (1 - s) + k
                    aside = (1 - c) * tensors + 2 * s + k
                    cross[0].append((here, along if k == 0 else aside))
                    cross[1].append((here, aside if k == 0 else along))

    def block_of(array, index):
        return lax.dynamic_index_in_dim(array, index, 0, keepdims=False)

    def pair_up(a, b):
        return jnp.concatenate([a, b], axis=0)

    def adapter_of(index, far):
        return block_of(index, 2 * ((side + far) % sides) + high)

    def up_pack(e, ups):
        up = block_of(ups[0], e)
        return jnp.concatenate(
            [up[0], up[1], up[2], block_of(ups[1], e)]
            + [block_of(ups[2], e).T, block_of(ups[3], e).T],
            axis=1,
        )

    def up_packs(index, ups):
        packs = [up_pack(adapter_of(index, 0), ups)]
        for far in range(1, sides):
            send = [(i, (i + 2 * far) % tensors) for i in range(tensors)]
            packs.append(lax.ppermute(up_pack(adapter_of(index, far), ups), "tensor", send))
        return packs

    attn_own = jnp.concatenate([w_qkv[:, j] for j in range(3)] + [w_proj], axis=1)
    ups = (qkv_up, fc1_up, proj_down, fc2_down)
    flows = {}

    if ringed:
        ff_own = pair_up(w_fc1, w_fc2)
        lines = [attn_own]
        got = fence(
            hop(attn_own, "shard"),
            lax.ppermute(attn_own, plane, cross[0]),
            lax.ppermute(ff_own, plane, cross[0]),
            tokens,
            cotangent,
            adapter_index,
            down_in,
            out_up,
            *ups,
        )
        lines.append(got[0])
        bases = [pair_up(attn_own, got[1])]
        ff = [pair_up(ff_own, got[2])]
        tokens, cotangent, adapter_index, down_in, out_up = got[3:8]
        packs = up_packs(adapter_index, got[8:])
        crossed = []
        ff_next = hop(ff[0], "shard")
        middle = min(2, shards - 1)
        for i in range(1, shards):
            step = [lax.ppermute(lines[i], plane, cross[0])]
            step.append(lax.ppermute(bases[i - 1], plane, cross[1]))
            if i + 1 < shards:
                step.append(hop(lines[i], "shard"))
            if i == 1:
                x_own = lax.ppermute(block_of(tokens, tensor), plane, to_owner)
                step.append(packs[1])
            if i == middle:
                step += [ff_next, x_own, cotangent]
            got = fence(*step)
            bases.append(pair_up(lines[i], got[0]))
            crossed.append(got[1])
            if i + 1 < shards:
                lines.append(got[2])
            if i == 1:
                packs[1] = got[-1] if middle > 1 else got[-4]
            if i == middle:
                ff_next, x_own, cotangent = got[-3:]
                ff.append(ff_next)
                x_other = swap(x_own)
                flows["ahead"] = hop(ff_next, "shard")
        flows["cross"] = lax.ppermute(ff[0], plane, cross[1])
        ff_crossed = []
        gy_own = lax.ppermute(block_of(cotangent, tensor), plane, to_owner)
        last, x_own, x_other = fence(
            lax.ppermute(bases[-1], plane, cross[1]), x_own, x_other
        )
        crossed.append(last)
        attn_parts = [part for i in range(shards) for part in (bases[i], crossed[i])]
        step_of = np.repeat(np.arange(shards), 4)
        near_0 = np.tile([0, 0, 1, 1], shards)
        far_0 = np.tile([0, 1, 0, 1], shards)
        near = jnp.where(core == 0, near_0, far_0)
        across = jnp.where(core == 0, far_0, near_0)
        row = (shard - step_of) % shards * contexts + (context - near) % contexts
        attn_place = jnp.stack([row, across]).astype(jnp.int32)
        attn_moves = [(2 * i + p // 2, p % 2 * depth, depth) for i in range(shards) for p in range(4)]
        ff_moves = [
            (2 * i + p // 2, p % 2 * 2 * depth + which * depth, depth, which)
            for which in range(2)
            for i in range(shards)
            for p in range(4)
        ]
        ff_place = jnp.concatenate([attn_place, attn_place], axis=1)

        def advance(*values):
            taken = len(ff_crossed)
            pending = [flows["cross"]] if taken < shards else []
            ahead = flows["ahead"] if len(ff) < shards else None
            wait = [] if ahead is None else [ahead]
            got = fence(*values, *pending, *wait)
            ff_crossed.append(got[len(values)])
            if ahead is not None:
                ff.append(got[-1])
                if len(ff) < shards:
                    flows["ahead"] = hop(ff[-1], "shard")
            if len(ff_crossed) < shards:
                flows["cross"] = lax.ppermute(ff[len(ff_crossed)], plane, cross[1])
            return got[: len(values)]

    else:

        def gather_plain(value):
            whole = lax.all_gather(value, ("shard", "context"), axis=0, tiled=True)
            return around(whole, "tensor")

        attn_parts = gather_plain(attn_own)
        fc1_parts = gather_plain(w_fc1)
        fc2_parts = gather_plain(w_fc2)
        packs = up_packs(adapter_index, ups)
        x_own = lax.ppermute(block_of(tokens, tensor), plane, to_owner)
        x_other = swap(x_own)
        gy_own = lax.ppermute(block_of(cotangent, tensor), plane, to_owner)
        attn_moves = [(k, 0, model) for k in range(sides)]
        attn_place = jnp.asarray([[0] * sides, list(range(sides))], jnp.int32)
        ff_moves = [(k, 0, model, k // sides) for k in range(2 * sides)]
        ff_place = jnp.concatenate([attn_place, attn_place], axis=1)

        def advance(*values):
            return values

    mine = adapter_of(adapter_index, 0)
    down = block_of(down_in, mine)
    down_t = jnp.transpose(down, (0, 2, 1)).reshape(4 * rank, model)
    out_t = block_of(out_up, mine)

    third = lax.broadcasted_iota(jnp.int32, (3 * rank, 3 * width), 0) // rank
    place = lax.broadcasted_iota(jnp.int32, (3 * rank, 3 * width), 1) // width

    def spread_out(pack):
        high_up = jnp.concatenate([pack[:, : 3 * width]] * 3, axis=0)
        return jnp.where(third == place, high_up, jnp.zeros_like(high_up))

    qkv_lift = jnp.concatenate([spread_out(pack) for pack in packs], axis=1)
    base = 3 * width
    fc1_lift = jnp.concatenate([pack[:, base : base + hidden] for pack in packs], axis=1)
    base += hidden
    proj_t = jnp.concatenate([pack[:, base : base + width] for pack in packs], axis=1)
    base += width
    fc2_t = jnp.concatenate([pack[:, base : base + hidden] for pack in packs], axis=1)

    w_in, w_out = assemble(attn_parts, attn_moves, attn_place, model, (3 * width, width))
    x_all = pair_up(x_own, x_other).astype(F32)
    normed, unit_one, inverse_one = normalize(x_all, ln1_gain, ln1_bias)
    n1 = normed.astype(BF16)
    u = dot_nt(n1, down_t[: 3 * rank]).astype(BF16)
    qkv = (dot(n1, w_in) + dot(u, qkv_lift)).astype(BF16)
    (qkv,) = advance(qkv)

    steps = [[h * half + i for i in range(half)] for h in range(2)]
    per_side = width // PAIR
    pairs = per_side * sides
    near, group_count = (per_side, sides) if half == 1 else (1, pairs // half)

    def to_heads(array, thirds_each):
        if half == 1:
            return array
        cells = array.reshape(array.shape[0], sides, thirds_each, per_side, PAIR)
        cells = jnp.transpose(cells, (0, 1, 3, 2, 4)).reshape(array.shape[0], pairs, -1)
        moved = lax.all_to_all(cells, "context", 1, 0, axis_index_groups=steps, tiled=True)
        return moved.reshape(moved.shape[0], -1)

    def to_rows(array, thirds_each):
        if half == 1:
            return array
        cells = array.reshape(array.shape[0], pairs // half, -1)
        moved = lax.all_to_all(cells, "context", 0, 1, axis_index_groups=steps, tiled=True)
        moved = moved.reshape(moved.shape[0], sides, per_side, thirds_each, PAIR)
        return jnp.transpose(moved, (0, 1, 3, 2, 4)).reshape(moved.shape[0], -1)

    qkv_heads = to_heads(qkv, 3)
    o_heads = None
    logs = []
    for group in range(group_count):
        o_heads, lse = attend(qkv_heads, group, near, o_heads)
        logs.append(lse)
        if group == 0:
            o_heads, qkv_heads = advance(o_heads, qkv_heads)
    o = to_rows(o_heads, 1)
    attn_far = dot_nt(o[rows:], w_out)
    c_part = dot_nt(o, proj_t)
    attn_far, c_part = advance(attn_far, c_part)
    attn_sum = swap(attn_far) + dot_nt(o[:rows], w_out)
    c_own = (c_part[:rows] + swap(c_part[rows:])).astype(BF16)
    h = x_all[:rows] + layer_scale[0] * (attn_sum + dot(c_own, out_t[0]))
    normed, unit_two, inverse_two = normalize(h, ln2_gain, ln2_bias)
    n2_own = normed.astype(BF16)
    gy_other = swap(gy_own)
    n2 = pair_up(n2_own, swap(n2_own))
    f = dot_nt(n2, down_t[3 * rank :]).astype(BF16)
    gy_all = pair_up(gy_own, gy_other)
    gb = (gy_all.astype(F32) * layer_scale[1]).astype(BF16)
    gm = dot_nt(gb, out_t[1]).astype(BF16)
    if ringed:
        f, gm = advance(f, gm)
        ff_parts = [part for i in range(shards) for part in (ff[i], ff_crossed[i])]
    else:
        ff_parts = fc1_parts + fc2_parts
    branch_own, branch_far, gn2_own, gn2_far, rank_own, rank_far, g_fc1, g_fc2 = mlp(
        n2, gb, f, gm, ff_parts, ff_moves, ff_place, fc1_lift, fc2_t, rows
    )
    ranks = rank_own + swap(rank_far)
    m_own = ranks[:, :rank].astype(BF16)
    gf_own = ranks[:, rank:].astype(BF16)
    branch = branch_own + swap(branch_far).astype(F32) + dot(m_own, out_t[1])
    result_own = (h + layer_scale[1] * branch).astype(BF16)
    gn2 = gn2_own + swap(gn2_far) + dot(gf_own, down_t[3 * rank :])
    g_out1 = dot_tn(m_own, gb[:rows])
    g_down3 = dot_tn(gf_own, n2_own)
    result_own, gn2, g_out1, g_down3 = fence(result_own, gn2, g_out1, g_down3)
    sent = [lax.ppermute(result_own, plane, to_home[far]) for far in range(sides)]

    cut = model // 2
    one = jnp.where(context % half == 0, mine, 0)
    mark = jnp.full((rank, 128), one).astype(BF16)

    def halves(shared):
        shared = jnp.stack(shared)
        away = lax.dynamic_slice_in_dim(shared, (1 - core) * cut, cut, 2)
        keep = lax.dynamic_slice_in_dim(shared, core * cut, cut, 2)
        both = keep + swap(away)
        return [both[j] for j in range(len(both))]

    def to_sides(slices, shared):
        packed = []
        for far in range(sides):
            pack = jnp.concatenate([part.astype(BF16) for part in slices[far] + shared] + [mark], axis=1)
            if far:
                send = [(i, (i - 2 * far) % tensors) for i in range(tensors)]
                pack = lax.ppermute(pack, "tensor", send)
            packed.append(pack)
        return jnp.stack(packed)

    def to_contexts(block):
        if half > 1:
            total = lax.psum(block.astype(F32), "context", axis_index_groups=steps)
            block = total.astype(BF16)
            opposite = [(i, (i + half) % contexts) for i in range(contexts)]
        else:
            opposite = ring["context"]
        return pair_up(block, lax.ppermute(block, "context", opposite))

    def columns(array, far, size):
        return array[:, far * size : (far + 1) * size]

    def both_cores(parts):
        return [item for part in parts for item in (part, swap(part))]

    early = to_sides(
        [[columns(g_fc1, far, hidden), columns(g_fc2, far, hidden)] for far in range(sides)],
        halves([g_down3, g_out1]),
    )
    gh = gy_own.astype(F32) + norm_back(gn2, unit_two, inverse_two, ln2_gain)
    gattn_own = (layer_scale[0] * gh).astype(BF16)
    gattn_own, early = fence(gattn_own, early)
    gattn = pair_up(gattn_own, swap(gattn_own))
    early = to_contexts(early)
    g_out0 = dot_tn(c_own, gattn_own)
    gc = dot_nt(gattn, out_t[0]).astype(BF16)
    g_proj = dot_tn(gc, o)
    mid = to_sides([[columns(g_proj, far, width)] for far in range(sides)], halves([g_out0]))
    go = (dot(gattn, w_out) + dot(gc, proj_t)).astype(BF16)
    early, mid, go = fence(early, mid, go)
    early_line = [early, hop(early, "shard")]
    mid = to_contexts(mid)
    go_heads = to_heads(go, 1)
    g_heads = None
    for group in range(group_count):
        g_heads = attend_back(qkv_heads, go_heads, o_heads, logs[group], group, near, g_heads)
        if group == 0:
            got = fence(g_heads, early_line[-1], mid, *sent)
            g_heads, early_line[-1], mid, sent = got[0], got[1], got[2], got[3:]
            early_line.append(hop(early_line[-1], "shard"))
            mid_line = [mid, hop(mid, "shard")]
            sent = both_cores(sent)
    got = fence(g_heads, early_line[-1], mid_line[-1], *sent)
    g_heads, early_line[-1], mid_line[-1], sent = got[0], got[1], got[2], got[3:]
    for _ in range(3, shards):
        early_line.append(hop(early_line[-1], "shard"))
    mid_line.append(hop(mid_line[-1], "shard"))
    g = to_rows(g_heads, 3)

    gu_part = dot_nt(g, qkv_lift)
    gu_own = (gu_part[:rows] + swap(gu_part[rows:])).astype(BF16)
    gn1_far = swap(dot_nt(g[rows:], w_in))
    g_up = dot_tn(u, g)
    gn1 = dot_nt(g[:rows], w_in) + gn1_far + dot(gu_own, down_t[: 3 * rank])
    g_down = dot_tn(gu_own, n1[:rows])
    late_slices = [
        [
            g_up[j * rank : (j + 1) * rank, (far * 3 + j) * width : (far * 3 + j + 1) * width]
            for j in range(3)
        ]
        for far in range(sides)
    ]
    late = to_sides(late_slices, halves([g_down[j * rank : (j + 1) * rank] for j in range(3)]))
    input_own = gh + norm_back(gn1, unit_one[:rows], inverse_one[:rows], ln1_gain)
    input_own = input_own.astype(BF16)
    late, input_own, early_line[-1], mid_line[-1] = fence(
        late, input_own, early_line[-1], mid_line[-1]
    )
    late = to_contexts(late)
    input_sent = [lax.ppermute(input_own, plane, to_home[far]) for far in range(sides)]
    for _ in range(3, shards):
        mid_line.append(hop(mid_line[-1], "shard"))

    aways = np.repeat(np.arange(sides), 2)
    flips = np.tile([0, 1], sides)
    where = (2 * ((side - aways) % sides) + (core ^ flips)).astype(jnp.int32)
    result = settle(sent, where, BF16)
    fc1_grad, fc2_grad, early_half = totals(early_line, (hidden, hidden, 2 * cut), adapters)
    late, result, fc1_grad, fc2_grad, early_half = fence(
        late, result, fc1_grad, fc2_grad, early_half
    )
    late_line = [late, hop(late, "shard")]
    early_twin = swap(early_half)
    late_line[1], early_half, early_twin, mid_line[-1] = fence(
        late_line[1], early_half, early_twin, mid_line[-1]
    )
    for _ in range(2, shards - 1):
        late_line.append(hop(late_line[-1], "shard"))
    proj_grad, mid_half = totals(mid_line, (width, cut), adapters)
    mid_twin = swap(mid_half)
    out_grad = spread(
        core, [mid_half, mid_twin, early_half, early_twin], ((0, 0), (1, 1)), cut
    )
    got = fence(late_line[-1], out_grad, proj_grad, *input_sent)
    late_line[-1], out_grad, proj_grad, input_sent = got[0], got[1], got[2], got[3:]
    if shards > 2:
        late_line.append(hop(late_line[-1], "shard"))
    got = fence(late_line[-1], *both_cores(input_sent))
    late_line[-1], input_sent = got[0], got[1:]
    qkv_grad, late_half = totals(late_line, (3 * width, 3 * cut), adapters)
    late_twin = swap(late_half)
    input_grad = settle(input_sent, where, F32)
    down_grad = spread(
        core,
        [late_half, late_twin, early_half, early_twin],
        ((0, 0), (0, 1), (0, 2), (1, 0)),
        cut,
    )
    qkv_grad = jnp.transpose(qkv_grad.reshape(adapters, rank, 3, width), (0, 2, 1, 3))
    return (
        result,
        input_grad,
        jnp.transpose(down_grad, (0, 1, 3, 2)),
        qkv_grad,
        fc1_grad,
        jnp.transpose(proj_grad, (0, 2, 1)),
        jnp.transpose(fc2_grad, (0, 2, 1)),
        out_grad,
    )


def solution(mesh):
    sizes = (mesh.shape["shard"], mesh.shape["context"], mesh.shape["tensor"])
    placed = (
        P("shard", "context", None),
        P("shard", "context", None),
        P("shard"),
        P(),
        P(),
        P(),
        P(),
        P(),
        P(("shard", "context"), None, "tensor"),
        P(("shard", "context"), "tensor"),
        P(("shard", "context"), "tensor"),
        P(("shard", "context"), "tensor"),
        P(),
        P(None, None, None, "tensor"),
        P(None, None, "tensor"),
        P(None, "tensor", None),
        P(None, "tensor", None),
        P(),
    )
    return jax.shard_map(
        functools.partial(per_device, sizes),
        mesh=mesh,
        in_specs=placed,
        out_specs=(
            P("shard", "context", None),
            P("shard", "context", None),
            P(),
            P(None, None, None, "tensor"),
            P(None, None, "tensor"),
            P(None, "tensor", None),
            P(None, "tensor", None),
            P(),
        ),
        check_vma=False,
    )
```

```python
import functools
import math

import jax
import jax.numpy as jnp
import numpy as np
from jax import lax
from jax.experimental import pallas as pl
from jax.experimental.pallas import tpu as pltpu
from jax.sharding import PartitionSpec as P

HEAD_DIM = 64
PAIR = 2 * HEAD_DIM
EPS = 1e-06
LOG2E = math.log2(math.e)
SCORE = 1.0 / math.sqrt(HEAD_DIM)
F32 = jnp.float32
BF16 = jnp.bfloat16
NT = (((1,), (1,)), ((), ()))
TN = (((0,), (0,)), ((), ()))
BRIEF = pl.CostEstimate(flops=1000, bytes_accessed=1000, transcendentals=0)


def dot(a, b):
    return jnp.dot(a, b, preferred_element_type=F32)


def dot_nt(a, b):
    return lax.dot_general(a, b, NT, preferred_element_type=F32)


def dot_tn(a, b):
    return lax.dot_general(a, b, TN, preferred_element_type=F32)


def head_masks(rows):
    lane = lax.broadcasted_iota(jnp.int32, (rows, PAIR), 1)
    return lane < HEAD_DIM


def attend_kernel(block, q_ref, k_ref, v_ref, _, o_ref, lse_ref):
    rows = q_ref.shape[0]
    keys = k_ref[...]
    values = jnp.concatenate([v_ref[...], jnp.ones((rows, PAIR), BF16)], axis=1)
    first = head_masks(block)

    def step(i, carry):
        at = pl.ds(pl.multiple_of(i * block, block), block)
        q = q_ref[at, :]
        outs = []
        logs = []
        for head in range(2):
            mine = first if head == 0 else jnp.logical_not(first)
            s = dot_nt(jnp.where(mine, q, jnp.zeros_like(q)), keys)
            peak = jnp.max(s, axis=1, keepdims=True)
            e = jnp.exp2((s - peak) * (SCORE * LOG2E))
            acc = dot(e.astype(BF16), values)
            total = acc[:, PAIR:]
            outs.append(acc[:, :PAIR] / total)
            logs.append(peak * (SCORE * LOG2E) + jnp.log2(total))
        o_ref[at, :] = jnp.where(first, outs[0], outs[1]).astype(BF16)
        lane = lax.broadcasted_iota(jnp.int32, (block, PAIR), 1)
        both = jnp.where(lane == 0, logs[0], logs[1])
        lse_ref[0, :, at] = jnp.transpose(both)[:8]
        return carry

    lax.fori_loop(0, rows // block, step, 0)


def thirds(rows, group, near):
    return [
        pl.BlockSpec((rows, PAIR), lambda p, j=j: (0, (group * 3 + j) * near + p))
        for j in range(3)
    ]


def attend(qkv, group, near, o):
    rows, width = qkv.shape
    pairs = width // (3 * PAIR)
    block = min(256, rows)
    anywhere = pl.BlockSpec(memory_space=pl.ANY)
    operands = [qkv, qkv, qkv, qkv if o is None else o]
    return pl.pallas_call(
        functools.partial(attend_kernel, block),
        grid=(near,),
        in_specs=thirds(rows, group, near) + [anywhere],
        out_specs=[
            pl.BlockSpec((rows, PAIR), lambda p: (0, group * near + p)),
            pl.BlockSpec((1, 8, rows), lambda p: (p, 0, 0)),
        ],
        out_shape=[
            jax.ShapeDtypeStruct((rows, pairs * PAIR), BF16),
            jax.ShapeDtypeStruct((near, 8, rows), F32),
        ],
        input_output_aliases={} if o is None else {3: 0},
        cost_estimate=BRIEF,
        name="attend",
    )(*operands)


def attend_back_kernel(
    block, near, q_ref, k_ref, v_ref, go_ref, o_ref, lse_ref, _, g_ref, gq_ref, d_ref
):
    rows = q_ref.shape[0]
    pair = pl.program_id(0)
    lanes = [pl.ds(pl.multiple_of((j * near + pair) * PAIR, PAIR), PAIR) for j in range(3)]
    first = head_masks(block)
    prod = o_ref[...].astype(F32) * go_ref[...].astype(F32)
    lane8 = lax.broadcasted_iota(jnp.int32, (8, PAIR), 1) // HEAD_DIM
    row8 = lax.broadcasted_iota(jnp.int32, (8, PAIR), 0)
    d_ref[...] = lax.dot_general(
        (lane8 == row8).astype(F32),
        prod,
        NT,
        preferred_element_type=F32,
        precision=lax.Precision.HIGHEST,
    )
    gq_ref[...] = jnp.zeros_like(gq_ref)

    def step(i, carry):
        at = pl.ds(pl.multiple_of(i * block, block), block)
        k = k_ref[at, :]
        v = v_ref[at, :]
        q = q_ref[...]
        go = go_ref[...]
        gks = []
        gvs = []
        gq = None
        for head in range(2):
            mine = first if head == 0 else jnp.logical_not(first)
            k_own = jnp.where(mine, k, jnp.zeros_like(k))
            v_own = jnp.where(mine, v, jnp.zeros_like(v))
            s = dot_nt(k_own, q)
            gp = dot_nt(v_own, go)
            p = jnp.exp2(s * (SCORE * LOG2E) - lse_ref[0, head : head + 1, :])
            gs = (p * (gp - d_ref[head : head + 1, :])).astype(BF16)
            gks.append(dot(gs, q))
            gvs.append(dot(p.astype(BF16), go))
            part = dot(jnp.transpose(k_own), gs)
            gq = part if gq is None else gq + part
        gq_ref[...] += gq
        g_ref[at, lanes[1]] = (jnp.where(first, gks[0], gks[1]) * SCORE).astype(BF16)
        g_ref[at, lanes[2]] = jnp.where(first, gvs[0], gvs[1]).astype(BF16)
        return carry

    lax.fori_loop(0, rows // block, step, 0)
    g_ref[:, lanes[0]] = (jnp.transpose(gq_ref[...]) * SCORE).astype(BF16)


def attend_back(qkv, go, o, lse, group, near, g):
    rows, width = qkv.shape
    block = min(256, rows)
    mine = pl.BlockSpec((rows, PAIR), lambda p: (0, group * near + p))
    anywhere = pl.BlockSpec(memory_space=pl.ANY)
    operands = [qkv, qkv, qkv, go, o, lse, qkv if g is None else g]
    return pl.pallas_call(
        functools.partial(attend_back_kernel, block, near),
        grid=(near,),
        in_specs=thirds(rows, group, near)
        + [mine, mine, pl.BlockSpec((1, 8, rows), lambda p: (p, 0, 0)), anywhere],
        out_specs=pl.BlockSpec((rows, 3 * near * PAIR), lambda p: (0, group)),
        out_shape=jax.ShapeDtypeStruct((rows, width), BF16),
        scratch_shapes=[pltpu.VMEM((PAIR, rows), F32), pltpu.VMEM((8, rows), F32)],
        input_output_aliases={} if g is None else {6: 0},
        cost_estimate=BRIEF,
        name="attend_back",
    )(*operands)


def mlp_kernel(
    block,
    own,
    moves,
    pieces,
    place_ref,
    gb_ref,
    down_ref,
    up_ref,
    u1_ref,
    d2_ref,
    n_own,
    n_far,
    *refs,
):
    parts = refs[:pieces]
    outs, scratch = refs[pieces : pieces + 10], refs[pieces + 10 :]
    branch_own, branch_far, gn_own, gn_far = outs[:4]
    m_own, m_far, gf_own, gf_far, gf1_ref, gf2_ref = outs[4:]
    w1_all, w2_all, n_ref, f_ref, gm_ref, branch_ref, gn_ref, m_ref, gf_ref, sems = scratch
    rows = n_ref.shape[0]
    chunk = u1_ref.shape[1]
    at_chunk = pl.ds(pl.multiple_of(pl.program_id(0) * chunk, chunk), chunk)

    @pl.when(pl.program_id(0) == 0)
    def _():
        copies = [
            pltpu.make_async_copy(n_own, n_ref.at[:own, :], sems.at[len(moves)]),
            pltpu.make_async_copy(n_far, n_ref.at[own:, :], sems.at[len(moves) + 1]),
        ]
        for k, (part, start, depth, which) in enumerate(moves):
            width = parts[part].shape[1]
            down = pl.ds(pl.multiple_of(place_ref[0, k] * depth, depth), depth)
            along = pl.ds(pl.multiple_of(place_ref[1, k] * width, width), width)
            copies.append(
                pltpu.make_async_copy(
                    parts[part].at[pl.ds(start, depth), :],
                    (w1_all, w2_all)[which].at[down, along],
                    sems.at[k],
                )
            )
        for copy in copies:
            copy.start()
        branch_ref[...] = jnp.zeros_like(branch_ref)
        gn_ref[...] = jnp.zeros_like(gn_ref)
        m_ref[...] = jnp.zeros_like(m_ref)
        gf_ref[...] = jnp.zeros_like(gf_ref)
        gm_ref[...] = dot_nt(gb_ref[...], up_ref[...]).astype(BF16)
        for copy in copies:
            copy.wait()
        f_ref[...] = dot_nt(n_ref[...], down_ref[...]).astype(BF16)

    gf1_ref[...] = jnp.zeros_like(gf1_ref)
    gf2_ref[...] = jnp.zeros_like(gf2_ref)

    def step(i, carry):
        at = pl.ds(pl.multiple_of(i * block, block), block)
        w1 = w1_all[:, at_chunk]
        w2 = w2_all[:, at_chunk]
        u1 = u1_ref[...]
        d2 = d2_ref[...]
        z = dot(n_ref[at, :], w1) + dot(f_ref[at, :], u1)
        cdf = 0.5 * (1.0 + lax.erf(z * (1.0 / math.sqrt(2.0))))
        a = (z * cdf).astype(BF16)
        slope = cdf + z * (jnp.exp2(z * z * (-0.5 * LOG2E)) * (1.0 / math.sqrt(2.0 * math.pi)))
        ga = dot(gb_ref[at, :], w2) + dot(gm_ref[at, :], d2)
        gz = (ga * slope).astype(BF16)
        branch_ref[at, :] += dot_nt(a, w2)
        m_ref[at, :] += dot_nt(a, d2)
        gn_ref[at, :] += dot_nt(gz, w1)
        gf_ref[at, :] += dot_nt(gz, u1)
        gf1_ref[...] += dot_tn(f_ref[at, :], gz)
        gf2_ref[...] += dot_tn(gm_ref[at, :], a)
        return carry

    lax.fori_loop(0, rows // block, step, 0)

    @pl.when(pl.program_id(0) == pl.num_programs(0) - 1)
    def _():
        branch_own[...] = branch_ref[:own, :]
        branch_far[...] = branch_ref[own:, :].astype(BF16)
        gn_own[...] = gn_ref[:own, :]
        gn_far[...] = gn_ref[own:, :]
        m_own[...] = m_ref[:own, :]
        m_far[...] = m_ref[own:, :]
        gf_own[...] = gf_ref[:own, :]
        gf_far[...] = gf_ref[own:, :]


def mlp(n_own, n_far, gb, down, up, parts, moves, place, u1, d2):
    own, model = n_own.shape
    rows = gb.shape[0]
    hidden = u1.shape[1]
    rank = down.shape[0]
    chunk = min(512, hidden)
    block = min(256, rows)
    whole = lambda shape: pl.BlockSpec(shape, lambda j, place: (0, 0))
    part = lambda depth: pl.BlockSpec((depth, chunk), lambda j, place: (0, j))
    far = rows - own
    shapes = [
        ((own, model), F32),
        ((far, model), BF16),
        ((own, model), F32),
        ((far, model), F32),
        ((own, rank), F32),
        ((far, rank), F32),
        ((own, rank), F32),
        ((far, rank), F32),
    ]
    return pl.pallas_call(
        functools.partial(mlp_kernel, block, own, moves, len(parts)),
        grid_spec=pltpu.PrefetchScalarGridSpec(
            num_scalar_prefetch=1,
            grid=(hidden // chunk,),
            in_specs=[
                whole((rows, model)),
                whole((rank, model)),
                whole((rank, model)),
                part(rank),
                part(rank),
            ]
            + [pl.BlockSpec(memory_space=pl.ANY)] * (2 + len(parts)),
            out_specs=[whole(shape) for shape, _ in shapes] + [part(rank), part(rank)],
            scratch_shapes=[
                pltpu.VMEM((model, hidden), BF16),
                pltpu.VMEM((model, hidden), BF16),
                pltpu.VMEM((rows, model), BF16),
                pltpu.VMEM((rows, rank), BF16),
                pltpu.VMEM((rows, rank), BF16),
                pltpu.VMEM((rows, model), F32),
                pltpu.VMEM((rows, model), F32),
                pltpu.VMEM((rows, rank), F32),
                pltpu.VMEM((rows, rank), F32),
                pltpu.SemaphoreType.DMA((len(moves) + 2,)),
            ],
        ),
        out_shape=[jax.ShapeDtypeStruct(*shape) for shape in shapes]
        + [jax.ShapeDtypeStruct((rank, hidden), F32)] * 2,
        cost_estimate=BRIEF,
        name="mlp",
    )(place, gb, down, up, u1, d2, n_own, n_far, *parts)


def project_kernel(moves, pieces, block, place_ref, n_ref, u_ref, lift_ref, *refs):
    parts, (w_in, w_out, qkv_ref, sems) = refs[:pieces], refs[pieces:]
    copies = []
    column = 0
    for j, out in enumerate((w_in, w_out)):
        width = out.shape[1] // 2
        for k, (part, start, depth) in enumerate(moves):
            down = pl.ds(pl.multiple_of(place_ref[0, k] * depth, depth), depth)
            along = pl.ds(pl.multiple_of(place_ref[1, k] * width, width), width)
            copies.append(
                pltpu.make_async_copy(
                    parts[part].at[pl.ds(start, depth), pl.ds(column, width)],
                    out.at[down, along],
                    sems.at[j, k],
                )
            )
        column += width
    for copy in copies:
        copy.start()
    for copy in copies[: len(moves)]:
        copy.wait()

    def step(i, carry):
        at = pl.ds(pl.multiple_of(i * block, block), block)
        sums = dot(n_ref[at, :], w_in[...]) + dot(u_ref[at, :], lift_ref[...])
        qkv_ref[at, :] = sums.astype(BF16)
        return carry

    lax.fori_loop(0, n_ref.shape[0] // block, step, 0)
    for copy in copies[len(moves) :]:
        copy.wait()


def project(n, u, lift, parts, moves, place, width):
    rows, model = n.shape
    block = min(256, rows)
    whole = lambda shape: pl.BlockSpec(shape, lambda i, place: (0, 0))
    shapes = [(model, 6 * width), (model, 2 * width), (rows, 6 * width)]
    return pl.pallas_call(
        functools.partial(project_kernel, moves, len(parts), block),
        grid_spec=pltpu.PrefetchScalarGridSpec(
            num_scalar_prefetch=1,
            grid=(1,),
            in_specs=[whole(n.shape), whole(u.shape), whole(lift.shape)]
            + [pl.BlockSpec(memory_space=pl.ANY)] * len(parts),
            out_specs=[whole(shape) for shape in shapes],
            scratch_shapes=[pltpu.SemaphoreType.DMA((2, len(moves)))],
        ),
        out_shape=[jax.ShapeDtypeStruct(shape, BF16) for shape in shapes],
        cost_estimate=BRIEF,
        name="project",
    )(place, n, u, lift, *parts)


def pick_kernel(sides, _, *refs):
    sources, outs = refs[: 4 * sides], refs[4 * sides :]
    for far, out in enumerate(outs):
        up, fc1, proj, fc2 = sources[4 * far : 4 * far + 4]
        column = 0
        for piece in [up[0, 0], up[0, 1], up[0, 2], fc1[0], proj[0], fc2[0]]:
            out[:, column : column + piece.shape[1]] = piece
            column += piece.shape[1]


def pick(chosen, ups):
    rank = ups[1].shape[1]
    wide = sum(up.shape[-1] for up in ups) + 2 * ups[0].shape[-1]
    sides = chosen.shape[0]
    specs = [
        pl.BlockSpec(
            (1,) + up.shape[1:],
            lambda i, e, far=far, n=up.ndim: (e[far],) + (0,) * (n - 1),
        )
        for far in range(sides)
        for up in ups
    ]
    return pl.pallas_call(
        functools.partial(pick_kernel, sides),
        grid_spec=pltpu.PrefetchScalarGridSpec(
            num_scalar_prefetch=1,
            grid=(1,),
            in_specs=specs,
            out_specs=[pl.BlockSpec((rank, wide), lambda i, e: (0, 0))] * sides,
        ),
        out_shape=[jax.ShapeDtypeStruct((rank, wide), BF16)] * sides,
        name="pick",
    )(chosen, *(list(ups) * sides))


def lifts_kernel(sizes, *refs):
    packs, (qkv_ref, fc1_ref, proj_ref, fc2_ref) = refs[:-4], refs[-4:]
    rank = fc1_ref.shape[0]
    width, hidden = sizes
    qkv_ref[...] = jnp.zeros_like(qkv_ref)
    for far, pack in enumerate(packs):
        for j in range(3):
            column = (3 * far + j) * width
            qkv_ref[j * rank : (j + 1) * rank, column : column + width] = pack[
                :, j * width : (j + 1) * width
            ]
        start = 3 * width
        for ref, size in ((fc1_ref, hidden), (proj_ref, width), (fc2_ref, hidden)):
            ref[:, far * size : (far + 1) * size] = pack[:, start : start + size]
            start += size


def lifts(packs, width, hidden):
    rank = packs[0].shape[0]
    sides = len(packs)
    shapes = [(3 * rank, 3 * width), (rank, hidden), (rank, width), (rank, hidden)]
    return pl.pallas_call(
        functools.partial(lifts_kernel, (width, hidden)),
        out_shape=[jax.ShapeDtypeStruct((r, sides * c), BF16) for r, c in shapes],
        name="lifts",
    )(*packs)


def totals_kernel(blocks, widths, *refs):
    sources, outs = refs[:blocks], refs[blocks:]
    for out in outs:
        out[...] = jnp.zeros_like(out)
    total = sum(widths)
    for source in sources:
        for k in range(source.shape[0]):
            owner = jnp.max(source[k, :, total:].astype(F32)).astype(jnp.int32)
            column = 0
            for out, width in zip(outs, widths):
                out[owner] += source[k, :, column : column + width].astype(F32)
                column += width


def totals(blocks, widths, adapters):
    rank = blocks[0].shape[1]
    return pl.pallas_call(
        functools.partial(totals_kernel, len(blocks), widths),
        out_shape=[jax.ShapeDtypeStruct((adapters, rank, width), F32) for width in widths],
        name="totals",
    )(*blocks)


def spread_kernel(order, core_ref, *refs):
    halves, target = refs[:-1], refs[-1]
    cut = target.shape[3] // 2
    first = core_ref[0] == 0
    for j, (pair, k) in enumerate(order):
        own = halves[2 * pair][:, :, k * cut : (k + 1) * cut]
        other = halves[2 * pair + 1][:, :, k * cut : (k + 1) * cut]
        target[:, j, :, :cut] = jnp.where(first, own, other)
        target[:, j, :, cut:] = jnp.where(first, other, own)


def spread(core, halves, order, cut):
    adapters, rank, _ = halves[0].shape
    return pl.pallas_call(
        functools.partial(spread_kernel, order),
        in_specs=[pl.BlockSpec(memory_space=pltpu.SMEM)]
        + [pl.BlockSpec(memory_space=pltpu.VMEM)] * len(halves),
        out_shape=jax.ShapeDtypeStruct((adapters, len(order), rank, 2 * cut), F32),
        name="spread",
    )(jnp.reshape(core, (1,)), *halves)


def settle_kernel(count, where_ref, *refs):
    parts, out = refs[:count], refs[-1]
    for k, part in enumerate(parts):

        @pl.when(pl.program_id(0) == k)
        def _():
            out[0] = part[...].astype(out.dtype)


def settle(parts, where, kind, images, base=None):
    rows, model = parts[0].shape
    extra = [] if base is None else [base]
    return pl.pallas_call(
        functools.partial(settle_kernel, len(parts)),
        grid_spec=pltpu.PrefetchScalarGridSpec(
            num_scalar_prefetch=1,
            grid=(len(parts),),
            in_specs=[pl.BlockSpec((rows, model), lambda k, where: (0, 0))] * len(parts)
            + [pl.BlockSpec(memory_space=pl.ANY)] * len(extra),
            out_specs=pl.BlockSpec((1, rows, model), lambda k, where: (where[k], 0, 0)),
        ),
        out_shape=jax.ShapeDtypeStruct((images, rows, model), kind),
        input_output_aliases={1 + len(parts): 0} if extra else {},
        name="settle",
    )(where, *parts, *extra)


def normalize(values, gain, shift):
    centre = values - jnp.mean(values, axis=-1, keepdims=True)
    inverse = lax.rsqrt(jnp.mean(centre * centre, axis=-1, keepdims=True) + EPS)
    unit = centre * inverse
    return unit * gain + shift, unit, inverse


def norm_back(grad, unit, inverse, gain):
    scaled = grad * gain
    centred = scaled - jnp.mean(scaled, axis=-1, keepdims=True)
    return inverse * (centred - unit * jnp.mean(scaled * unit, axis=-1, keepdims=True))


def per_device(
    sizes,
    tokens,
    cotangent,
    adapter_index,
    ln1_gain,
    ln1_bias,
    ln2_gain,
    ln2_bias,
    layer_scale,
    w_qkv,
    w_proj,
    w_fc1,
    w_fc2,
    down_in,
    qkv_up,
    fc1_up,
    proj_down,
    fc2_down,
    out_up,
):
    shards, contexts, tensors = sizes
    half = contexts // 2
    sides = tensors // 2
    images, rows, model = tokens.shape
    rank = down_in.shape[-1]
    depth = w_fc1.shape[0]
    width = w_proj.shape[1]
    hidden = w_fc1.shape[1]
    pairs = width // PAIR
    adapters = down_in.shape[0]
    shard = lax.axis_index("shard")
    context = lax.axis_index("context")
    tensor = lax.axis_index("tensor")
    side, core = tensor // 2, tensor % 2
    high = context // half

    ring = {
        "shard": [(i, (i + 1) % shards) for i in range(shards)],
        "context": [(i, (i + 1) % contexts) for i in range(contexts)],
        "tensor": [(i, (i + 2) % tensors) for i in range(tensors)],
    }
    count = {"shard": shards, "context": contexts, "tensor": sides}
    twin = [(i, i ^ 1) for i in range(tensors)]
    plane = ("context", "tensor")

    def hop(value, axis):
        return lax.ppermute(value, axis, ring[axis])

    def swap(value):
        return lax.ppermute(value, "tensor", twin)

    def around(value, axis):
        out = [value]
        for _ in range(count[axis] - 1):
            out.append(hop(out[-1], axis))
        return out

    def fence(*values):
        return lax.optimization_barrier(values)

    to_owner = []
    to_home = {far: [] for far in range(sides)}
    for c in range(contexts):
        for s in range(sides):
            for k in range(2):
                here = c * tensors + 2 * s + k
                source = 2 * (c % half) + k
                to_owner.append((source * tensors + 2 * s + c // half, here))
                for far in range(sides):
                    there = (s + far) % sides
                    to_home[far].append((here, source * tensors + 2 * there + c // half))

    ringed = contexts == 2 and sides == 2 and shards == 4
    cross = {0: [], 1: []}
    if ringed:
        for c in range(2):
            for s in range(2):
                for k in range(2):
                    here = c * tensors + 2 * s + k
                    along = c * tensors + 2 * (1 - s) + k
                    aside = (1 - c) * tensors + 2 * s + k
                    cross[0].append((here, along if k == 0 else aside))
                    cross[1].append((here, aside if k == 0 else along))

    def block_of(array, index):
        return lax.dynamic_index_in_dim(array, index, 0, keepdims=False)

    def deliver(value, pairs):
        stay = np.zeros(contexts * tensors, np.int32)
        for a, b in pairs:
            stay[a] = a == b
        got = lax.ppermute(value, plane, [(a, b) for a, b in pairs if a != b])
        if not stay.any():
            return got
        return jnp.where(jnp.asarray(stay)[context * tensors + tensor] == 1, value, got)

    def pair_up(a, b):
        return jnp.concatenate([a, b], axis=0)

    def adapter_of(index, far):
        return block_of(index, 2 * ((side + far) % sides) + high)

    def up_packs(index, ups):
        chosen = jnp.stack([adapter_of(index, far) for far in range(sides)])
        packs = list(pick(chosen, ups))
        for far in range(1, sides):
            send = [(i, (i + 2 * far) % tensors) for i in range(tensors)]
            packs[far] = lax.ppermute(packs[far], "tensor", send)
        return packs

    attn_own = jnp.concatenate([w_qkv[:, j] for j in range(3)] + [w_proj], axis=1)
    ups = (qkv_up, fc1_up, jnp.transpose(proj_down, (0, 2, 1)), jnp.transpose(fc2_down, (0, 2, 1)))
    flows = {}

    def cross_to(value, turn):
        return lax.ppermute(value, plane, cross[turn])

    if ringed:
        z, b, c, d = [attn_own], [], [], []
        ff_own = pair_up(w_fc1, w_fc2)
        got = fence(
            hop(attn_own, "shard"),
            cross_to(attn_own, 0),
            cross_to(attn_own, 1),
            deliver(block_of(tokens, tensor), to_owner),
            hop(ff_own, "shard"),
            ff_own,
            cotangent,
            adapter_index,
            down_in,
            out_up,
            *ups,
        )
        z.append(got[0])
        b.append(got[1])
        c.append(got[2])
        x_own = got[3]
        own = [got[5], got[4]]
        cotangent, adapter_index, down_in, out_up = got[6:10]
        ups = got[10:]
        got = fence(
            hop(z[1], "shard"),
            cross_to(z[1], 0),
            cross_to(z[1], 1),
            cross_to(b[0], 1),
            cross_to(own[0], 0),
            x_own,
            own[1],
            adapter_index,
            *ups,
        )
        z.append(got[0])
        b.append(got[1])
        c.append(got[2])
        d.append(got[3])
        aside = [got[4]]
        x_own, own[1], adapter_index = got[5:8]
        ups = got[8:]
        got = fence(
            hop(z[2], "shard"),
            cross_to(z[2], 0),
            cross_to(z[2], 1),
            cross_to(b[1], 1),
            swap(x_own),
            x_own,
            own[1],
            aside[0],
        )
        z.append(got[0])
        b.append(got[1])
        c.append(got[2])
        d.append(got[3])
        x_other, x_own, own[1], aside[0] = got[4:]
        packs = up_packs(adapter_index, ups)
        own.append(hop(own[1], "shard"))
        aside.append(hop(aside[0], "shard"))
        got = fence(cross_to(z[3], 0), cross_to(z[3], 1), cross_to(b[2], 1), cotangent)
        b.append(got[0])
        c.append(got[1])
        d.append(got[2])
        cotangent = got[3]
        last = cross_to(b[3], 1)
        own_over, aside_over = [], []

        step_of = np.repeat(np.arange(shards), 4)
        near_0 = np.tile([0, 0, 1, 1], shards)
        far_0 = np.tile([0, 1, 0, 1], shards)
        near = jnp.where(core == 0, near_0, far_0)
        across = jnp.where(core == 0, far_0, near_0)
        row = (shard - step_of) % shards * contexts + (context - near) % contexts
        attn_place = jnp.stack([row, across]).astype(jnp.int32)
        attn_moves = [(k, 0, depth) for k in range(4 * shards)]
        ff_moves = [(k, which * depth, depth, which) for which in range(2) for k in range(4 * shards)]
        ff_place = jnp.concatenate([attn_place, attn_place], axis=1)
        gy_own = None

        def start(*values):
            got = fence(*values, last, packs[1], own[0], aside[0])
            d.append(got[-4])
            packs[1], own[0], aside[0] = got[-3:]
            own_over.append(cross_to(own[0], 1))
            aside_over.append(cross_to(aside[0], 1))
            return got[:-4]

        def advance(stage, *values):
            count = len(values)
            if stage == 0:
                got = fence(*values, own[2], aside[1], own_over[0], aside_over[0])
                own[2], aside[1], own_over[0], aside_over[0] = got[count:]
                own.append(hop(own[2], "shard"))
                own_over.append(cross_to(own[1], 1))
                aside_over.append(cross_to(aside[1], 1))
            elif stage == 1:
                got = fence(*values, own[3], own_over[1], aside_over[1], aside[1], cotangent)
                own[3], own_over[1], aside_over[1], aside[1], late_cotangent = got[count:]
                aside.append(hop(aside[1], "shard"))
                own_over.append(cross_to(own[2], 1))
                return (*got[:count], deliver(block_of(late_cotangent, tensor), to_owner))
            elif stage == 2:
                got = fence(*values, aside[2], own_over[2])
                aside[2], own_over[2] = got[count:]
                aside.append(hop(aside[2], "shard"))
                own_over.append(cross_to(own[3], 1))
                aside_over.append(cross_to(aside[2], 1))
            else:
                got = fence(*values, aside[3], own_over[3], aside_over[2])
                aside[3], own_over[3], aside_over[2] = got[count:]
                aside_over.append(cross_to(aside[3], 1))
            return got[:count]

    else:

        def gather_plain(value):
            whole = lax.all_gather(value, ("shard", "context"), axis=0, tiled=True)
            return around(whole, "tensor")

        attn_parts = gather_plain(attn_own)
        fc1_parts = gather_plain(w_fc1)
        fc2_parts = gather_plain(w_fc2)
        packs = up_packs(adapter_index, ups)
        x_own = deliver(block_of(tokens, tensor), to_owner)
        x_other = swap(x_own)
        gy_own = deliver(block_of(cotangent, tensor), to_owner)
        attn_moves = [(k, 0, model) for k in range(sides)]
        attn_place = jnp.asarray([[0] * sides, list(range(sides))], jnp.int32)
        ff_moves = [(k, 0, model, k // sides) for k in range(2 * sides)]
        ff_place = jnp.concatenate([attn_place, attn_place], axis=1)

        def start(*values):
            return values

        def advance(stage, *values):
            return (*values, gy_own) if stage == 1 else values

    mine = adapter_of(adapter_index, 0)
    down = block_of(down_in, mine)
    down_t = jnp.transpose(down, (0, 2, 1)).reshape(4 * rank, model)
    out_t = block_of(out_up, mine)

    x_all = pair_up(x_own, x_other).astype(F32)
    normed, unit_one, inverse_one = normalize(x_all, ln1_gain, ln1_bias)
    n1 = normed.astype(BF16)
    u = dot_nt(n1, down_t[: 3 * rank]).astype(BF16)
    n1, u = start(n1, u)
    qkv_lift, fc1_lift, proj_t, fc2_t = lifts(packs, width, hidden)
    if ringed:
        attn_parts = [part for i in range(shards) for part in (z[i], b[i], c[i], d[i])]
    w_in, w_out, qkv = project(n1, u, qkv_lift, attn_parts, attn_moves, attn_place, width)
    (qkv,) = advance(0, qkv)

    steps = [[h * half + i for i in range(half)] for h in range(2)]
    per_side = width // PAIR
    pairs = per_side * sides
    near, group_count = (per_side, sides) if half == 1 else (1, pairs // half)

    def to_heads(array, thirds_each):
        if half == 1:
            return array
        cells = array.reshape(array.shape[0], sides, thirds_each, per_side, PAIR)
        cells = jnp.transpose(cells, (0, 1, 3, 2, 4)).reshape(array.shape[0], pairs, -1)
        moved = lax.all_to_all(cells, "context", 1, 0, axis_index_groups=steps, tiled=True)
        return moved.reshape(moved.shape[0], -1)

    def to_rows(array, thirds_each):
        if half == 1:
            return array
        cells = array.reshape(array.shape[0], pairs // half, -1)
        moved = lax.all_to_all(cells, "context", 0, 1, axis_index_groups=steps, tiled=True)
        moved = moved.reshape(moved.shape[0], sides, per_side, thirds_each, PAIR)
        return jnp.transpose(moved, (0, 1, 3, 2, 4)).reshape(moved.shape[0], -1)

    qkv_heads = to_heads(qkv, 3)
    o_heads = None
    logs = []
    for group in range(group_count):
        o_heads, lse = attend(qkv_heads, group, near, o_heads)
        logs.append(lse)
        if group == 0:
            o_heads, qkv_heads, gy_own = advance(1, o_heads, qkv_heads)
    (o_heads,) = advance(2, o_heads)
    o = to_rows(o_heads, 1)
    attn_far = dot_nt(o[rows:], w_out)
    c_part = dot_nt(o, proj_t)
    attn_sum = swap(attn_far) + dot_nt(o[:rows], w_out)
    c_own = (c_part[:rows] + swap(c_part[rows:])).astype(BF16)
    h = x_all[:rows] + layer_scale[0] * (attn_sum + dot(c_own, out_t[0]))
    normed, unit_two, inverse_two = normalize(h, ln2_gain, ln2_bias)
    n2_own = normed.astype(BF16)
    n2_own, gy_own = advance(3, n2_own, gy_own)
    n2_far = swap(n2_own)
    gy_all = pair_up(gy_own, swap(gy_own))
    gb = (gy_all.astype(F32) * layer_scale[1]).astype(BF16)
    if ringed:
        ff_parts = [
            part
            for i in range(shards)
            for part in (own[i], aside[i], own_over[i], aside_over[i])
        ]
    else:
        ff_parts = fc1_parts + fc2_parts
    branch_own, branch_far, gn2_own, gn2_far, m_part, m_far, gf_part, gf_far, g_fc1, g_fc2 = mlp(
        n2_own, n2_far, gb, down_t[3 * rank :], out_t[1], ff_parts, ff_moves, ff_place, fc1_lift, fc2_t
    )
    m_own = (m_part + swap(m_far)).astype(BF16)
    gf_own = (gf_part + swap(gf_far)).astype(BF16)
    branch = branch_own + swap(branch_far).astype(F32) + dot(m_own, out_t[1])
    result_own = (h + layer_scale[1] * branch).astype(BF16)
    gn2 = gn2_own + swap(gn2_far) + dot(gf_own, down_t[3 * rank :])
    g_out1 = dot_tn(m_own, gb[:rows])
    g_down3 = dot_tn(gf_own, n2_own)

    cut = model // 2
    one = jnp.where(context % half == 0, mine, 0)
    mark = jnp.full((rank, 128), one).astype(BF16)

    def halves(shared):
        shared = jnp.stack(shared)
        away = lax.dynamic_slice_in_dim(shared, (1 - core) * cut, cut, 2)
        keep = lax.dynamic_slice_in_dim(shared, core * cut, cut, 2)
        both = keep + swap(away)
        return [both[j] for j in range(len(both))]

    def to_sides(slices, shared):
        packed = []
        for far in range(sides):
            pack = jnp.concatenate([part.astype(BF16) for part in slices[far] + shared] + [mark], axis=1)
            if far:
                send = [(i, (i - 2 * far) % tensors) for i in range(tensors)]
                pack = lax.ppermute(pack, "tensor", send)
            packed.append(pack)
        return jnp.stack(packed)

    def to_contexts(block):
        if half > 1:
            total = lax.psum(block.astype(F32), "context", axis_index_groups=steps)
            block = total.astype(BF16)
            opposite = [(i, (i + half) % contexts) for i in range(contexts)]
        else:
            opposite = ring["context"]
        return pair_up(block, lax.ppermute(block, "context", opposite))

    def columns(array, far, size):
        return array[:, far * size : (far + 1) * size]

    early = to_sides(
        [[columns(g_fc1, far, hidden), columns(g_fc2, far, hidden)] for far in range(sides)],
        halves([g_down3, g_out1]),
    )
    gh = gy_own.astype(F32) + norm_back(gn2, unit_two, inverse_two, ln2_gain)
    gattn_own = (layer_scale[0] * gh).astype(BF16)
    gattn_own, early = fence(gattn_own, early)
    gattn = pair_up(gattn_own, swap(gattn_own))
    early = to_contexts(early)
    g_out0 = dot_tn(c_own, gattn_own)
    gc = dot_nt(gattn, out_t[0]).astype(BF16)
    g_proj = dot_tn(gc, o)
    mid = to_sides([[columns(g_proj, far, width)] for far in range(sides)], halves([g_out0]))
    go = (dot(gattn, w_out) + dot(gc, proj_t)).astype(BF16)
    early, mid, go = fence(early, mid, go)
    early_line = [early, hop(early, "shard")]
    mid = to_contexts(mid)
    go_heads = to_heads(go, 1)
    g_heads = None
    for group in range(group_count):
        g_heads = attend_back(qkv_heads, go_heads, o_heads, logs[group], group, near, g_heads)
        if group == 0:
            g_heads, early_line[-1], mid, result_own = fence(
                g_heads, early_line[-1], mid, result_own
            )
            early_line.append(hop(early_line[-1], "shard"))
            mid_line = [mid, hop(mid, "shard")]
            sent = [deliver(result_own, to_home[far]) for far in range(sides)]
    g_heads, early_line[-1], mid_line[-1] = fence(g_heads, early_line[-1], mid_line[-1])
    for _ in range(3, shards):
        early_line.append(hop(early_line[-1], "shard"))
    g = to_rows(g_heads, 3)

    gu_part = dot_nt(g, qkv_lift)
    gu_own = (gu_part[:rows] + swap(gu_part[rows:])).astype(BF16)
    gn1_far = swap(dot_nt(g[rows:], w_in))
    g_up = dot_tn(u, g)
    gn1 = dot_nt(g[:rows], w_in) + gn1_far + dot(gu_own, down_t[: 3 * rank])
    g_down = dot_tn(gu_own, n1[:rows])
    late_slices = [
        [
            g_up[j * rank : (j + 1) * rank, (far * 3 + j) * width : (far * 3 + j + 1) * width]
            for j in range(3)
        ]
        for far in range(sides)
    ]
    late = to_sides(late_slices, halves([g_down[j * rank : (j + 1) * rank] for j in range(3)]))
    input_own = gh + norm_back(gn1, unit_one[:rows], inverse_one[:rows], ln1_gain)
    input_own = input_own.astype(BF16)
    late, input_own, early_line[-1], *sent = fence(late, input_own, early_line[-1], *sent)
    late = to_contexts(late)
    mid_line.append(hop(mid_line[-1], "shard"))
    sent += [swap(part) for part in sent]
    late, input_own, mid_line[-1], *sent = fence(late, input_own, mid_line[-1], *sent)

    aways = np.arange(sides)
    mine_at = (2 * ((side - aways) % sides) + core).astype(jnp.int32)
    twin_at = (2 * ((side - aways) % sides) + 1 - core).astype(jnp.int32)
    late_line = [late, hop(late, "shard")]
    input_sent = [deliver(input_own, to_home[far]) for far in range(sides)]
    for _ in range(3, shards):
        mid_line.append(hop(mid_line[-1], "shard"))
    result = settle(sent, jnp.concatenate([mine_at, twin_at]), BF16, images)
    fc1_grad, fc2_grad, early_half = totals(early_line, (hidden, hidden, 2 * cut), adapters)
    late_line[1], early_half, result, *mid_line = fence(
        late_line[1], early_half, result, *mid_line
    )
    for _ in range(2, shards - 1):
        late_line.append(hop(late_line[-1], "shard"))
    early_twin = swap(early_half)
    proj_grad, mid_half = totals(mid_line, (width, cut), adapters)
    mid_twin = swap(mid_half)
    got = fence(late_line[-1], proj_grad, early_half, early_twin, mid_half, mid_twin, *input_sent)
    late_line[-1], proj_grad, early_half, early_twin, mid_half, mid_twin = got[:6]
    input_sent = got[6:]
    if shards > 2:
        late_line.append(hop(late_line[-1], "shard"))
    input_twins = [swap(part) for part in input_sent]
    out_grad = spread(
        core, [mid_half, mid_twin, early_half, early_twin], ((0, 0), (1, 1)), cut
    )
    input_grad = settle(list(input_sent), mine_at, F32, images)
    late_line[-1], input_grad, out_grad, *input_twins = fence(
        late_line[-1], input_grad, out_grad, *input_twins
    )
    qkv_grad, late_half = totals(late_line, (3 * width, 3 * cut), adapters)
    late_twin = swap(late_half)
    input_grad = settle(input_twins, twin_at, F32, images, input_grad)
    down_grad = spread(
        core,
        [late_half, late_twin, early_half, early_twin],
        ((0, 0), (0, 1), (0, 2), (1, 0)),
        cut,
    )
    qkv_grad = jnp.transpose(qkv_grad.reshape(adapters, rank, 3, width), (0, 2, 1, 3))
    return (
        result,
        input_grad,
        jnp.transpose(down_grad, (0, 1, 3, 2)),
        qkv_grad,
        fc1_grad,
        jnp.transpose(proj_grad, (0, 2, 1)),
        jnp.transpose(fc2_grad, (0, 2, 1)),
        out_grad,
    )


def solution(mesh):
    sizes = (mesh.shape["shard"], mesh.shape["context"], mesh.shape["tensor"])
    placed = (
        P("shard", "context", None),
        P("shard", "context", None),
        P("shard"),
        P(),
        P(),
        P(),
        P(),
        P(),
        P(("shard", "context"), None, "tensor"),
        P(("shard", "context"), "tensor"),
        P(("shard", "context"), "tensor"),
        P(("shard", "context"), "tensor"),
        P(),
        P(None, None, None, "tensor"),
        P(None, None, "tensor"),
        P(None, "tensor", None),
        P(None, "tensor", None),
        P(),
    )
    return jax.shard_map(
        functools.partial(per_device, sizes),
        mesh=mesh,
        in_specs=placed,
        out_specs=(
            P("shard", "context", None),
            P("shard", "context", None),
            P(),
            P(None, None, None, "tensor"),
            P(None, None, "tensor"),
            P(None, "tensor", None),
            P(None, "tensor", None),
            P(),
        ),
        check_vma=False,
    )
```

```python
import functools
import math

import jax
import jax.numpy as jnp
import numpy as np
from jax import lax
from jax.experimental import pallas as pl
from jax.experimental.pallas import tpu as pltpu
from jax.sharding import PartitionSpec as P

HEAD_DIM = 64
PAIR = 2 * HEAD_DIM
EPS = 1e-06
LOG2E = math.log2(math.e)
SCORE = 1.0 / math.sqrt(HEAD_DIM)
F32 = jnp.float32
BF16 = jnp.bfloat16
NT = (((1,), (1,)), ((), ()))
TN = (((0,), (0,)), ((), ()))
BRIEF = pl.CostEstimate(flops=1000, bytes_accessed=1000, transcendentals=0)


def dot(a, b):
    return jnp.dot(a, b, preferred_element_type=F32)


def dot_nt(a, b):
    return lax.dot_general(a, b, NT, preferred_element_type=F32)


def dot_tn(a, b):
    return lax.dot_general(a, b, TN, preferred_element_type=F32)


def head_masks(rows):
    lane = lax.broadcasted_iota(jnp.int32, (rows, PAIR), 1)
    return lane < HEAD_DIM


def attend_kernel(block, q_ref, k_ref, v_ref, _, o_ref, lse_ref):
    rows = q_ref.shape[0]
    keys = k_ref[...]
    values = jnp.concatenate([v_ref[...], jnp.ones((rows, PAIR), BF16)], axis=1)
    first = head_masks(block)

    def step(i, carry):
        at = pl.ds(pl.multiple_of(i * block, block), block)
        q = q_ref[at, :]
        outs = []
        logs = []
        for head in range(2):
            mine = first if head == 0 else jnp.logical_not(first)
            s = dot_nt(jnp.where(mine, q, jnp.zeros_like(q)), keys)
            peak = jnp.max(s, axis=1, keepdims=True)
            e = jnp.exp2((s - peak) * (SCORE * LOG2E))
            acc = dot(e.astype(BF16), values)
            total = acc[:, PAIR:]
            outs.append(acc[:, :PAIR] / total)
            logs.append(peak * (SCORE * LOG2E) + jnp.log2(total))
        o_ref[at, :] = jnp.where(first, outs[0], outs[1]).astype(BF16)
        lane = lax.broadcasted_iota(jnp.int32, (block, PAIR), 1)
        both = jnp.where(lane == 0, logs[0], logs[1])
        lse_ref[0, :, at] = jnp.transpose(both)[:8]
        return carry

    lax.fori_loop(0, rows // block, step, 0)


def thirds(rows, group, near):
    return [
        pl.BlockSpec((rows, PAIR), lambda p, j=j: (0, (group * 3 + j) * near + p))
        for j in range(3)
    ]


def attend(qkv, group, near, o):
    rows, width = qkv.shape
    pairs = width // (3 * PAIR)
    block = min(256, rows)
    anywhere = pl.BlockSpec(memory_space=pl.ANY)
    operands = [qkv, qkv, qkv, qkv if o is None else o]
    return pl.pallas_call(
        functools.partial(attend_kernel, block),
        grid=(near,),
        in_specs=thirds(rows, group, near) + [anywhere],
        out_specs=[
            pl.BlockSpec((rows, PAIR), lambda p: (0, group * near + p)),
            pl.BlockSpec((1, 8, rows), lambda p: (p, 0, 0)),
        ],
        out_shape=[
            jax.ShapeDtypeStruct((rows, pairs * PAIR), BF16),
            jax.ShapeDtypeStruct((near, 8, rows), F32),
        ],
        input_output_aliases={} if o is None else {3: 0},
        cost_estimate=BRIEF,
        name="attend",
    )(*operands)


def attend_back_kernel(
    block, near, q_ref, k_ref, v_ref, go_ref, o_ref, lse_ref, _, g_ref, gq_ref, d_ref
):
    rows = q_ref.shape[0]
    pair = pl.program_id(0)
    lanes = [pl.ds(pl.multiple_of((j * near + pair) * PAIR, PAIR), PAIR) for j in range(3)]
    first = head_masks(block)
    prod = o_ref[...].astype(F32) * go_ref[...].astype(F32)
    lane8 = lax.broadcasted_iota(jnp.int32, (8, PAIR), 1) // HEAD_DIM
    row8 = lax.broadcasted_iota(jnp.int32, (8, PAIR), 0)
    d_ref[...] = lax.dot_general(
        (lane8 == row8).astype(F32),
        prod,
        NT,
        preferred_element_type=F32,
        precision=lax.Precision.HIGHEST,
    )
    gq_ref[...] = jnp.zeros_like(gq_ref)

    def step(i, carry):
        at = pl.ds(pl.multiple_of(i * block, block), block)
        k = k_ref[at, :]
        v = v_ref[at, :]
        q = q_ref[...]
        go = go_ref[...]
        gks = []
        gvs = []
        gq = None
        for head in range(2):
            mine = first if head == 0 else jnp.logical_not(first)
            k_own = jnp.where(mine, k, jnp.zeros_like(k))
            v_own = jnp.where(mine, v, jnp.zeros_like(v))
            s = dot_nt(k_own, q)
            gp = dot_nt(v_own, go)
            p = jnp.exp2(s * (SCORE * LOG2E) - lse_ref[0, head : head + 1, :])
            gs = (p * (gp - d_ref[head : head + 1, :])).astype(BF16)
            gks.append(dot(gs, q))
            gvs.append(dot(p.astype(BF16), go))
            part = dot(jnp.transpose(k_own), gs)
            gq = part if gq is None else gq + part
        gq_ref[...] += gq
        g_ref[at, lanes[1]] = (jnp.where(first, gks[0], gks[1]) * SCORE).astype(BF16)
        g_ref[at, lanes[2]] = jnp.where(first, gvs[0], gvs[1]).astype(BF16)
        return carry

    lax.fori_loop(0, rows // block, step, 0)
    g_ref[:, lanes[0]] = (jnp.transpose(gq_ref[...]) * SCORE).astype(BF16)


def attend_back(qkv, go, o, lse, group, near, g):
    rows, width = qkv.shape
    block = min(256, rows)
    mine = pl.BlockSpec((rows, PAIR), lambda p: (0, group * near + p))
    anywhere = pl.BlockSpec(memory_space=pl.ANY)
    operands = [qkv, qkv, qkv, go, o, lse, qkv if g is None else g]
    return pl.pallas_call(
        functools.partial(attend_back_kernel, block, near),
        grid=(near,),
        in_specs=thirds(rows, group, near)
        + [mine, mine, pl.BlockSpec((1, 8, rows), lambda p: (p, 0, 0)), anywhere],
        out_specs=pl.BlockSpec((rows, 3 * near * PAIR), lambda p: (0, group)),
        out_shape=jax.ShapeDtypeStruct((rows, width), BF16),
        scratch_shapes=[pltpu.VMEM((PAIR, rows), F32), pltpu.VMEM((8, rows), F32)],
        input_output_aliases={} if g is None else {6: 0},
        cost_estimate=BRIEF,
        name="attend_back",
    )(*operands)


def mlp_kernel(
    block,
    own,
    moves,
    pieces,
    place_ref,
    gb_ref,
    down_ref,
    up_ref,
    u1_ref,
    d2_ref,
    n_own,
    n_far,
    *refs,
):
    parts = refs[:pieces]
    outs, scratch = refs[pieces : pieces + 8], refs[pieces + 8 :]
    branch_own, branch_far, gn_own, gn_far = outs[:4]
    rank_own, rank_far, gf1_out, gf2_out = outs[4:]
    w1_all, w2_all, n_ref, f_ref, gm_ref, branch_ref, gn_ref = scratch[:7]
    rank_ref, gf1_ref, gf2_ref, sems, row_sems = scratch[7:]
    rank = f_ref.shape[0]
    rows = n_ref.shape[0]
    chunk = u1_ref.shape[1]
    at_chunk = pl.ds(pl.multiple_of(pl.program_id(0) * chunk, chunk), chunk)

    @pl.when(pl.program_id(0) == 0)
    def _():
        rows_in = [
            pltpu.make_async_copy(n_own, n_ref.at[:own, :], row_sems.at[0]),
            pltpu.make_async_copy(n_far, n_ref.at[own:, :], row_sems.at[1]),
        ]
        for copy in rows_in:
            copy.start()
        for split in range(parts[0].shape[1] // chunk):
            for k, (part, start, depth, which) in enumerate(moves):
                number = place_ref[1, k] * (parts[part].shape[1] // chunk) + split
                down = pl.ds(pl.multiple_of(place_ref[0, k] * depth, depth), depth)
                along = pl.ds(pl.multiple_of(number * chunk, chunk), chunk)
                pltpu.make_async_copy(
                    parts[part].at[pl.ds(start, depth), pl.ds(split * chunk, chunk)],
                    (w1_all, w2_all)[which].at[down, along],
                    sems.at[which, number],
                ).start()
        branch_ref[...] = jnp.zeros_like(branch_ref)
        gn_ref[...] = jnp.zeros_like(gn_ref)
        rank_ref[...] = jnp.zeros_like(rank_ref)
        gm_ref[...] = dot_nt(up_ref[...], gb_ref[...]).astype(BF16)
        for copy in rows_in:
            copy.wait()
        f_ref[...] = dot_nt(down_ref[...], n_ref[...]).astype(BF16)

    for which, target in enumerate((w1_all, w2_all)):
        area = target.at[:, at_chunk]
        pltpu.make_async_copy(area, area, sems.at[which, pl.program_id(0)]).wait()
    gf1_ref[...] = jnp.zeros_like(gf1_ref)
    gf2_ref[...] = jnp.zeros_like(gf2_ref)

    def step(i, carry):
        at = pl.ds(pl.multiple_of(i * block, block), block)
        w1 = w1_all[:, at_chunk]
        w2 = w2_all[:, at_chunk]
        u1 = u1_ref[...]
        d2 = d2_ref[...]
        z = dot(n_ref[at, :], w1) + dot_tn(f_ref[:, at], u1)
        cdf = 0.5 * (1.0 + lax.erf(z * (1.0 / math.sqrt(2.0))))
        a = (z * cdf).astype(BF16)
        slope = cdf + z * (jnp.exp2(z * z * (-0.5 * LOG2E)) * (1.0 / math.sqrt(2.0 * math.pi)))
        ga = dot(gb_ref[at, :], w2) + dot_tn(gm_ref[:, at], d2)
        gz = (ga * slope).astype(BF16)
        branch_ref[at, :] += dot_nt(a, w2)
        rank_ref[:rank, at] += dot_nt(d2, a)
        gn_ref[at, :] += dot_nt(gz, w1)
        rank_ref[rank:, at] += dot_nt(u1, gz)
        gf1_ref[...] += dot(f_ref[:, at], gz)
        gf2_ref[...] += dot(gm_ref[:, at], a)
        return carry

    lax.fori_loop(0, rows // block, step, 0)
    gf1_out[...] = gf1_ref[...].astype(BF16)
    gf2_out[...] = gf2_ref[...].astype(BF16)

    @pl.when(pl.program_id(0) == pl.num_programs(0) - 1)
    def _():
        rank_own[...] = rank_ref[:, :own]
        rank_far[...] = rank_ref[:, own:]
        branch_own[...] = branch_ref[:own, :]
        branch_far[...] = branch_ref[own:, :].astype(BF16)
        gn_own[...] = gn_ref[:own, :]
        gn_far[...] = gn_ref[own:, :]


def mlp(n_own, n_far, gb, down, up, parts, moves, place, u1, d2):
    own, model = n_own.shape
    rows = gb.shape[0]
    hidden = u1.shape[1]
    rank = down.shape[0]
    chunk = min(512, hidden)
    block = min(256, rows)
    whole = lambda shape: pl.BlockSpec(shape, lambda j, place: (0, 0))
    part = lambda depth: pl.BlockSpec((depth, chunk), lambda j, place: (0, j))
    far = rows - own
    shapes = [
        ((own, model), F32),
        ((far, model), BF16),
        ((own, model), F32),
        ((far, model), F32),
        ((2 * rank, own), F32),
        ((2 * rank, far), F32),
    ]
    return pl.pallas_call(
        functools.partial(mlp_kernel, block, own, moves, len(parts)),
        grid_spec=pltpu.PrefetchScalarGridSpec(
            num_scalar_prefetch=1,
            grid=(hidden // chunk,),
            in_specs=[
                whole((rows, model)),
                whole((rank, model)),
                whole((rank, model)),
                part(rank),
                part(rank),
            ]
            + [pl.BlockSpec(memory_space=pl.ANY)] * (2 + len(parts)),
            out_specs=[whole(shape) for shape, _ in shapes] + [part(rank), part(rank)],
            scratch_shapes=[
                pltpu.VMEM((model, hidden), BF16),
                pltpu.VMEM((model, hidden), BF16),
                pltpu.VMEM((rows, model), BF16),
                pltpu.VMEM((rank, rows), BF16),
                pltpu.VMEM((rank, rows), BF16),
                pltpu.VMEM((rows, model), F32),
                pltpu.VMEM((rows, model), F32),
                pltpu.VMEM((2 * rank, rows), F32),
                pltpu.VMEM((rank, chunk), F32),
                pltpu.VMEM((rank, chunk), F32),
                pltpu.SemaphoreType.DMA((2, hidden // chunk)),
                pltpu.SemaphoreType.DMA((2,)),
            ],
        ),
        out_shape=[jax.ShapeDtypeStruct(*shape) for shape in shapes]
        + [jax.ShapeDtypeStruct((rank, hidden), BF16)] * 2,
        cost_estimate=BRIEF,
        name="mlp",
    )(place, gb, down, up, u1, d2, n_own, n_far, *parts)


def project_kernel(moves, pieces, place_ref, n_ref, u_ref, lift_ref, *refs):
    parts, (w_in, w_out, qkv_ref, in_all, out_all, sems, back) = refs[:pieces], refs[pieces:]

    def copies():
        column = 0
        for j, target in enumerate((in_all, out_all)):
            width = target.shape[1] // 2
            for k, (part, start, depth) in enumerate(moves):
                down = pl.ds(pl.multiple_of(place_ref[0, k] * depth, depth), depth)
                along = pl.ds(pl.multiple_of(place_ref[1, k] * width, width), width)
                yield pltpu.make_async_copy(
                    parts[part].at[pl.ds(start, depth), pl.ds(column, width)],
                    target.at[down, along],
                    sems.at[j, k],
                )
            column += width

    backs = [
        pltpu.make_async_copy(in_all, w_in, back.at[0]),
        pltpu.make_async_copy(out_all, w_out, back.at[1]),
    ]

    @pl.when(pl.program_id(0) == 0)
    def _():
        pending = list(copies())
        for copy in pending:
            copy.start()
        for copy in pending:
            copy.wait()
        for copy in backs:
            copy.start()

    sums = dot(n_ref[...], in_all[...]) + dot_tn(u_ref[...], lift_ref[...])
    qkv_ref[...] = sums.astype(BF16)

    @pl.when(pl.program_id(0) == pl.num_programs(0) - 1)
    def _():
        for copy in backs:
            copy.wait()


def project(n, u, lift, parts, moves, place, width):
    rows, model = n.shape
    block = min(256, rows)
    anywhere = pl.BlockSpec(memory_space=pl.ANY)
    shapes = [(model, 6 * width), (model, 2 * width), (rows, 6 * width)]
    return pl.pallas_call(
        functools.partial(project_kernel, moves, len(parts)),
        grid_spec=pltpu.PrefetchScalarGridSpec(
            num_scalar_prefetch=1,
            grid=(rows // block,),
            in_specs=[
                pl.BlockSpec((block, model), lambda i, place: (i, 0)),
                pl.BlockSpec((u.shape[0], block), lambda i, place: (0, i)),
                pl.BlockSpec(lift.shape, lambda i, place: (0, 0)),
            ]
            + [anywhere] * len(parts),
            out_specs=[
                anywhere,
                anywhere,
                pl.BlockSpec((block, 6 * width), lambda i, place: (i, 0)),
            ],
            scratch_shapes=[
                pltpu.VMEM((model, 6 * width), BF16),
                pltpu.VMEM((model, 2 * width), BF16),
                pltpu.SemaphoreType.DMA((2, len(moves))),
                pltpu.SemaphoreType.DMA((2,)),
            ],
        ),
        out_shape=[jax.ShapeDtypeStruct(shape, BF16) for shape in shapes],
        cost_estimate=BRIEF,
        name="project",
    )(place, n, u, lift, *parts)


def pick_kernel(sides, _, *refs):
    sources, outs = refs[: 4 * sides], refs[4 * sides :]
    for far, out in enumerate(outs):
        up, fc1, proj, fc2 = sources[4 * far : 4 * far + 4]
        column = 0
        for piece in [up[0, 0], up[0, 1], up[0, 2], fc1[0], proj[0], fc2[0]]:
            out[:, column : column + piece.shape[1]] = piece
            column += piece.shape[1]


def pick(chosen, ups):
    rank = ups[1].shape[1]
    wide = sum(up.shape[-1] for up in ups) + 2 * ups[0].shape[-1]
    sides = chosen.shape[0]
    specs = [
        pl.BlockSpec(
            (1,) + up.shape[1:],
            lambda i, e, far=far, n=up.ndim: (e[far],) + (0,) * (n - 1),
        )
        for far in range(sides)
        for up in ups
    ]
    return pl.pallas_call(
        functools.partial(pick_kernel, sides),
        grid_spec=pltpu.PrefetchScalarGridSpec(
            num_scalar_prefetch=1,
            grid=(1,),
            in_specs=specs,
            out_specs=[pl.BlockSpec((rank, wide), lambda i, e: (0, 0))] * sides,
        ),
        out_shape=[jax.ShapeDtypeStruct((rank, wide), BF16)] * sides,
        name="pick",
    )(chosen, *(list(ups) * sides))


def lifts_kernel(sizes, *refs):
    packs, (qkv_ref, fc1_ref, proj_ref, fc2_ref) = refs[:-4], refs[-4:]
    rank = fc1_ref.shape[0]
    width, hidden = sizes
    qkv_ref[...] = jnp.zeros_like(qkv_ref)
    for far, pack in enumerate(packs):
        for j in range(3):
            column = (3 * far + j) * width
            qkv_ref[j * rank : (j + 1) * rank, column : column + width] = pack[
                :, j * width : (j + 1) * width
            ]
        start = 3 * width
        for ref, size in ((fc1_ref, hidden), (proj_ref, width), (fc2_ref, hidden)):
            ref[:, far * size : (far + 1) * size] = pack[:, start : start + size]
            start += size


def lifts(packs, width, hidden):
    rank = packs[0].shape[0]
    sides = len(packs)
    shapes = [(3 * rank, 3 * width), (rank, hidden), (rank, width), (rank, hidden)]
    return pl.pallas_call(
        functools.partial(lifts_kernel, (width, hidden)),
        out_shape=[jax.ShapeDtypeStruct((r, sides * c), BF16) for r, c in shapes],
        name="lifts",
    )(*packs)


def totals_kernel(blocks, widths, *refs):
    sources, outs = refs[:blocks], refs[blocks:]
    for out in outs:
        out[...] = jnp.zeros_like(out)
    total = sum(widths)
    for source in sources:
        for k in range(source.shape[0]):
            owner = jnp.max(source[k, :, total:].astype(F32)).astype(jnp.int32)
            column = 0
            for out, width in zip(outs, widths):
                split = out.shape[1] if len(out.shape) == 4 else 1
                for j in range(split):
                    part = source[k, :, column : column + width // split].astype(F32)
                    if split > 1:
                        out[owner, j] += part
                    else:
                        out[owner] += part
                    column += width // split


def totals(blocks, widths, adapters, split=1):
    rank = blocks[0].shape[1]
    return pl.pallas_call(
        functools.partial(totals_kernel, len(blocks), widths),
        out_shape=[
            jax.ShapeDtypeStruct(
                (adapters, split, rank, width // split)
                if split > 1 and k == 0
                else (adapters, rank, width),
                F32,
            )
            for k, width in enumerate(widths)
        ],
        name="totals",
    )(*blocks)


def spread_kernel(order, core_ref, *refs):
    halves, target = refs[:-1], refs[-1]
    cut = target.shape[3] // 2
    first = core_ref[0] == 0
    for j, (pair, k) in enumerate(order):
        own = halves[2 * pair][:, :, k * cut : (k + 1) * cut]
        other = halves[2 * pair + 1][:, :, k * cut : (k + 1) * cut]
        target[:, j, :, :cut] = jnp.where(first, own, other)
        target[:, j, :, cut:] = jnp.where(first, other, own)


def spread(core, halves, order, cut):
    adapters, rank, _ = halves[0].shape
    return pl.pallas_call(
        functools.partial(spread_kernel, order),
        in_specs=[pl.BlockSpec(memory_space=pltpu.SMEM)]
        + [pl.BlockSpec(memory_space=pltpu.VMEM)] * len(halves),
        out_shape=jax.ShapeDtypeStruct((adapters, len(order), rank, 2 * cut), F32),
        name="spread",
    )(jnp.reshape(core, (1,)), *halves)


def settle_kernel(count, where_ref, *refs):
    parts, out = refs[:count], refs[-1]
    for k, part in enumerate(parts):

        @pl.when(pl.program_id(0) == k)
        def _():
            out[0] = part[...].astype(out.dtype)


def settle(parts, where, first, stride, kind, images, base=None):
    rows, model = parts[0].shape
    extra = [] if base is None else [base]
    return pl.pallas_call(
        functools.partial(settle_kernel, len(parts)),
        grid_spec=pltpu.PrefetchScalarGridSpec(
            num_scalar_prefetch=1,
            grid=(len(parts),),
            in_specs=[pl.BlockSpec((rows, model), lambda k, where: (0, 0))] * len(parts)
            + [pl.BlockSpec(memory_space=pl.ANY)] * len(extra),
            out_specs=pl.BlockSpec((1, rows, model), lambda k, where: (where[first + stride * k], 0, 0)),
        ),
        out_shape=jax.ShapeDtypeStruct((images, rows, model), kind),
        input_output_aliases={1 + len(parts): 0} if extra else {},
        name="settle",
    )(where, *parts, *extra)


def normalize(values, gain, shift):
    centre = values - jnp.mean(values, axis=-1, keepdims=True)
    inverse = lax.rsqrt(jnp.mean(centre * centre, axis=-1, keepdims=True) + EPS)
    unit = centre * inverse
    return unit * gain + shift, unit, inverse


def norm_back(grad, unit, inverse, gain):
    scaled = grad * gain
    centred = scaled - jnp.mean(scaled, axis=-1, keepdims=True)
    return inverse * (centred - unit * jnp.mean(scaled * unit, axis=-1, keepdims=True))


def per_device(
    sizes,
    tokens,
    cotangent,
    adapter_index,
    ln1_gain,
    ln1_bias,
    ln2_gain,
    ln2_bias,
    layer_scale,
    w_qkv,
    w_proj,
    w_fc1,
    w_fc2,
    down_in,
    qkv_up,
    fc1_up,
    proj_down,
    fc2_down,
    out_up,
):
    shards, contexts, tensors = sizes
    half = contexts // 2
    sides = tensors // 2
    images, rows, model = tokens.shape
    rank = down_in.shape[-1]
    depth = w_fc1.shape[0]
    width = w_proj.shape[1]
    hidden = w_fc1.shape[1]
    pairs = width // PAIR
    adapters = down_in.shape[0]
    shard = lax.axis_index("shard")
    context = lax.axis_index("context")
    tensor = lax.axis_index("tensor")
    side, core = tensor // 2, tensor % 2
    high = context // half

    ring = {
        "shard": [(i, (i + 1) % shards) for i in range(shards)],
        "context": [(i, (i + 1) % contexts) for i in range(contexts)],
        "tensor": [(i, (i + 2) % tensors) for i in range(tensors)],
    }
    count = {"shard": shards, "context": contexts, "tensor": sides}
    twin = [(i, i ^ 1) for i in range(tensors)]
    plane = ("context", "tensor")

    def hop(value, axis):
        return lax.ppermute(value, axis, ring[axis])

    def swap(value):
        return lax.ppermute(value, "tensor", twin)

    def around(value, axis):
        out = [value]
        for _ in range(count[axis] - 1):
            out.append(hop(out[-1], axis))
        return out

    def fence(*values):
        return lax.optimization_barrier(values)

    to_owner = []
    to_home = {far: [] for far in range(sides)}
    for c in range(contexts):
        for s in range(sides):
            for k in range(2):
                here = c * tensors + 2 * s + k
                source = 2 * (c % half) + k
                to_owner.append((source * tensors + 2 * s + c // half, here))
                for far in range(sides):
                    there = (s + far) % sides
                    to_home[far].append((here, source * tensors + 2 * there + c // half))

    ringed = contexts == 2 and sides == 2 and shards == 4
    cross = {0: [], 1: []}
    if ringed:
        for c in range(2):
            for s in range(2):
                for k in range(2):
                    here = c * tensors + 2 * s + k
                    along = c * tensors + 2 * (1 - s) + k
                    aside = (1 - c) * tensors + 2 * s + k
                    cross[0].append((here, along if k == 0 else aside))
                    cross[1].append((here, aside if k == 0 else along))

    def block_of(array, index):
        return lax.dynamic_index_in_dim(array, index, 0, keepdims=False)

    def deliver(value, pairs):
        stay = np.zeros(contexts * tensors, np.int32)
        for a, b in pairs:
            stay[a] = a == b
        got = lax.ppermute(value, plane, [(a, b) for a, b in pairs if a != b])
        if not stay.any():
            return got
        return jnp.where(jnp.asarray(stay)[context * tensors + tensor] == 1, value, got)

    def stays(value, other):
        return jnp.where(core == context, value, other)

    relay = [[], []]
    for c in range(2 if ringed else 0):
        for s in range(2):
            for k in range(2):
                here = c * tensors + 2 * s + k
                along = c * tensors + 2 * (1 - s) + k
                relay[0].append((here, along if k == c else (1 - c) * tensors + 2 * s + 1 - k))
                if k != c:
                    relay[1].append((here, along))

    def send_first(value):
        if ringed:
            return [lax.ppermute(value, plane, relay[0])]
        return [deliver(value, to_home[far]) for far in range(sides)]

    def send_second(value, got):
        if ringed:
            return [got[0], stays(value, lax.ppermute(got[0], plane, relay[1]))]
        return got

    def pair_up(a, b):
        return jnp.concatenate([a, b], axis=0)

    def adapter_of(index, far):
        return block_of(index, 2 * ((side + far) % sides) + high)

    def up_packs(index, ups):
        chosen = jnp.stack([adapter_of(index, far) for far in range(sides)])
        packs = list(pick(chosen, ups))
        for far in range(1, sides):
            send = [(i, (i + 2 * far) % tensors) for i in range(tensors)]
            packs[far] = lax.ppermute(packs[far], "tensor", send)
        return packs

    attn_own = jnp.concatenate([w_qkv[:, j] for j in range(3)] + [w_proj], axis=1)
    ups = (qkv_up, fc1_up, jnp.transpose(proj_down, (0, 2, 1)), jnp.transpose(fc2_down, (0, 2, 1)))
    flows = {}

    def cross_to(value, turn):
        return lax.ppermute(value, plane, cross[turn])

    if ringed:
        z, b, c, d = [attn_own], [], [], []
        ff_own = pair_up(w_fc1, w_fc2)
        got = fence(
            hop(attn_own, "shard"),
            cross_to(attn_own, 0),
            cross_to(attn_own, 1),
            deliver(block_of(tokens, tensor), to_owner),
            hop(ff_own, "shard"),
            ff_own,
            cotangent,
            adapter_index,
            down_in,
            out_up,
            *ups,
        )
        z.append(got[0])
        b.append(got[1])
        c.append(got[2])
        x_own = got[3]
        own = [got[5], got[4]]
        cotangent, adapter_index, down_in, out_up = got[6:10]
        ups = got[10:]
        got = fence(
            hop(z[1], "shard"),
            cross_to(z[1], 0),
            cross_to(z[1], 1),
            cross_to(b[0], 1),
            cross_to(own[0], 0),
            x_own,
            own[1],
            adapter_index,
            *ups,
        )
        z.append(got[0])
        b.append(got[1])
        c.append(got[2])
        d.append(got[3])
        aside = [got[4]]
        x_own, own[1], adapter_index = got[5:8]
        ups = got[8:]
        got = fence(
            hop(z[2], "shard"),
            cross_to(z[2], 0),
            cross_to(z[2], 1),
            cross_to(b[1], 1),
            swap(x_own),
            x_own,
            own[1],
            aside[0],
        )
        z.append(got[0])
        b.append(got[1])
        c.append(got[2])
        d.append(got[3])
        x_other, x_own, own[1], aside[0] = got[4:]
        packs = up_packs(adapter_index, ups)
        own.append(hop(own[1], "shard"))
        got = fence(cross_to(z[3], 0), cross_to(z[3], 1), cross_to(b[2], 1), cotangent, packs[1])
        b.append(got[0])
        c.append(got[1])
        d.append(got[2])
        cotangent, packs[1] = got[3:]
        last = cross_to(b[3], 1)
        own_over, aside_over = [], []

        step_of = np.repeat(np.arange(shards), 4)
        near_0 = np.tile([0, 0, 1, 1], shards)
        far_0 = np.tile([0, 1, 0, 1], shards)
        near = jnp.where(core == 0, near_0, far_0)
        across = jnp.where(core == 0, far_0, near_0)
        row = (shard - step_of) % shards * contexts + (context - near) % contexts
        attn_place = jnp.stack([row, across]).astype(jnp.int32)
        attn_moves = [(k, 0, depth) for k in range(4 * shards)]
        ff_moves = [(k, which * depth, depth, which) for which in range(2) for k in range(4 * shards)]
        ff_place = jnp.concatenate([attn_place, attn_place], axis=1)

        def start(*values):
            got = fence(*values, last, own[0], aside[0], own[2])
            d.append(got[-4])
            own[0], aside[0], own[2] = got[-3:]
            aside.append(hop(aside[0], "shard"))
            own_over.append(cross_to(own[0], 1))
            aside_over.append(cross_to(aside[0], 1))
            return got[:-4]

        def advance(stage, *values):
            count = len(values)
            if stage == 0:
                got = fence(*values, own[2], aside[1], own_over[0], aside_over[0], cotangent)
                own[2], aside[1], own_over[0], aside_over[0], late_cotangent = got[count:]
                own.append(hop(own[2], "shard"))
                own_over.append(cross_to(own[1], 1))
                flows["gy"] = deliver(block_of(late_cotangent, tensor), to_owner)
            elif stage == 1:
                got = fence(*values, own[3], own[2], aside[1])
                own[3], own[2], aside[1] = got[count:]
                aside.append(hop(aside[1], "shard"))
                aside_over.append(cross_to(aside[1], 1))
                own_over.append(cross_to(own[2], 1))
            elif stage == 2:
                got = fence(
                    *values, aside[2], own_over[1], own_over[2], aside_over[1], own[3], flows["gy"]
                )
                aside[2], own_over[1], own_over[2], aside_over[1], own[3], flows["gy"] = got[count:]
                aside.append(hop(aside[2], "shard"))
                own_over.append(cross_to(own[3], 1))
                aside_over.append(cross_to(aside[2], 1))
            else:
                got = fence(*values, aside[3], own_over[3], aside_over[2])
                aside[3], own_over[3], aside_over[2] = got[count:]
                aside_over.append(cross_to(aside[3], 1))
            return got[:count]

    else:

        def gather_plain(value):
            whole = lax.all_gather(value, ("shard", "context"), axis=0, tiled=True)
            return around(whole, "tensor")

        attn_parts = gather_plain(attn_own)
        fc1_parts = gather_plain(w_fc1)
        fc2_parts = gather_plain(w_fc2)
        packs = up_packs(adapter_index, ups)
        x_own = deliver(block_of(tokens, tensor), to_owner)
        x_other = swap(x_own)
        flows["gy"] = deliver(block_of(cotangent, tensor), to_owner)
        attn_moves = [(k, 0, model) for k in range(sides)]
        attn_place = jnp.asarray([[0] * sides, list(range(sides))], jnp.int32)
        ff_moves = [(k, 0, model, k // sides) for k in range(2 * sides)]
        ff_place = jnp.concatenate([attn_place, attn_place], axis=1)

        def start(*values):
            return values

        def advance(stage, *values):
            return values

    mine = adapter_of(adapter_index, 0)
    down = block_of(down_in, mine)
    down_t = jnp.transpose(down, (0, 2, 1)).reshape(4 * rank, model)
    out_t = block_of(out_up, mine)

    x_all = pair_up(x_own, x_other).astype(F32)
    normed, unit_one, inverse_one = normalize(x_all, ln1_gain, ln1_bias)
    n1 = normed.astype(BF16)
    u = dot_nt(down_t[: 3 * rank], n1).astype(BF16)
    qkv_lift, fc1_lift, proj_t, fc2_t = lifts(packs, width, hidden)
    n1, u, qkv_lift = start(n1, u, qkv_lift)
    if ringed:
        attn_parts = [part for i in range(shards) for part in (z[i], b[i], c[i], d[i])]
    w_in, w_out, qkv = project(n1, u, qkv_lift, attn_parts, attn_moves, attn_place, width)
    (qkv,) = advance(0, qkv)

    steps = [[h * half + i for i in range(half)] for h in range(2)]
    per_side = width // PAIR
    pairs = per_side * sides
    near, group_count = (per_side, sides) if half == 1 else (1, pairs // half)

    def to_heads(array, thirds_each):
        if half == 1:
            return array
        cells = array.reshape(array.shape[0], sides, thirds_each, per_side, PAIR)
        cells = jnp.transpose(cells, (0, 1, 3, 2, 4)).reshape(array.shape[0], pairs, -1)
        moved = lax.all_to_all(cells, "context", 1, 0, axis_index_groups=steps, tiled=True)
        return moved.reshape(moved.shape[0], -1)

    def to_rows(array, thirds_each):
        if half == 1:
            return array
        cells = array.reshape(array.shape[0], pairs // half, -1)
        moved = lax.all_to_all(cells, "context", 0, 1, axis_index_groups=steps, tiled=True)
        moved = moved.reshape(moved.shape[0], sides, per_side, thirds_each, PAIR)
        return jnp.transpose(moved, (0, 1, 3, 2, 4)).reshape(moved.shape[0], -1)

    qkv_heads = to_heads(qkv, 3)
    o_heads = None
    logs = []
    for group in range(group_count):
        o_heads, lse = attend(qkv_heads, group, near, o_heads)
        logs.append(lse)
        if group == 0:
            o_heads, qkv_heads = advance(1, o_heads, qkv_heads)
    (o_heads,) = advance(2, o_heads)
    gy_own = flows["gy"]
    o = to_rows(o_heads, 1)
    attn_far = dot_nt(o[rows:], w_out)
    c_part = dot_nt(proj_t, o)
    attn_sum = swap(attn_far) + dot_nt(o[:rows], w_out)
    c_own = (c_part[:, :rows] + swap(c_part[:, rows:])).astype(BF16)
    h = x_all[:rows] + layer_scale[0] * (attn_sum + dot_tn(c_own, out_t[0]))
    normed, unit_two, inverse_two = normalize(h, ln2_gain, ln2_bias)
    n2_own = normed.astype(BF16)
    gb_own = (gy_own.astype(F32) * layer_scale[1]).astype(BF16)
    gb = pair_up(gb_own, swap(gb_own))
    n2_own, gb = advance(3, n2_own, gb)
    n2_far = swap(n2_own)
    if ringed:
        ff_parts = [
            part
            for i in range(shards)
            for part in (own[i], aside[i], own_over[i], aside_over[i])
        ]
    else:
        ff_parts = fc1_parts + fc2_parts
    branch_own, branch_far, gn2_own, gn2_far, rank_own, rank_far, g_fc1, g_fc2 = mlp(
        n2_own, n2_far, gb, down_t[3 * rank :], out_t[1], ff_parts, ff_moves, ff_place, fc1_lift, fc2_t
    )
    ranks = (rank_own + swap(rank_far)).astype(BF16)
    m_own, gf_own = ranks[:rank], ranks[rank:]
    branch = branch_own + swap(branch_far).astype(F32) + dot_tn(m_own, out_t[1])
    result_own = (h + layer_scale[1] * branch).astype(BF16)
    gn2 = gn2_own + swap(gn2_far) + dot_tn(gf_own, down_t[3 * rank :])
    g_out1 = dot(m_own, gb[:rows])
    g_down3 = dot(gf_own, n2_own)

    cut = model // 2
    one = jnp.where(context % half == 0, mine, 0)
    mark = jnp.full((rank, 128), one).astype(BF16)

    def halves(shared):
        shared = jnp.stack(shared)
        away = lax.dynamic_slice_in_dim(shared, (1 - core) * cut, cut, 2)
        keep = lax.dynamic_slice_in_dim(shared, core * cut, cut, 2)
        both = keep + swap(away)
        return [both[j] for j in range(len(both))]

    def to_sides(slices, shared):
        packed = []
        for far in range(sides):
            pack = jnp.concatenate([part.astype(BF16) for part in slices[far] + shared] + [mark], axis=1)
            if far:
                send = [(i, (i - 2 * far) % tensors) for i in range(tensors)]
                pack = lax.ppermute(pack, "tensor", send)
            packed.append(pack)
        return jnp.stack(packed)

    def to_contexts(block):
        if half > 1:
            total = lax.psum(block.astype(F32), "context", axis_index_groups=steps)
            block = total.astype(BF16)
            opposite = [(i, (i + half) % contexts) for i in range(contexts)]
        else:
            opposite = ring["context"]
        return pair_up(block, lax.ppermute(block, "context", opposite))

    def columns(array, far, size):
        return array[:, far * size : (far + 1) * size]

    early = to_sides(
        [[columns(g_fc1, far, hidden), columns(g_fc2, far, hidden)] for far in range(sides)],
        halves([g_down3, g_out1]),
    )
    gh = gy_own.astype(F32) + norm_back(gn2, unit_two, inverse_two, ln2_gain)
    gattn_own = (layer_scale[0] * gh).astype(BF16)
    gattn_own, early = fence(gattn_own, early)
    gattn = pair_up(gattn_own, swap(gattn_own))
    early = to_contexts(early)
    g_out0 = dot(c_own, gattn_own)
    gc = dot_nt(out_t[0], gattn).astype(BF16)
    g_proj = dot(gc, o)
    mid = to_sides([[columns(g_proj, far, width)] for far in range(sides)], halves([g_out0]))
    go = (dot(gattn, w_out) + dot_tn(gc, proj_t)).astype(BF16)
    early_line = [early, hop(early, "shard")]
    early_line[1], early_line[0], mid, go = fence(early_line[1], early, mid, go)
    early_line.append(hop(early_line[-1], "shard"))
    mid = to_contexts(mid)
    go_heads = to_heads(go, 1)
    g_heads = None
    for group in range(group_count):
        g_heads = attend_back(qkv_heads, go_heads, o_heads, logs[group], group, near, g_heads)
        if group == 0:
            g_heads, early_line[-1], mid, result_own = fence(
                g_heads, early_line[-1], mid, result_own
            )
            for _ in range(3, shards):
                early_line.append(hop(early_line[-1], "shard"))
            mid_line = [mid, hop(mid, "shard")]
            sent = send_first(result_own)
    g_heads, mid_line[-1], early_line[-1], *sent = fence(
        g_heads, mid_line[-1], early_line[-1], *sent
    )
    mid_line.append(hop(mid_line[-1], "shard"))
    sent = send_second(result_own, sent)
    g = to_rows(g_heads, 3)

    gu_part = dot_nt(qkv_lift, g)
    gu_own = (gu_part[:, :rows] + swap(gu_part[:, rows:])).astype(BF16)
    gn1_far = swap(dot_nt(g[rows:], w_in))
    g_up = dot(u, g)
    gn1 = dot_nt(g[:rows], w_in) + gn1_far + dot_tn(gu_own, down_t[: 3 * rank])
    g_down = dot(gu_own, n1[:rows])
    late_slices = [
        [
            g_up[j * rank : (j + 1) * rank, (far * 3 + j) * width : (far * 3 + j + 1) * width]
            for j in range(3)
        ]
        for far in range(sides)
    ]
    late = to_sides(late_slices, halves([g_down[j * rank : (j + 1) * rank] for j in range(3)]))
    input_own = gh + norm_back(gn1, unit_one[:rows], inverse_one[:rows], ln1_gain)
    input_own = input_own.astype(BF16)
    late = to_contexts(late)
    late, input_own, mid_line[-1], *sent = fence(late, input_own, mid_line[-1], *sent)

    order = np.tile(np.arange(sides), 2)
    flip = np.repeat([0, 1], sides)
    far = jnp.where((core ^ flip) == context, 1 - order, order) if ringed else order
    where = (2 * ((side - far) % sides) + (core ^ flip)).astype(jnp.int32)
    late_line = [late, hop(late, "shard")]
    input_sent = send_first(input_own)
    for _ in range(3, shards):
        mid_line.append(hop(mid_line[-1], "shard"))
    sent += [swap(part) for part in sent]
    fc1_grad, fc2_grad, early_half = totals(early_line, (hidden, hidden, 2 * cut), adapters)
    late_line[1], early_half, mid_line[-1], *got = fence(
        late_line[1], early_half, mid_line[-1], *sent, *input_sent
    )
    sent, input_sent = got[: 2 * sides], got[2 * sides :]
    for _ in range(2, shards - 1):
        late_line.append(hop(late_line[-1], "shard"))
    first_twin = swap(input_sent[0])
    input_sent = send_second(input_own, input_sent)
    early_twin = swap(early_half)
    proj_grad, mid_half = totals(mid_line, (width, cut), adapters)
    result = settle(sent, where, 0, 1, BF16, images)
    late_line[-1], early_half, early_twin, proj_grad, mid_half, result, first_twin, *input_sent = fence(
        late_line[-1], early_half, early_twin, proj_grad, mid_half, result, first_twin, *input_sent
    )
    if shards > 2:
        late_line.append(hop(late_line[-1], "shard"))
    mid_twin = swap(mid_half)
    input_grad = settle(
        [input_sent[0], first_twin],
        where,
        0,
        sides,
        F32,
        images,
    )
    out_grad = spread(
        core, [mid_half, mid_twin, early_half, early_twin], ((0, 0), (1, 1)), cut
    )
    last_sent = list(input_sent[1:])
    last_twins = [swap(part) for part in last_sent]
    late_line[-1], input_grad, out_grad, *last_twins = fence(
        late_line[-1], input_grad, out_grad, *last_twins
    )
    qkv_grad, late_half = totals(late_line, (3 * width, 3 * cut), adapters, 3)
    late_twin = swap(late_half)
    input_grad = settle(
        last_sent + last_twins,
        where,
        1,
        sides,
        F32,
        images,
        input_grad,
    )
    down_grad = spread(
        core,
        [late_half, late_twin, early_half, early_twin],
        ((0, 0), (0, 1), (0, 2), (1, 0)),
        cut,
    )
    return (
        result,
        input_grad,
        jnp.transpose(down_grad, (0, 1, 3, 2)),
        qkv_grad,
        fc1_grad,
        jnp.transpose(proj_grad, (0, 2, 1)),
        jnp.transpose(fc2_grad, (0, 2, 1)),
        out_grad,
    )


def solution(mesh):
    sizes = (mesh.shape["shard"], mesh.shape["context"], mesh.shape["tensor"])
    placed = (
        P("shard", "context", None),
        P("shard", "context", None),
        P("shard"),
        P(),
        P(),
        P(),
        P(),
        P(),
        P(("shard", "context"), None, "tensor"),
        P(("shard", "context"), "tensor"),
        P(("shard", "context"), "tensor"),
        P(("shard", "context"), "tensor"),
        P(),
        P(None, None, None, "tensor"),
        P(None, None, "tensor"),
        P(None, "tensor", None),
        P(None, "tensor", None),
        P(),
    )
    return jax.shard_map(
        functools.partial(per_device, sizes),
        mesh=mesh,
        in_specs=placed,
        out_specs=(
            P("shard", "context", None),
            P("shard", "context", None),
            P(),
            P(None, None, None, "tensor"),
            P(None, None, "tensor"),
            P(None, "tensor", None),
            P(None, "tensor", None),
            P(),
        ),
        check_vma=False,
    )
```

```python
import functools
import math

import jax
import jax.numpy as jnp
import numpy as np
from jax import lax
from jax.experimental import pallas as pl
from jax.experimental.pallas import tpu as pltpu
from jax.sharding import PartitionSpec as P

HEAD_DIM = 64
PAIR = 2 * HEAD_DIM
EPS = 1e-06
LOG2E = math.log2(math.e)
SCORE = 1.0 / math.sqrt(HEAD_DIM)
F32 = jnp.float32
BF16 = jnp.bfloat16
NT = (((1,), (1,)), ((), ()))
TN = (((0,), (0,)), ((), ()))
BRIEF = pl.CostEstimate(flops=1000, bytes_accessed=1000, transcendentals=0)


def dot(a, b):
    return jnp.dot(a, b, preferred_element_type=F32)


def dot_nt(a, b):
    return lax.dot_general(a, b, NT, preferred_element_type=F32)


def dot_tn(a, b):
    return lax.dot_general(a, b, TN, preferred_element_type=F32)


def head_masks(rows):
    lane = lax.broadcasted_iota(jnp.int32, (rows, PAIR), 1)
    return lane < HEAD_DIM


def attend_kernel(block, q_ref, k_ref, v_ref, _, o_ref, lse_ref):
    rows = q_ref.shape[0]
    keys = k_ref[...]
    values = jnp.concatenate([v_ref[...], jnp.ones((rows, PAIR), BF16)], axis=1)
    first = head_masks(block)

    def step(i, carry):
        at = pl.ds(pl.multiple_of(i * block, block), block)
        q = q_ref[at, :]
        outs = []
        logs = []
        for head in range(2):
            mine = first if head == 0 else jnp.logical_not(first)
            s = dot_nt(jnp.where(mine, q, jnp.zeros_like(q)), keys)
            peak = jnp.max(s, axis=1, keepdims=True)
            e = jnp.exp2((s - peak) * (SCORE * LOG2E))
            acc = dot(e.astype(BF16), values)
            total = acc[:, PAIR:]
            outs.append(acc[:, :PAIR] / total)
            logs.append(peak * (SCORE * LOG2E) + jnp.log2(total))
        o_ref[at, :] = jnp.where(first, outs[0], outs[1]).astype(BF16)
        lane = lax.broadcasted_iota(jnp.int32, (block, PAIR), 1)
        both = jnp.where(lane == 0, logs[0], logs[1])
        lse_ref[0, :, at] = jnp.transpose(both)[:8]
        return carry

    lax.fori_loop(0, rows // block, step, 0)


def thirds(rows, group, near):
    return [
        pl.BlockSpec((rows, PAIR), lambda p, j=j: (0, (group * 3 + j) * near + p))
        for j in range(3)
    ]


def attend(qkv, group, near, o):
    rows, width = qkv.shape
    pairs = width // (3 * PAIR)
    block = min(256, rows)
    anywhere = pl.BlockSpec(memory_space=pl.ANY)
    operands = [qkv, qkv, qkv, qkv if o is None else o]
    return pl.pallas_call(
        functools.partial(attend_kernel, block),
        grid=(near,),
        in_specs=thirds(rows, group, near) + [anywhere],
        out_specs=[
            pl.BlockSpec((rows, PAIR), lambda p: (0, group * near + p)),
            pl.BlockSpec((1, 8, rows), lambda p: (p, 0, 0)),
        ],
        out_shape=[
            jax.ShapeDtypeStruct((rows, pairs * PAIR), BF16),
            jax.ShapeDtypeStruct((near, 8, rows), F32),
        ],
        input_output_aliases={} if o is None else {3: 0},
        cost_estimate=BRIEF,
        name="attend",
    )(*operands)


def attend_back_kernel(
    block, near, q_ref, k_ref, v_ref, go_ref, o_ref, lse_ref, _, g_ref, gq_ref, d_ref
):
    rows = q_ref.shape[0]
    pair = pl.program_id(0)
    lanes = [pl.ds(pl.multiple_of((j * near + pair) * PAIR, PAIR), PAIR) for j in range(3)]
    first = head_masks(block)
    prod = o_ref[...].astype(F32) * go_ref[...].astype(F32)
    lane8 = lax.broadcasted_iota(jnp.int32, (8, PAIR), 1) // HEAD_DIM
    row8 = lax.broadcasted_iota(jnp.int32, (8, PAIR), 0)
    d_ref[...] = lax.dot_general(
        (lane8 == row8).astype(F32),
        prod,
        NT,
        preferred_element_type=F32,
        precision=lax.Precision.HIGHEST,
    )
    gq_ref[...] = jnp.zeros_like(gq_ref)

    def step(i, carry):
        at = pl.ds(pl.multiple_of(i * block, block), block)
        k = k_ref[at, :]
        v = v_ref[at, :]
        q = q_ref[...]
        go = go_ref[...]
        gks = []
        gvs = []
        gq = None
        for head in range(2):
            mine = first if head == 0 else jnp.logical_not(first)
            k_own = jnp.where(mine, k, jnp.zeros_like(k))
            v_own = jnp.where(mine, v, jnp.zeros_like(v))
            s = dot_nt(k_own, q)
            gp = dot_nt(v_own, go)
            p = jnp.exp2(s * (SCORE * LOG2E) - lse_ref[0, head : head + 1, :])
            gs = (p * (gp - d_ref[head : head + 1, :])).astype(BF16)
            gks.append(dot(gs, q))
            gvs.append(dot(p.astype(BF16), go))
            part = dot(jnp.transpose(k_own), gs)
            gq = part if gq is None else gq + part
        gq_ref[...] += gq
        g_ref[at, lanes[1]] = (jnp.where(first, gks[0], gks[1]) * SCORE).astype(BF16)
        g_ref[at, lanes[2]] = jnp.where(first, gvs[0], gvs[1]).astype(BF16)
        return carry

    lax.fori_loop(0, rows // block, step, 0)
    g_ref[:, lanes[0]] = (jnp.transpose(gq_ref[...]) * SCORE).astype(BF16)


def attend_back(qkv, go, o, lse, group, near, g):
    rows, width = qkv.shape
    block = min(256, rows)
    mine = pl.BlockSpec((rows, PAIR), lambda p: (0, group * near + p))
    anywhere = pl.BlockSpec(memory_space=pl.ANY)
    operands = [qkv, qkv, qkv, go, o, lse, qkv if g is None else g]
    return pl.pallas_call(
        functools.partial(attend_back_kernel, block, near),
        grid=(near,),
        in_specs=thirds(rows, group, near)
        + [mine, mine, pl.BlockSpec((1, 8, rows), lambda p: (p, 0, 0)), anywhere],
        out_specs=pl.BlockSpec((rows, 3 * near * PAIR), lambda p: (0, group)),
        out_shape=jax.ShapeDtypeStruct((rows, width), BF16),
        scratch_shapes=[pltpu.VMEM((PAIR, rows), F32), pltpu.VMEM((8, rows), F32)],
        input_output_aliases={} if g is None else {6: 0},
        cost_estimate=BRIEF,
        name="attend_back",
    )(*operands)


def mlp_kernel(
    block,
    own,
    moves,
    pieces,
    place_ref,
    gb_ref,
    down_ref,
    up_ref,
    u1_ref,
    d2_ref,
    n_own,
    n_far,
    *refs,
):
    parts = refs[:pieces]
    outs, scratch = refs[pieces : pieces + 8], refs[pieces + 8 :]
    branch_own, branch_far, gn_own, gn_far = outs[:4]
    rank_own, rank_far, gf1_out, gf2_out = outs[4:]
    w1_all, w2_all, n_ref, f_ref, gm_ref, branch_ref, gn_ref = scratch[:7]
    rank_ref, gf1_ref, gf2_ref, cast_ref, sems, row_sems, out_sems = scratch[7:]
    rank = f_ref.shape[0]
    rows = n_ref.shape[0]
    chunk = u1_ref.shape[1]
    at_chunk = pl.ds(pl.multiple_of(pl.program_id(0) * chunk, chunk), chunk)

    @pl.when(pl.program_id(0) == 0)
    def _():
        rows_in = [
            pltpu.make_async_copy(n_own, n_ref.at[:own, :], row_sems.at[0]),
            pltpu.make_async_copy(n_far, n_ref.at[own:, :], row_sems.at[1]),
        ]
        for copy in rows_in:
            copy.start()
        for split in range(parts[0].shape[1] // chunk):
            for k, (part, start, depth, which) in enumerate(moves):
                number = place_ref[1, k] * (parts[part].shape[1] // chunk) + split
                down = pl.ds(pl.multiple_of(place_ref[0, k] * depth, depth), depth)
                along = pl.ds(pl.multiple_of(number * chunk, chunk), chunk)
                pltpu.make_async_copy(
                    parts[part].at[pl.ds(start, depth), pl.ds(split * chunk, chunk)],
                    (w1_all, w2_all)[which].at[down, along],
                    sems.at[which, number],
                ).start()
        branch_ref[...] = jnp.zeros_like(branch_ref)
        gn_ref[...] = jnp.zeros_like(gn_ref)
        rank_ref[...] = jnp.zeros_like(rank_ref)
        gm_ref[...] = dot_nt(up_ref[...], gb_ref[...]).astype(BF16)
        for copy in rows_in:
            copy.wait()
        f_ref[...] = dot_nt(down_ref[...], n_ref[...]).astype(BF16)

    final = pl.program_id(0) == pl.num_programs(0) - 1

    def leave(i, at, to, home):
        branch = branch_ref.at[at, :] if home else cast_ref.at[to, :]
        target = branch_own if home else branch_far
        gn_target = gn_own if home else gn_far
        return [
            pltpu.make_async_copy(branch, target.at[to, :], out_sems.at[0, i]),
            pltpu.make_async_copy(gn_ref.at[at, :], gn_target.at[to, :], out_sems.at[1, i]),
        ]

    for which, target in enumerate((w1_all, w2_all)):
        area = target.at[:, at_chunk]
        pltpu.make_async_copy(area, area, sems.at[which, pl.program_id(0)]).wait()
    gf1_ref[...] = jnp.zeros_like(gf1_ref)
    gf2_ref[...] = jnp.zeros_like(gf2_ref)

    def step(i, carry):
        at = pl.ds(pl.multiple_of(i * block, block), block)
        w1 = w1_all[:, at_chunk]
        w2 = w2_all[:, at_chunk]
        u1 = u1_ref[...]
        d2 = d2_ref[...]
        z = dot(n_ref[at, :], w1) + dot_tn(f_ref[:, at], u1)
        cdf = 0.5 * (1.0 + lax.erf(z * (1.0 / math.sqrt(2.0))))
        a = (z * cdf).astype(BF16)
        slope = cdf + z * (jnp.exp2(z * z * (-0.5 * LOG2E)) * (1.0 / math.sqrt(2.0 * math.pi)))
        ga = dot(gb_ref[at, :], w2) + dot_tn(gm_ref[:, at], d2)
        gz = (ga * slope).astype(BF16)
        branch_ref[at, :] += dot_nt(a, w2)
        rank_ref[:rank, at] += dot_nt(d2, a)
        gn_ref[at, :] += dot_nt(gz, w1)
        rank_ref[rank:, at] += dot_nt(u1, gz)
        gf1_ref[...] += dot(f_ref[:, at], gz)
        gf2_ref[...] += dot(gm_ref[:, at], a)

        @pl.when(jnp.logical_and(final, i < own // block))
        def _():
            for copy in leave(i, at, at, True):
                copy.start()

        @pl.when(jnp.logical_and(final, i >= own // block))
        def _():
            to = pl.ds(pl.multiple_of(i * block - own, block), block)
            cast_ref[to, :] = branch_ref[at, :].astype(BF16)
            for copy in leave(i, at, to, False):
                copy.start()

        return carry

    lax.fori_loop(0, rows // block, step, 0)
    gf1_out[...] = gf1_ref[...].astype(BF16)
    gf2_out[...] = gf2_ref[...].astype(BF16)

    @pl.when(pl.program_id(0) == pl.num_programs(0) - 1)
    def _():
        rank_own[...] = rank_ref[:, :own]
        rank_far[...] = rank_ref[:, own:]
        for i in range(rows // block):
            home = i < own // block
            at = pl.ds(i * block, block)
            to = at if home else pl.ds(i * block - own, block)
            for copy in leave(i, at, to, home):
                copy.wait()


def mlp(n_own, n_far, gb, down, up, parts, moves, place, u1, d2):
    own, model = n_own.shape
    rows = gb.shape[0]
    hidden = u1.shape[1]
    rank = down.shape[0]
    chunk = min(512, hidden)
    block = min(256, own)
    whole = lambda shape: pl.BlockSpec(shape, lambda j, place: (0, 0))
    part = lambda depth: pl.BlockSpec((depth, chunk), lambda j, place: (0, j))
    far = rows - own
    shapes = [
        ((own, model), F32),
        ((far, model), BF16),
        ((own, model), F32),
        ((far, model), F32),
        ((2 * rank, own), F32),
        ((2 * rank, far), F32),
    ]
    return pl.pallas_call(
        functools.partial(mlp_kernel, block, own, moves, len(parts)),
        grid_spec=pltpu.PrefetchScalarGridSpec(
            num_scalar_prefetch=1,
            grid=(hidden // chunk,),
            in_specs=[
                whole((rows, model)),
                whole((rank, model)),
                whole((rank, model)),
                part(rank),
                part(rank),
            ]
            + [pl.BlockSpec(memory_space=pl.ANY)] * (2 + len(parts)),
            out_specs=[pl.BlockSpec(memory_space=pl.ANY)] * 4
            + [whole(shape) for shape, _ in shapes[4:]]
            + [part(rank), part(rank)],
            scratch_shapes=[
                pltpu.VMEM((model, hidden), BF16),
                pltpu.VMEM((model, hidden), BF16),
                pltpu.VMEM((rows, model), BF16),
                pltpu.VMEM((rank, rows), BF16),
                pltpu.VMEM((rank, rows), BF16),
                pltpu.VMEM((rows, model), F32),
                pltpu.VMEM((rows, model), F32),
                pltpu.VMEM((2 * rank, rows), F32),
                pltpu.VMEM((rank, chunk), F32),
                pltpu.VMEM((rank, chunk), F32),
                pltpu.VMEM((far, model), BF16),
                pltpu.SemaphoreType.DMA((2, hidden // chunk)),
                pltpu.SemaphoreType.DMA((2,)),
                pltpu.SemaphoreType.DMA((2, rows // block)),
            ],
        ),
        out_shape=[jax.ShapeDtypeStruct(*shape) for shape in shapes]
        + [jax.ShapeDtypeStruct((rank, hidden), BF16)] * 2,
        cost_estimate=BRIEF,
        name="mlp",
    )(place, gb, down, up, u1, d2, n_own, n_far, *parts)


def project_kernel(moves, pieces, place_ref, n_ref, u_ref, lift_ref, *refs):
    parts, (w_in, w_out, qkv_ref, in_all, out_all, sems, back) = refs[:pieces], refs[pieces:]

    def copies():
        column = 0
        for j, target in enumerate((in_all, out_all)):
            width = target.shape[1] // 2
            for k, (part, start, depth) in enumerate(moves):
                down = pl.ds(pl.multiple_of(place_ref[0, k] * depth, depth), depth)
                along = pl.ds(pl.multiple_of(place_ref[1, k] * width, width), width)
                yield pltpu.make_async_copy(
                    parts[part].at[pl.ds(start, depth), pl.ds(column, width)],
                    target.at[down, along],
                    sems.at[j, k],
                )
            column += width

    backs = [
        pltpu.make_async_copy(in_all, w_in, back.at[0]),
        pltpu.make_async_copy(out_all, w_out, back.at[1]),
    ]

    @pl.when(pl.program_id(0) == 0)
    def _():
        pending = list(copies())
        for copy in pending:
            copy.start()
        for copy in pending:
            copy.wait()
        for copy in backs:
            copy.start()

    sums = dot(n_ref[...], in_all[...]) + dot_tn(u_ref[...], lift_ref[...])
    qkv_ref[...] = sums.astype(BF16)

    @pl.when(pl.program_id(0) == pl.num_programs(0) - 1)
    def _():
        for copy in backs:
            copy.wait()


def project(n, u, lift, parts, moves, place, width):
    rows, model = n.shape
    block = min(256, rows)
    anywhere = pl.BlockSpec(memory_space=pl.ANY)
    shapes = [(model, 6 * width), (model, 2 * width), (rows, 6 * width)]
    return pl.pallas_call(
        functools.partial(project_kernel, moves, len(parts)),
        grid_spec=pltpu.PrefetchScalarGridSpec(
            num_scalar_prefetch=1,
            grid=(rows // block,),
            in_specs=[
                pl.BlockSpec((block, model), lambda i, place: (i, 0)),
                pl.BlockSpec((u.shape[0], block), lambda i, place: (0, i)),
                pl.BlockSpec(lift.shape, lambda i, place: (0, 0)),
            ]
            + [anywhere] * len(parts),
            out_specs=[
                anywhere,
                anywhere,
                pl.BlockSpec((block, 6 * width), lambda i, place: (i, 0)),
            ],
            scratch_shapes=[
                pltpu.VMEM((model, 6 * width), BF16),
                pltpu.VMEM((model, 2 * width), BF16),
                pltpu.SemaphoreType.DMA((2, len(moves))),
                pltpu.SemaphoreType.DMA((2,)),
            ],
        ),
        out_shape=[jax.ShapeDtypeStruct(shape, BF16) for shape in shapes],
        cost_estimate=BRIEF,
        name="project",
    )(place, n, u, lift, *parts)


def pick_kernel(sides, _, *refs):
    sources, outs = refs[: 4 * sides], refs[4 * sides :]
    for far, out in enumerate(outs):
        up, fc1, proj, fc2 = sources[4 * far : 4 * far + 4]
        column = 0
        for piece in [up[0, 0], up[0, 1], up[0, 2], fc1[0], proj[0], fc2[0]]:
            out[:, column : column + piece.shape[1]] = piece
            column += piece.shape[1]


def pick(chosen, ups):
    rank = ups[1].shape[1]
    wide = sum(up.shape[-1] for up in ups) + 2 * ups[0].shape[-1]
    sides = chosen.shape[0]
    specs = [
        pl.BlockSpec(
            (1,) + up.shape[1:],
            lambda i, e, far=far, n=up.ndim: (e[far],) + (0,) * (n - 1),
        )
        for far in range(sides)
        for up in ups
    ]
    return pl.pallas_call(
        functools.partial(pick_kernel, sides),
        grid_spec=pltpu.PrefetchScalarGridSpec(
            num_scalar_prefetch=1,
            grid=(1,),
            in_specs=specs,
            out_specs=[pl.BlockSpec((rank, wide), lambda i, e: (0, 0))] * sides,
        ),
        out_shape=[jax.ShapeDtypeStruct((rank, wide), BF16)] * sides,
        name="pick",
    )(chosen, *(list(ups) * sides))


def lifts_kernel(sizes, *refs):
    packs, (qkv_ref, fc1_ref, proj_ref, fc2_ref) = refs[:-4], refs[-4:]
    rank = fc1_ref.shape[0]
    width, hidden = sizes
    qkv_ref[...] = jnp.zeros_like(qkv_ref)
    for far, pack in enumerate(packs):
        for j in range(3):
            column = (3 * far + j) * width
            qkv_ref[j * rank : (j + 1) * rank, column : column + width] = pack[
                :, j * width : (j + 1) * width
            ]
        start = 3 * width
        for ref, size in ((fc1_ref, hidden), (proj_ref, width), (fc2_ref, hidden)):
            ref[:, far * size : (far + 1) * size] = pack[:, start : start + size]
            start += size


def lifts(packs, width, hidden):
    rank = packs[0].shape[0]
    sides = len(packs)
    shapes = [(3 * rank, 3 * width), (rank, hidden), (rank, width), (rank, hidden)]
    return pl.pallas_call(
        functools.partial(lifts_kernel, (width, hidden)),
        out_shape=[jax.ShapeDtypeStruct((r, sides * c), BF16) for r, c in shapes],
        name="lifts",
    )(*packs)


def totals_kernel(blocks, widths, *refs):
    sources, outs = refs[:blocks], refs[blocks:]
    for out in outs:
        out[...] = jnp.zeros_like(out)
    total = sum(widths)
    for source in sources:
        for k in range(source.shape[0]):
            owner = jnp.max(source[k, :, total:].astype(F32)).astype(jnp.int32)
            column = 0
            for out, width in zip(outs, widths):
                split = out.shape[1] if len(out.shape) == 4 else 1
                for j in range(split):
                    part = source[k, :, column : column + width // split].astype(F32)
                    if split > 1:
                        out[owner, j] += part
                    else:
                        out[owner] += part
                    column += width // split


def totals(blocks, widths, adapters, split=1):
    rank = blocks[0].shape[1]
    return pl.pallas_call(
        functools.partial(totals_kernel, len(blocks), widths),
        out_shape=[
            jax.ShapeDtypeStruct(
                (adapters, split, rank, width // split)
                if split > 1 and k == 0
                else (adapters, rank, width),
                F32,
            )
            for k, width in enumerate(widths)
        ],
        name="totals",
    )(*blocks)


def spread_kernel(order, core_ref, *refs):
    halves, target = refs[:-1], refs[-1]
    cut = target.shape[3] // 2
    first = core_ref[0] == 0
    for j, (pair, k) in enumerate(order):
        own = halves[2 * pair][:, :, k * cut : (k + 1) * cut]
        other = halves[2 * pair + 1][:, :, k * cut : (k + 1) * cut]
        target[:, j, :, :cut] = jnp.where(first, own, other)
        target[:, j, :, cut:] = jnp.where(first, other, own)


def spread(core, halves, order, cut):
    adapters, rank, _ = halves[0].shape
    return pl.pallas_call(
        functools.partial(spread_kernel, order),
        in_specs=[pl.BlockSpec(memory_space=pltpu.SMEM)]
        + [pl.BlockSpec(memory_space=pltpu.VMEM)] * len(halves),
        out_shape=jax.ShapeDtypeStruct((adapters, len(order), rank, 2 * cut), F32),
        name="spread",
    )(jnp.reshape(core, (1,)), *halves)


def settle_kernel(count, where_ref, *refs):
    parts, out = refs[:count], refs[-1]
    for k, part in enumerate(parts):

        @pl.when(pl.program_id(0) == k)
        def _():
            out[0] = part[...].astype(out.dtype)


def settle(parts, where, first, stride, kind, images, base=None):
    rows, model = parts[0].shape
    extra = [] if base is None else [base]
    return pl.pallas_call(
        functools.partial(settle_kernel, len(parts)),
        grid_spec=pltpu.PrefetchScalarGridSpec(
            num_scalar_prefetch=1,
            grid=(len(parts),),
            in_specs=[pl.BlockSpec((rows, model), lambda k, where: (0, 0))] * len(parts)
            + [pl.BlockSpec(memory_space=pl.ANY)] * len(extra),
            out_specs=pl.BlockSpec((1, rows, model), lambda k, where: (where[first + stride * k], 0, 0)),
        ),
        out_shape=jax.ShapeDtypeStruct((images, rows, model), kind),
        input_output_aliases={1 + len(parts): 0} if extra else {},
        name="settle",
    )(where, *parts, *extra)


def normalize(values, gain, shift):
    centre = values - jnp.mean(values, axis=-1, keepdims=True)
    inverse = lax.rsqrt(jnp.mean(centre * centre, axis=-1, keepdims=True) + EPS)
    unit = centre * inverse
    return unit * gain + shift, unit, inverse


def norm_back(grad, unit, inverse, gain):
    scaled = grad * gain
    centred = scaled - jnp.mean(scaled, axis=-1, keepdims=True)
    return inverse * (centred - unit * jnp.mean(scaled * unit, axis=-1, keepdims=True))


def per_device(
    sizes,
    tokens,
    cotangent,
    adapter_index,
    ln1_gain,
    ln1_bias,
    ln2_gain,
    ln2_bias,
    layer_scale,
    w_qkv,
    w_proj,
    w_fc1,
    w_fc2,
    down_in,
    qkv_up,
    fc1_up,
    proj_down,
    fc2_down,
    out_up,
):
    shards, contexts, tensors = sizes
    half = contexts // 2
    sides = tensors // 2
    images, rows, model = tokens.shape
    rank = down_in.shape[-1]
    depth = w_fc1.shape[0]
    width = w_proj.shape[1]
    hidden = w_fc1.shape[1]
    pairs = width // PAIR
    adapters = down_in.shape[0]
    shard = lax.axis_index("shard")
    context = lax.axis_index("context")
    tensor = lax.axis_index("tensor")
    side, core = tensor // 2, tensor % 2
    high = context // half

    ring = {
        "shard": [(i, (i + 1) % shards) for i in range(shards)],
        "context": [(i, (i + 1) % contexts) for i in range(contexts)],
        "tensor": [(i, (i + 2) % tensors) for i in range(tensors)],
    }
    count = {"shard": shards, "context": contexts, "tensor": sides}
    twin = [(i, i ^ 1) for i in range(tensors)]
    plane = ("context", "tensor")

    def hop(value, axis):
        return lax.ppermute(value, axis, ring[axis])

    def swap(value):
        return lax.ppermute(value, "tensor", twin)

    def around(value, axis):
        out = [value]
        for _ in range(count[axis] - 1):
            out.append(hop(out[-1], axis))
        return out

    def fence(*values):
        return lax.optimization_barrier(values)

    to_owner = []
    to_home = {far: [] for far in range(sides)}
    for c in range(contexts):
        for s in range(sides):
            for k in range(2):
                here = c * tensors + 2 * s + k
                source = 2 * (c % half) + k
                to_owner.append((source * tensors + 2 * s + c // half, here))
                for far in range(sides):
                    there = (s + far) % sides
                    to_home[far].append((here, source * tensors + 2 * there + c // half))

    ringed = contexts == 2 and sides == 2 and shards == 4
    cross = {0: [], 1: []}
    if ringed:
        for c in range(2):
            for s in range(2):
                for k in range(2):
                    here = c * tensors + 2 * s + k
                    along = c * tensors + 2 * (1 - s) + k
                    aside = (1 - c) * tensors + 2 * s + k
                    cross[0].append((here, along if k == 0 else aside))
                    cross[1].append((here, aside if k == 0 else along))

    def block_of(array, index):
        return lax.dynamic_index_in_dim(array, index, 0, keepdims=False)

    def deliver(value, pairs):
        stay = np.zeros(contexts * tensors, np.int32)
        for a, b in pairs:
            stay[a] = a == b
        got = lax.ppermute(value, plane, [(a, b) for a, b in pairs if a != b])
        if not stay.any():
            return got
        return jnp.where(jnp.asarray(stay)[context * tensors + tensor] == 1, value, got)

    def stays(value, other):
        return jnp.where(core == context, value, other)

    relay = [[], []]
    for c in range(2 if ringed else 0):
        for s in range(2):
            for k in range(2):
                here = c * tensors + 2 * s + k
                along = c * tensors + 2 * (1 - s) + k
                relay[0].append((here, along if k == c else (1 - c) * tensors + 2 * s + 1 - k))
                if k != c:
                    relay[1].append((here, along))

    def send_first(value):
        if ringed:
            return [lax.ppermute(value, plane, relay[0])]
        return [deliver(value, to_home[far]) for far in range(sides)]

    def send_second(value, got):
        if ringed:
            return [got[0], stays(value, lax.ppermute(got[0], plane, relay[1]))]
        return got

    def pair_up(a, b):
        return jnp.concatenate([a, b], axis=0)

    def adapter_of(index, far):
        return block_of(index, 2 * ((side + far) % sides) + high)

    def up_packs(index, ups):
        chosen = jnp.stack([adapter_of(index, far) for far in range(sides)])
        packs = list(pick(chosen, ups))
        for far in range(1, sides):
            send = [(i, (i + 2 * far) % tensors) for i in range(tensors)]
            packs[far] = lax.ppermute(packs[far], "tensor", send)
        return packs

    attn_own = jnp.concatenate([w_qkv[:, j] for j in range(3)] + [w_proj], axis=1)
    ups = (qkv_up, fc1_up, jnp.transpose(proj_down, (0, 2, 1)), jnp.transpose(fc2_down, (0, 2, 1)))
    flows = {}

    def cross_to(value, turn):
        return lax.ppermute(value, plane, cross[turn])

    if ringed:
        z, b, c, d = [attn_own], [], [], []
        ff_own = pair_up(w_fc1, w_fc2)
        got = fence(
            hop(attn_own, "shard"),
            cross_to(attn_own, 0),
            cross_to(attn_own, 1),
            deliver(block_of(tokens, tensor), to_owner),
            hop(ff_own, "shard"),
            ff_own,
            cotangent,
            adapter_index,
            down_in,
            out_up,
            *ups,
        )
        z.append(got[0])
        b.append(got[1])
        c.append(got[2])
        x_own = got[3]
        own = [got[5], got[4]]
        cotangent, adapter_index, down_in, out_up = got[6:10]
        ups = got[10:]
        got = fence(
            hop(z[1], "shard"),
            cross_to(z[1], 0),
            cross_to(z[1], 1),
            cross_to(b[0], 1),
            cross_to(own[0], 0),
            x_own,
            own[1],
            adapter_index,
            *ups,
        )
        z.append(got[0])
        b.append(got[1])
        c.append(got[2])
        d.append(got[3])
        aside = [got[4]]
        x_own, own[1], adapter_index = got[5:8]
        ups = got[8:]
        got = fence(
            hop(z[2], "shard"),
            cross_to(z[2], 0),
            cross_to(z[2], 1),
            cross_to(b[1], 1),
            swap(x_own),
            x_own,
            own[1],
            aside[0],
        )
        z.append(got[0])
        b.append(got[1])
        c.append(got[2])
        d.append(got[3])
        x_other, x_own, own[1], aside[0] = got[4:]
        packs = up_packs(adapter_index, ups)
        own.append(hop(own[1], "shard"))
        got = fence(cross_to(z[3], 0), cross_to(z[3], 1), cross_to(b[2], 1), cotangent, packs[1])
        b.append(got[0])
        c.append(got[1])
        d.append(got[2])
        cotangent, packs[1] = got[3:]
        last = cross_to(b[3], 1)
        own_over, aside_over = [], []

        step_of = np.repeat(np.arange(shards), 4)
        near_0 = np.tile([0, 0, 1, 1], shards)
        far_0 = np.tile([0, 1, 0, 1], shards)
        near = jnp.where(core == 0, near_0, far_0)
        across = jnp.where(core == 0, far_0, near_0)
        row = (shard - step_of) % shards * contexts + (context - near) % contexts
        attn_place = jnp.stack([row, across]).astype(jnp.int32)
        attn_moves = [(k, 0, depth) for k in range(4 * shards)]
        ff_moves = [(k, which * depth, depth, which) for which in range(2) for k in range(4 * shards)]
        ff_place = jnp.concatenate([attn_place, attn_place], axis=1)

        def start(*values):
            got = fence(*values, last, own[0], aside[0], own[2])
            d.append(got[-4])
            own[0], aside[0], own[2] = got[-3:]
            aside.append(hop(aside[0], "shard"))
            own_over.append(cross_to(own[0], 1))
            aside_over.append(cross_to(aside[0], 1))
            return got[:-4]

        def advance(stage, *values):
            count = len(values)
            if stage == 0:
                got = fence(*values, own[2], aside[1], own_over[0], aside_over[0], cotangent)
                own[2], aside[1], own_over[0], aside_over[0], late_cotangent = got[count:]
                own.append(hop(own[2], "shard"))
                own_over.append(cross_to(own[1], 1))
                flows["gy"] = deliver(block_of(late_cotangent, tensor), to_owner)
            elif stage == 1:
                got = fence(*values, own[3], own[2], aside[1])
                own[3], own[2], aside[1] = got[count:]
                aside.append(hop(aside[1], "shard"))
                aside_over.append(cross_to(aside[1], 1))
                own_over.append(cross_to(own[2], 1))
            elif stage == 2:
                got = fence(
                    *values, aside[2], own_over[1], own_over[2], aside_over[1], own[3], flows["gy"]
                )
                aside[2], own_over[1], own_over[2], aside_over[1], own[3], flows["gy"] = got[count:]
                aside.append(hop(aside[2], "shard"))
                own_over.append(cross_to(own[3], 1))
                aside_over.append(cross_to(aside[2], 1))
            else:
                got = fence(*values, aside[3], own_over[3], aside_over[2])
                aside[3], own_over[3], aside_over[2] = got[count:]
                aside_over.append(cross_to(aside[3], 1))
            return got[:count]

    else:

        def gather_plain(value):
            whole = lax.all_gather(value, ("shard", "context"), axis=0, tiled=True)
            return around(whole, "tensor")

        attn_parts = gather_plain(attn_own)
        fc1_parts = gather_plain(w_fc1)
        fc2_parts = gather_plain(w_fc2)
        packs = up_packs(adapter_index, ups)
        x_own = deliver(block_of(tokens, tensor), to_owner)
        x_other = swap(x_own)
        flows["gy"] = deliver(block_of(cotangent, tensor), to_owner)
        attn_moves = [(k, 0, model) for k in range(sides)]
        attn_place = jnp.asarray([[0] * sides, list(range(sides))], jnp.int32)
        ff_moves = [(k, 0, model, k // sides) for k in range(2 * sides)]
        ff_place = jnp.concatenate([attn_place, attn_place], axis=1)

        def start(*values):
            return values

        def advance(stage, *values):
            return values

    mine = adapter_of(adapter_index, 0)
    down = block_of(down_in, mine)
    down_t = jnp.transpose(down, (0, 2, 1)).reshape(4 * rank, model)
    out_t = block_of(out_up, mine)

    x_all = pair_up(x_own, x_other).astype(F32)
    normed, unit_one, inverse_one = normalize(x_all, ln1_gain, ln1_bias)
    n1 = normed.astype(BF16)
    u = dot_nt(down_t[: 3 * rank], n1).astype(BF16)
    qkv_lift, fc1_lift, proj_t, fc2_t = lifts(packs, width, hidden)
    n1, u, qkv_lift = start(n1, u, qkv_lift)
    if ringed:
        attn_parts = [part for i in range(shards) for part in (z[i], b[i], c[i], d[i])]
    w_in, w_out, qkv = project(n1, u, qkv_lift, attn_parts, attn_moves, attn_place, width)
    (qkv,) = advance(0, qkv)

    steps = [[h * half + i for i in range(half)] for h in range(2)]
    per_side = width // PAIR
    pairs = per_side * sides
    near, group_count = (per_side, sides) if half == 1 else (1, pairs // half)

    def to_heads(array, thirds_each):
        if half == 1:
            return array
        cells = array.reshape(array.shape[0], sides, thirds_each, per_side, PAIR)
        cells = jnp.transpose(cells, (0, 1, 3, 2, 4)).reshape(array.shape[0], pairs, -1)
        moved = lax.all_to_all(cells, "context", 1, 0, axis_index_groups=steps, tiled=True)
        return moved.reshape(moved.shape[0], -1)

    def to_rows(array, thirds_each):
        if half == 1:
            return array
        cells = array.reshape(array.shape[0], pairs // half, -1)
        moved = lax.all_to_all(cells, "context", 0, 1, axis_index_groups=steps, tiled=True)
        moved = moved.reshape(moved.shape[0], sides, per_side, thirds_each, PAIR)
        return jnp.transpose(moved, (0, 1, 3, 2, 4)).reshape(moved.shape[0], -1)

    qkv_heads = to_heads(qkv, 3)
    o_heads = None
    logs = []
    for group in range(group_count):
        o_heads, lse = attend(qkv_heads, group, near, o_heads)
        logs.append(lse)
        if group == 0:
            o_heads, qkv_heads = advance(1, o_heads, qkv_heads)
    (o_heads,) = advance(2, o_heads)
    gy_own = flows["gy"]
    o = to_rows(o_heads, 1)
    attn_far = dot_nt(o[rows:], w_out)
    c_part = dot_nt(proj_t, o)
    attn_sum = swap(attn_far) + dot_nt(o[:rows], w_out)
    c_own = (c_part[:, :rows] + swap(c_part[:, rows:])).astype(BF16)
    h = x_all[:rows] + layer_scale[0] * (attn_sum + dot_tn(c_own, out_t[0]))
    normed, unit_two, inverse_two = normalize(h, ln2_gain, ln2_bias)
    n2_own = normed.astype(BF16)
    gb_own = (gy_own.astype(F32) * layer_scale[1]).astype(BF16)
    gb = pair_up(gb_own, swap(gb_own))
    n2_own, gb = advance(3, n2_own, gb)
    n2_far = swap(n2_own)
    if ringed:
        ff_parts = [
            part
            for i in range(shards)
            for part in (own[i], aside[i], own_over[i], aside_over[i])
        ]
    else:
        ff_parts = fc1_parts + fc2_parts
    branch_own, branch_far, gn2_own, gn2_far, rank_own, rank_far, g_fc1, g_fc2 = mlp(
        n2_own, n2_far, gb, down_t[3 * rank :], out_t[1], ff_parts, ff_moves, ff_place, fc1_lift, fc2_t
    )
    ranks = (rank_own + swap(rank_far)).astype(BF16)
    m_own, gf_own = ranks[:rank], ranks[rank:]
    branch = branch_own + swap(branch_far).astype(F32) + dot_tn(m_own, out_t[1])
    result_own = (h + layer_scale[1] * branch).astype(BF16)
    gn2 = gn2_own + swap(gn2_far) + dot_tn(gf_own, down_t[3 * rank :])
    g_out1 = dot(m_own, gb[:rows])
    g_down3 = dot(gf_own, n2_own)

    cut = model // 2
    one = jnp.where(context % half == 0, mine, 0)
    mark = jnp.full((rank, 128), one).astype(BF16)

    def halves(shared):
        shared = jnp.stack(shared)
        away = lax.dynamic_slice_in_dim(shared, (1 - core) * cut, cut, 2)
        keep = lax.dynamic_slice_in_dim(shared, core * cut, cut, 2)
        both = keep + swap(away)
        return [both[j] for j in range(len(both))]

    def to_sides(slices, shared):
        packed = []
        for far in range(sides):
            pack = jnp.concatenate([part.astype(BF16) for part in slices[far] + shared] + [mark], axis=1)
            if far:
                send = [(i, (i - 2 * far) % tensors) for i in range(tensors)]
                pack = lax.ppermute(pack, "tensor", send)
            packed.append(pack)
        return jnp.stack(packed)

    opposite = [(i, (i + half) % contexts) for i in range(contexts)]

    def merge(block):
        if half == 1:
            return block
        total = lax.psum(block.astype(F32), "context", axis_index_groups=steps)
        return total.astype(BF16)

    def over(block):
        return lax.ppermute(block, "context", opposite)

    def columns(array, far, size):
        return array[:, far * size : (far + 1) * size]

    early = to_sides(
        [[columns(g_fc1, far, hidden), columns(g_fc2, far, hidden)] for far in range(sides)],
        halves([g_down3, g_out1]),
    )
    gh = gy_own.astype(F32) + norm_back(gn2, unit_two, inverse_two, ln2_gain)
    gattn_own = (layer_scale[0] * gh).astype(BF16)
    gattn_far, early = fence(swap(gattn_own), early)
    gattn = pair_up(gattn_own, gattn_far)
    early_line = [merge(early)]
    early_line.append(hop(early_line[0], "shard"))
    early_over = [over(early_line[0])]
    g_out0 = dot(c_own, gattn_own)
    gc = dot_nt(out_t[0], gattn).astype(BF16)
    g_proj = dot(gc, o)
    mid = to_sides([[columns(g_proj, far, width)] for far in range(sides)], halves([g_out0]))
    go = (dot(gattn, w_out) + dot_tn(gc, proj_t)).astype(BF16)
    early_line[1], early_over[0], mid, go, result_own = fence(
        early_line[1], early_over[0], mid, go, result_own
    )
    early_line.append(hop(early_line[1], "shard"))
    early_over.append(over(early_line[1]))
    mid = merge(mid)
    mid_over = over(mid)
    sent = send_first(result_own)
    go_heads = to_heads(go, 1)
    g_heads = None
    for group in range(group_count):
        g_heads = attend_back(qkv_heads, go_heads, o_heads, logs[group], group, near, g_heads)
        if group == 0:
            g_heads, mid_over, early_line[2], *sent = fence(
                g_heads, mid_over, early_line[2], *sent
            )
            early_over.append(over(early_line[2]))
            for _ in range(3, shards):
                early_line.append(hop(early_line[-1], "shard"))
            mid_line = [pair_up(mid, mid_over)]
            mid_line.append(hop(mid_line[0], "shard"))
            sent = send_second(result_own, sent)
    g_heads, mid_line[1], early_over[1], early_over[2], *got = fence(
        g_heads, mid_line[1], early_over[1], early_over[2], *early_line[3:], *sent
    )
    early_line[3:], sent = got[: shards - 3], got[shards - 3 :]
    early_over.extend([over(block) for block in early_line[3:]])
    mid_line.append(hop(mid_line[1], "shard"))
    g = to_rows(g_heads, 3)

    gu_part = dot_nt(qkv_lift, g)
    gu_own = (gu_part[:, :rows] + swap(gu_part[:, rows:])).astype(BF16)
    gn1_far = swap(dot_nt(g[rows:], w_in))
    g_up = dot(u, g)
    gn1 = dot_nt(g[:rows], w_in) + gn1_far + dot_tn(gu_own, down_t[: 3 * rank])
    g_down = dot(gu_own, n1[:rows])
    late_slices = [
        [
            g_up[j * rank : (j + 1) * rank, (far * 3 + j) * width : (far * 3 + j + 1) * width]
            for j in range(3)
        ]
        for far in range(sides)
    ]
    late = to_sides(late_slices, halves([g_down[j * rank : (j + 1) * rank] for j in range(3)]))
    input_own = gh + norm_back(gn1, unit_one[:rows], inverse_one[:rows], ln1_gain)
    input_own = input_own.astype(BF16)
    late_line = [merge(late)]
    late_line.append(hop(late_line[0], "shard"))
    late_over = [over(late_line[0])]
    last_over = early_over[3:]
    late_line[1], late_over[0], input_own, mid_line[2], *got = fence(
        late_line[1], late_over[0], input_own, mid_line[2], *last_over, *sent
    )
    early_over[3:], sent = got[: len(last_over)], got[len(last_over) :]

    order = np.tile(np.arange(sides), 2)
    flip = np.repeat([0, 1], sides)
    far = jnp.where((core ^ flip) == context, 1 - order, order) if ringed else order
    where = (2 * ((side - far) % sides) + (core ^ flip)).astype(jnp.int32)
    late_line.append(hop(late_line[1], "shard"))
    input_sent = send_first(input_own)
    for _ in range(3, shards):
        mid_line.append(hop(mid_line[-1], "shard"))
    sent = list(sent) + [swap(part) for part in sent]
    fc1_grad, fc2_grad, early_half = totals(
        early_line + early_over, (hidden, hidden, 2 * cut), adapters
    )
    late_line[1], late_line[2], early_half, *got = fence(
        late_line[1], late_line[2], early_half, *sent, *mid_line
    )
    sent, mid_line = got[: 2 * sides], got[2 * sides :]
    for _ in range(3, shards):
        late_line.append(hop(late_line[-1], "shard"))
    late_over.append(over(late_line[1]))
    early_twin = swap(early_half)
    result = settle(sent, where, 0, 1, BF16, images)
    proj_grad, mid_half = totals(mid_line, (width, cut), adapters)
    late_line[-1], late_over[1], early_half, early_twin, mid_half, result, *input_sent = fence(
        late_line[-1], late_over[1], early_half, early_twin, mid_half, result, *input_sent
    )
    late_over.extend([over(block) for block in late_line[2:]])
    first_twin = swap(input_sent[0])
    input_sent = send_second(input_own, input_sent)
    mid_twin = swap(mid_half)
    input_grad = settle([input_sent[0], first_twin], where, 0, sides, F32, images)
    out_grad = spread(
        core, [mid_half, mid_twin, early_half, early_twin], ((0, 0), (1, 1)), cut
    )
    late_line[0], input_grad, out_grad, *late_over = fence(
        late_line[0], input_grad, out_grad, *late_over
    )
    qkv_grad, late_half = totals(late_line + late_over, (3 * width, 3 * cut), adapters, 3)
    late_half, qkv_grad, *input_sent = fence(late_half, qkv_grad, *input_sent)
    late_twin = swap(late_half)
    last_twins = [swap(part) for part in input_sent[1:]]
    input_grad = settle(input_sent[1:] + last_twins, where, 1, sides, F32, images, input_grad)
    down_grad = spread(
        core,
        [late_half, late_twin, early_half, early_twin],
        ((0, 0), (0, 1), (0, 2), (1, 0)),
        cut,
    )
    return (
        result,
        input_grad,
        jnp.transpose(down_grad, (0, 1, 3, 2)),
        qkv_grad,
        fc1_grad,
        jnp.transpose(proj_grad, (0, 2, 1)),
        jnp.transpose(fc2_grad, (0, 2, 1)),
        out_grad,
    )


def solution(mesh):
    sizes = (mesh.shape["shard"], mesh.shape["context"], mesh.shape["tensor"])
    placed = (
        P("shard", "context", None),
        P("shard", "context", None),
        P("shard"),
        P(),
        P(),
        P(),
        P(),
        P(),
        P(("shard", "context"), None, "tensor"),
        P(("shard", "context"), "tensor"),
        P(("shard", "context"), "tensor"),
        P(("shard", "context"), "tensor"),
        P(),
        P(None, None, None, "tensor"),
        P(None, None, "tensor"),
        P(None, "tensor", None),
        P(None, "tensor", None),
        P(),
    )
    return jax.shard_map(
        functools.partial(per_device, sizes),
        mesh=mesh,
        in_specs=placed,
        out_specs=(
            P("shard", "context", None),
            P("shard", "context", None),
            P(),
            P(None, None, None, "tensor"),
            P(None, None, "tensor"),
            P(None, "tensor", None),
            P(None, "tensor", None),
            P(),
        ),
        check_vma=False,
    )
```

```python
import functools
import math

import jax
import jax.numpy as jnp
import numpy as np
from jax import lax
from jax.experimental import pallas as pl
from jax.experimental.pallas import tpu as pltpu
from jax.sharding import PartitionSpec as P

HEAD_DIM = 64
PAIR = 2 * HEAD_DIM
EPS = 1e-06
LOG2E = math.log2(math.e)
SCORE = 1.0 / math.sqrt(HEAD_DIM)
F32 = jnp.float32
BF16 = jnp.bfloat16
NT = (((1,), (1,)), ((), ()))
TN = (((0,), (0,)), ((), ()))
BRIEF = pl.CostEstimate(flops=1000, bytes_accessed=1000, transcendentals=0)


def dot(a, b):
    return jnp.dot(a, b, preferred_element_type=F32)


def dot_nt(a, b):
    return lax.dot_general(a, b, NT, preferred_element_type=F32)


def dot_tn(a, b):
    return lax.dot_general(a, b, TN, preferred_element_type=F32)


def head_masks(rows):
    lane = lax.broadcasted_iota(jnp.int32, (rows, PAIR), 1)
    return lane < HEAD_DIM


def attend_kernel(block, q_ref, k_ref, v_ref, _, o_ref, lse_ref):
    rows = q_ref.shape[0]
    keys = k_ref[...]
    values = jnp.concatenate([v_ref[...], jnp.ones((rows, PAIR), BF16)], axis=1)
    first = head_masks(block)

    def step(i, carry):
        at = pl.ds(pl.multiple_of(i * block, block), block)
        q = q_ref[at, :]
        outs = []
        logs = []
        for head in range(2):
            mine = first if head == 0 else jnp.logical_not(first)
            s = dot_nt(jnp.where(mine, q, jnp.zeros_like(q)), keys)
            peak = jnp.max(s, axis=1, keepdims=True)
            e = jnp.exp2((s - peak) * (SCORE * LOG2E))
            acc = dot(e.astype(BF16), values)
            total = acc[:, PAIR:]
            outs.append(acc[:, :PAIR] / total)
            logs.append(peak * (SCORE * LOG2E) + jnp.log2(total))
        o_ref[at, :] = jnp.where(first, outs[0], outs[1]).astype(BF16)
        lane = lax.broadcasted_iota(jnp.int32, (block, PAIR), 1)
        both = jnp.where(lane == 0, logs[0], logs[1])
        lse_ref[0, :, at] = jnp.transpose(both)[:8]
        return carry

    lax.fori_loop(0, rows // block, step, 0)


def thirds(rows, group, near):
    return [
        pl.BlockSpec((rows, PAIR), lambda p, j=j: (0, (group * 3 + j) * near + p))
        for j in range(3)
    ]


def attend(qkv, group, near, o):
    rows, width = qkv.shape
    pairs = width // (3 * PAIR)
    block = min(256, rows)
    anywhere = pl.BlockSpec(memory_space=pl.ANY)
    operands = [qkv, qkv, qkv, qkv if o is None else o]
    return pl.pallas_call(
        functools.partial(attend_kernel, block),
        grid=(near,),
        in_specs=thirds(rows, group, near) + [anywhere],
        out_specs=[
            pl.BlockSpec((rows, PAIR), lambda p: (0, group * near + p)),
            pl.BlockSpec((1, 8, rows), lambda p: (p, 0, 0)),
        ],
        out_shape=[
            jax.ShapeDtypeStruct((rows, pairs * PAIR), BF16),
            jax.ShapeDtypeStruct((near, 8, rows), F32),
        ],
        input_output_aliases={} if o is None else {3: 0},
        cost_estimate=BRIEF,
        name="attend",
    )(*operands)


def attend_back_kernel(
    block, near, q_ref, k_ref, v_ref, go_ref, o_ref, lse_ref, _, g_ref, gq_ref, d_ref
):
    rows = q_ref.shape[0]
    pair = pl.program_id(0)
    lanes = [pl.ds(pl.multiple_of((j * near + pair) * PAIR, PAIR), PAIR) for j in range(3)]
    first = head_masks(block)
    prod = o_ref[...].astype(F32) * go_ref[...].astype(F32)
    lane8 = lax.broadcasted_iota(jnp.int32, (8, PAIR), 1) // HEAD_DIM
    row8 = lax.broadcasted_iota(jnp.int32, (8, PAIR), 0)
    d_ref[...] = lax.dot_general(
        (lane8 == row8).astype(F32),
        prod,
        NT,
        preferred_element_type=F32,
        precision=lax.Precision.HIGHEST,
    )
    gq_ref[...] = jnp.zeros_like(gq_ref)

    def step(i, carry):
        at = pl.ds(pl.multiple_of(i * block, block), block)
        k = k_ref[at, :]
        v = v_ref[at, :]
        q = q_ref[...]
        go = go_ref[...]
        gks = []
        gvs = []
        gq = None
        for head in range(2):
            mine = first if head == 0 else jnp.logical_not(first)
            k_own = jnp.where(mine, k, jnp.zeros_like(k))
            v_own = jnp.where(mine, v, jnp.zeros_like(v))
            s = dot_nt(k_own, q)
            gp = dot_nt(v_own, go)
            p = jnp.exp2(s * (SCORE * LOG2E) - lse_ref[0, head : head + 1, :])
            gs = (p * (gp - d_ref[head : head + 1, :])).astype(BF16)
            gks.append(dot(gs, q))
            gvs.append(dot(p.astype(BF16), go))
            part = dot(jnp.transpose(k_own), gs)
            gq = part if gq is None else gq + part
        gq_ref[...] += gq
        g_ref[at, lanes[1]] = (jnp.where(first, gks[0], gks[1]) * SCORE).astype(BF16)
        g_ref[at, lanes[2]] = jnp.where(first, gvs[0], gvs[1]).astype(BF16)
        return carry

    lax.fori_loop(0, rows // block, step, 0)
    g_ref[:, lanes[0]] = (jnp.transpose(gq_ref[...]) * SCORE).astype(BF16)


def attend_back(qkv, go, o, lse, group, near, g):
    rows, width = qkv.shape
    block = min(256, rows)
    mine = pl.BlockSpec((rows, PAIR), lambda p: (0, group * near + p))
    anywhere = pl.BlockSpec(memory_space=pl.ANY)
    operands = [qkv, qkv, qkv, go, o, lse, qkv if g is None else g]
    return pl.pallas_call(
        functools.partial(attend_back_kernel, block, near),
        grid=(near,),
        in_specs=thirds(rows, group, near)
        + [mine, mine, pl.BlockSpec((1, 8, rows), lambda p: (p, 0, 0)), anywhere],
        out_specs=pl.BlockSpec((rows, 3 * near * PAIR), lambda p: (0, group)),
        out_shape=jax.ShapeDtypeStruct((rows, width), BF16),
        scratch_shapes=[pltpu.VMEM((PAIR, rows), F32), pltpu.VMEM((8, rows), F32)],
        input_output_aliases={} if g is None else {6: 0},
        cost_estimate=BRIEF,
        name="attend_back",
    )(*operands)


def mlp_kernel(
    block,
    own,
    moves,
    pieces,
    place_ref,
    gb_ref,
    down_ref,
    up_ref,
    u1_ref,
    d2_ref,
    n_own,
    n_far,
    *refs,
):
    parts = refs[:pieces]
    outs, scratch = refs[pieces : pieces + 8], refs[pieces + 8 :]
    branch_own, branch_far, gn_own, gn_far = outs[:4]
    rank_own, rank_far, gf1_out, gf2_out = outs[4:]
    w1_all, w2_all, n_ref, f_ref, gm_ref, branch_ref, gn_ref = scratch[:7]
    rank_ref, gf1_ref, gf2_ref, cast_ref, sems, row_sems, out_sems = scratch[7:]
    rank = f_ref.shape[0]
    rows = n_ref.shape[0]
    chunk = u1_ref.shape[1]
    at_chunk = pl.ds(pl.multiple_of(pl.program_id(0) * chunk, chunk), chunk)

    @pl.when(pl.program_id(0) == 0)
    def _():
        rows_in = [
            pltpu.make_async_copy(n_own, n_ref.at[:own, :], row_sems.at[0]),
            pltpu.make_async_copy(n_far, n_ref.at[own:, :], row_sems.at[1]),
        ]
        for copy in rows_in:
            copy.start()
        for split in range(parts[0].shape[1] // chunk):
            for k, (part, start, depth, which) in enumerate(moves):
                number = place_ref[1, k] * (parts[part].shape[1] // chunk) + split
                down = pl.ds(pl.multiple_of(place_ref[0, k] * depth, depth), depth)
                along = pl.ds(pl.multiple_of(number * chunk, chunk), chunk)
                pltpu.make_async_copy(
                    parts[part].at[pl.ds(start, depth), pl.ds(split * chunk, chunk)],
                    (w1_all, w2_all)[which].at[down, along],
                    sems.at[which, number],
                ).start()
        branch_ref[...] = jnp.zeros_like(branch_ref)
        gn_ref[...] = jnp.zeros_like(gn_ref)
        rank_ref[...] = jnp.zeros_like(rank_ref)
        gm_ref[...] = dot_nt(up_ref[...], gb_ref[...]).astype(BF16)
        for copy in rows_in:
            copy.wait()
        f_ref[...] = dot_nt(down_ref[...], n_ref[...]).astype(BF16)

    final = pl.program_id(0) == pl.num_programs(0) - 1

    def leave(i, at, to, home):
        branch = branch_ref.at[at, :] if home else cast_ref.at[to, :]
        target = branch_own if home else branch_far
        gn_target = gn_own if home else gn_far
        return [
            pltpu.make_async_copy(branch, target.at[to, :], out_sems.at[0, i]),
            pltpu.make_async_copy(gn_ref.at[at, :], gn_target.at[to, :], out_sems.at[1, i]),
        ]

    for which, target in enumerate((w1_all, w2_all)):
        area = target.at[:, at_chunk]
        pltpu.make_async_copy(area, area, sems.at[which, pl.program_id(0)]).wait()
    gf1_ref[...] = jnp.zeros_like(gf1_ref)
    gf2_ref[...] = jnp.zeros_like(gf2_ref)

    def step(i, carry):
        at = pl.ds(pl.multiple_of(i * block, block), block)
        w1 = w1_all[:, at_chunk]
        w2 = w2_all[:, at_chunk]
        u1 = u1_ref[...]
        d2 = d2_ref[...]
        z = dot(n_ref[at, :], w1) + dot_tn(f_ref[:, at], u1)
        cdf = 0.5 * (1.0 + lax.erf(z * (1.0 / math.sqrt(2.0))))
        a = (z * cdf).astype(BF16)
        slope = cdf + z * (jnp.exp2(z * z * (-0.5 * LOG2E)) * (1.0 / math.sqrt(2.0 * math.pi)))
        ga = dot(gb_ref[at, :], w2) + dot_tn(gm_ref[:, at], d2)
        gz = (ga * slope).astype(BF16)
        branch_ref[at, :] += dot_nt(a, w2)
        rank_ref[:rank, at] += dot_nt(d2, a)
        gn_ref[at, :] += dot_nt(gz, w1)
        rank_ref[rank:, at] += dot_nt(u1, gz)
        gf1_ref[...] += dot(f_ref[:, at], gz)
        gf2_ref[...] += dot(gm_ref[:, at], a)

        @pl.when(jnp.logical_and(final, i < own // block))
        def _():
            for copy in leave(i, at, at, True):
                copy.start()

        @pl.when(jnp.logical_and(final, i >= own // block))
        def _():
            to = pl.ds(pl.multiple_of(i * block - own, block), block)
            cast_ref[to, :] = branch_ref[at, :].astype(BF16)
            for copy in leave(i, at, to, False):
                copy.start()

        return carry

    lax.fori_loop(0, rows // block, step, 0)
    gf1_out[...] = gf1_ref[...].astype(BF16)
    gf2_out[...] = gf2_ref[...].astype(BF16)

    @pl.when(pl.program_id(0) == pl.num_programs(0) - 1)
    def _():
        rank_own[...] = rank_ref[:, :own]
        rank_far[...] = rank_ref[:, own:]
        for i in range(rows // block):
            home = i < own // block
            at = pl.ds(i * block, block)
            to = at if home else pl.ds(i * block - own, block)
            for copy in leave(i, at, to, home):
                copy.wait()


def mlp(n_own, n_far, gb, down, up, parts, moves, place, u1, d2):
    own, model = n_own.shape
    rows = gb.shape[0]
    hidden = u1.shape[1]
    rank = down.shape[0]
    chunk = min(512, hidden)
    block = min(256, own)
    whole = lambda shape: pl.BlockSpec(shape, lambda j, place: (0, 0))
    part = lambda depth: pl.BlockSpec((depth, chunk), lambda j, place: (0, j))
    far = rows - own
    shapes = [
        ((own, model), F32),
        ((far, model), BF16),
        ((own, model), F32),
        ((far, model), F32),
        ((2 * rank, own), F32),
        ((2 * rank, far), F32),
    ]
    return pl.pallas_call(
        functools.partial(mlp_kernel, block, own, moves, len(parts)),
        grid_spec=pltpu.PrefetchScalarGridSpec(
            num_scalar_prefetch=1,
            grid=(hidden // chunk,),
            in_specs=[
                whole((rows, model)),
                whole((rank, model)),
                whole((rank, model)),
                part(rank),
                part(rank),
            ]
            + [pl.BlockSpec(memory_space=pl.ANY)] * (2 + len(parts)),
            out_specs=[pl.BlockSpec(memory_space=pl.ANY)] * 4
            + [whole(shape) for shape, _ in shapes[4:]]
            + [part(rank), part(rank)],
            scratch_shapes=[
                pltpu.VMEM((model, hidden), BF16),
                pltpu.VMEM((model, hidden), BF16),
                pltpu.VMEM((rows, model), BF16),
                pltpu.VMEM((rank, rows), BF16),
                pltpu.VMEM((rank, rows), BF16),
                pltpu.VMEM((rows, model), F32),
                pltpu.VMEM((rows, model), F32),
                pltpu.VMEM((2 * rank, rows), F32),
                pltpu.VMEM((rank, chunk), F32),
                pltpu.VMEM((rank, chunk), F32),
                pltpu.VMEM((far, model), BF16),
                pltpu.SemaphoreType.DMA((2, hidden // chunk)),
                pltpu.SemaphoreType.DMA((2,)),
                pltpu.SemaphoreType.DMA((2, rows // block)),
            ],
        ),
        out_shape=[jax.ShapeDtypeStruct(*shape) for shape in shapes]
        + [jax.ShapeDtypeStruct((rank, hidden), BF16)] * 2,
        cost_estimate=BRIEF,
        name="mlp",
    )(place, gb, down, up, u1, d2, n_own, n_far, *parts)


def project_kernel(moves, pieces, place_ref, n_ref, u_ref, lift_ref, *refs):
    parts, (w_in, w_out, qkv_ref, in_all, out_all, sems, back) = refs[:pieces], refs[pieces:]

    def copies():
        column = 0
        for j, target in enumerate((in_all, out_all)):
            width = target.shape[1] // 2
            for k, (part, start, depth) in enumerate(moves):
                down = pl.ds(pl.multiple_of(place_ref[0, k] * depth, depth), depth)
                along = pl.ds(pl.multiple_of(place_ref[1, k] * width, width), width)
                yield pltpu.make_async_copy(
                    parts[part].at[pl.ds(start, depth), pl.ds(column, width)],
                    target.at[down, along],
                    sems.at[j, k],
                )
            column += width

    backs = [
        pltpu.make_async_copy(in_all, w_in, back.at[0]),
        pltpu.make_async_copy(out_all, w_out, back.at[1]),
    ]

    @pl.when(pl.program_id(0) == 0)
    def _():
        pending = list(copies())
        for copy in pending:
            copy.start()
        for copy in pending:
            copy.wait()
        for copy in backs:
            copy.start()

    sums = dot(n_ref[...], in_all[...]) + dot_tn(u_ref[...], lift_ref[...])
    qkv_ref[...] = sums.astype(BF16)

    @pl.when(pl.program_id(0) == pl.num_programs(0) - 1)
    def _():
        for copy in backs:
            copy.wait()


def project(n, u, lift, parts, moves, place, width):
    rows, model = n.shape
    block = min(256, rows)
    anywhere = pl.BlockSpec(memory_space=pl.ANY)
    shapes = [(model, 6 * width), (model, 2 * width), (rows, 6 * width)]
    return pl.pallas_call(
        functools.partial(project_kernel, moves, len(parts)),
        grid_spec=pltpu.PrefetchScalarGridSpec(
            num_scalar_prefetch=1,
            grid=(rows // block,),
            in_specs=[
                pl.BlockSpec((block, model), lambda i, place: (i, 0)),
                pl.BlockSpec((u.shape[0], block), lambda i, place: (0, i)),
                pl.BlockSpec(lift.shape, lambda i, place: (0, 0)),
            ]
            + [anywhere] * len(parts),
            out_specs=[
                anywhere,
                anywhere,
                pl.BlockSpec((block, 6 * width), lambda i, place: (i, 0)),
            ],
            scratch_shapes=[
                pltpu.VMEM((model, 6 * width), BF16),
                pltpu.VMEM((model, 2 * width), BF16),
                pltpu.SemaphoreType.DMA((2, len(moves))),
                pltpu.SemaphoreType.DMA((2,)),
            ],
        ),
        out_shape=[jax.ShapeDtypeStruct(shape, BF16) for shape in shapes],
        cost_estimate=BRIEF,
        name="project",
    )(place, n, u, lift, *parts)


def pick_kernel(sides, _, *refs):
    sources, outs = refs[: 4 * sides], refs[4 * sides :]
    for far, out in enumerate(outs):
        up, fc1, proj, fc2 = sources[4 * far : 4 * far + 4]
        column = 0
        for piece in [up[0, 0], up[0, 1], up[0, 2], fc1[0], proj[0], fc2[0]]:
            out[:, column : column + piece.shape[1]] = piece
            column += piece.shape[1]


def pick(chosen, ups):
    rank = ups[1].shape[1]
    wide = sum(up.shape[-1] for up in ups) + 2 * ups[0].shape[-1]
    sides = chosen.shape[0]
    specs = [
        pl.BlockSpec(
            (1,) + up.shape[1:],
            lambda i, e, far=far, n=up.ndim: (e[far],) + (0,) * (n - 1),
        )
        for far in range(sides)
        for up in ups
    ]
    return pl.pallas_call(
        functools.partial(pick_kernel, sides),
        grid_spec=pltpu.PrefetchScalarGridSpec(
            num_scalar_prefetch=1,
            grid=(1,),
            in_specs=specs,
            out_specs=[pl.BlockSpec((rank, wide), lambda i, e: (0, 0))] * sides,
        ),
        out_shape=[jax.ShapeDtypeStruct((rank, wide), BF16)] * sides,
        name="pick",
    )(chosen, *(list(ups) * sides))


def lifts_kernel(sizes, *refs):
    packs, (qkv_ref, fc1_ref, proj_ref, fc2_ref) = refs[:-4], refs[-4:]
    rank = fc1_ref.shape[0]
    width, hidden = sizes
    qkv_ref[...] = jnp.zeros_like(qkv_ref)
    for far, pack in enumerate(packs):
        for j in range(3):
            column = (3 * far + j) * width
            qkv_ref[j * rank : (j + 1) * rank, column : column + width] = pack[
                :, j * width : (j + 1) * width
            ]
        start = 3 * width
        for ref, size in ((fc1_ref, hidden), (proj_ref, width), (fc2_ref, hidden)):
            ref[:, far * size : (far + 1) * size] = pack[:, start : start + size]
            start += size


def lifts(packs, width, hidden):
    rank = packs[0].shape[0]
    sides = len(packs)
    shapes = [(3 * rank, 3 * width), (rank, hidden), (rank, width), (rank, hidden)]
    return pl.pallas_call(
        functools.partial(lifts_kernel, (width, hidden)),
        out_shape=[jax.ShapeDtypeStruct((r, sides * c), BF16) for r, c in shapes],
        name="lifts",
    )(*packs)


def totals_kernel(blocks, widths, *refs):
    sources, outs = refs[:blocks], refs[blocks:]
    for out in outs:
        out[...] = jnp.zeros_like(out)
    total = sum(widths)
    for source in sources:
        for k in range(source.shape[0]):
            owner = jnp.max(source[k, :, total:].astype(F32)).astype(jnp.int32)
            column = 0
            for out, width in zip(outs, widths):
                split = out.shape[1] if len(out.shape) == 4 else 1
                for j in range(split):
                    part = source[k, :, column : column + width // split].astype(F32)
                    if split > 1:
                        out[owner, j] += part
                    else:
                        out[owner] += part
                    column += width // split


def totals(blocks, widths, adapters, split=1):
    rank = blocks[0].shape[1]
    return pl.pallas_call(
        functools.partial(totals_kernel, len(blocks), widths),
        out_shape=[
            jax.ShapeDtypeStruct(
                (adapters, split, rank, width // split)
                if split > 1 and k == 0
                else (adapters, rank, width),
                F32,
            )
            for k, width in enumerate(widths)
        ],
        name="totals",
    )(*blocks)


def spread_kernel(order, core_ref, *refs):
    halves, target = refs[:-1], refs[-1]
    cut = target.shape[3] // 2
    first = core_ref[0] == 0
    for j, (pair, k) in enumerate(order):
        own = halves[2 * pair][:, :, k * cut : (k + 1) * cut]
        other = halves[2 * pair + 1][:, :, k * cut : (k + 1) * cut]
        target[:, j, :, :cut] = jnp.where(first, own, other)
        target[:, j, :, cut:] = jnp.where(first, other, own)


def spread(core, halves, order, cut):
    adapters, rank, _ = halves[0].shape
    return pl.pallas_call(
        functools.partial(spread_kernel, order),
        in_specs=[pl.BlockSpec(memory_space=pltpu.SMEM)]
        + [pl.BlockSpec(memory_space=pltpu.VMEM)] * len(halves),
        out_shape=jax.ShapeDtypeStruct((adapters, len(order), rank, 2 * cut), F32),
        name="spread",
    )(jnp.reshape(core, (1,)), *halves)


def settle_kernel(count, where_ref, *refs):
    parts, out = refs[:count], refs[-1]
    for k, part in enumerate(parts):

        @pl.when(pl.program_id(0) == k)
        def _():
            out[0] = part[...].astype(out.dtype)


def settle(parts, where, first, stride, kind, images, base=None):
    rows, model = parts[0].shape
    extra = [] if base is None else [base]
    return pl.pallas_call(
        functools.partial(settle_kernel, len(parts)),
        grid_spec=pltpu.PrefetchScalarGridSpec(
            num_scalar_prefetch=1,
            grid=(len(parts),),
            in_specs=[pl.BlockSpec((rows, model), lambda k, where: (0, 0))] * len(parts)
            + [pl.BlockSpec(memory_space=pl.ANY)] * len(extra),
            out_specs=pl.BlockSpec((1, rows, model), lambda k, where: (where[first + stride * k], 0, 0)),
        ),
        out_shape=jax.ShapeDtypeStruct((images, rows, model), kind),
        input_output_aliases={1 + len(parts): 0} if extra else {},
        name="settle",
    )(where, *parts, *extra)


def normalize(values, gain, shift):
    centre = values - jnp.mean(values, axis=-1, keepdims=True)
    inverse = lax.rsqrt(jnp.mean(centre * centre, axis=-1, keepdims=True) + EPS)
    unit = centre * inverse
    return unit * gain + shift, unit, inverse


def norm_back(grad, unit, inverse, gain):
    scaled = grad * gain
    centred = scaled - jnp.mean(scaled, axis=-1, keepdims=True)
    return inverse * (centred - unit * jnp.mean(scaled * unit, axis=-1, keepdims=True))


def per_device(
    sizes,
    tokens,
    cotangent,
    adapter_index,
    ln1_gain,
    ln1_bias,
    ln2_gain,
    ln2_bias,
    layer_scale,
    w_qkv,
    w_proj,
    w_fc1,
    w_fc2,
    down_in,
    qkv_up,
    fc1_up,
    proj_down,
    fc2_down,
    out_up,
):
    shards, contexts, tensors = sizes
    half = contexts // 2
    sides = tensors // 2
    images, rows, model = tokens.shape
    rank = down_in.shape[-1]
    depth = w_fc1.shape[0]
    width = w_proj.shape[1]
    hidden = w_fc1.shape[1]
    pairs = width // PAIR
    adapters = down_in.shape[0]
    shard = lax.axis_index("shard")
    context = lax.axis_index("context")
    tensor = lax.axis_index("tensor")
    side, core = tensor // 2, tensor % 2
    high = context // half

    ring = {
        "shard": [(i, (i + 1) % shards) for i in range(shards)],
        "context": [(i, (i + 1) % contexts) for i in range(contexts)],
        "tensor": [(i, (i + 2) % tensors) for i in range(tensors)],
    }
    count = {"shard": shards, "context": contexts, "tensor": sides}
    twin = [(i, i ^ 1) for i in range(tensors)]
    plane = ("context", "tensor")

    def hop(value, axis):
        return lax.ppermute(value, axis, ring[axis])

    def swap(value):
        return lax.ppermute(value, "tensor", twin)

    def around(value, axis):
        out = [value]
        for _ in range(count[axis] - 1):
            out.append(hop(out[-1], axis))
        return out

    def fence(*values):
        return lax.optimization_barrier(values)

    to_owner = []
    to_home = {far: [] for far in range(sides)}
    for c in range(contexts):
        for s in range(sides):
            for k in range(2):
                here = c * tensors + 2 * s + k
                source = 2 * (c % half) + k
                to_owner.append((source * tensors + 2 * s + c // half, here))
                for far in range(sides):
                    there = (s + far) % sides
                    to_home[far].append((here, source * tensors + 2 * there + c // half))

    ringed = contexts == 2 and sides == 2 and shards == 4
    cross = {0: [], 1: []}
    if ringed:
        for c in range(2):
            for s in range(2):
                for k in range(2):
                    here = c * tensors + 2 * s + k
                    along = c * tensors + 2 * (1 - s) + k
                    aside = (1 - c) * tensors + 2 * s + k
                    cross[0].append((here, along if k == 0 else aside))
                    cross[1].append((here, aside if k == 0 else along))

    def block_of(array, index):
        return lax.dynamic_index_in_dim(array, index, 0, keepdims=False)

    def deliver(value, pairs):
        stay = np.zeros(contexts * tensors, np.int32)
        for a, b in pairs:
            stay[a] = a == b
        got = lax.ppermute(value, plane, [(a, b) for a, b in pairs if a != b])
        if not stay.any():
            return got
        return jnp.where(jnp.asarray(stay)[context * tensors + tensor] == 1, value, got)

    def stays(value, other):
        return jnp.where(core == context, value, other)

    relay = [[], []]
    for c in range(2 if ringed else 0):
        for s in range(2):
            for k in range(2):
                here = c * tensors + 2 * s + k
                along = c * tensors + 2 * (1 - s) + k
                relay[0].append((here, along if k == c else (1 - c) * tensors + 2 * s + 1 - k))
                if k != c:
                    relay[1].append((here, along))

    def send_first(value):
        if ringed:
            return [lax.ppermute(value, plane, relay[0])]
        return [deliver(value, to_home[far]) for far in range(sides)]

    def send_second(value, got):
        if ringed:
            return [got[0], stays(value, lax.ppermute(got[0], plane, relay[1]))]
        return got

    def pair_up(a, b):
        return jnp.concatenate([a, b], axis=0)

    def adapter_of(index, far):
        return block_of(index, 2 * ((side + far) % sides) + high)

    def up_packs(index, ups):
        chosen = jnp.stack([adapter_of(index, far) for far in range(sides)])
        packs = list(pick(chosen, ups))
        for far in range(1, sides):
            send = [(i, (i + 2 * far) % tensors) for i in range(tensors)]
            packs[far] = lax.ppermute(packs[far], "tensor", send)
        return packs

    attn_own = jnp.concatenate([w_qkv[:, j] for j in range(3)] + [w_proj], axis=1)
    ups = (qkv_up, fc1_up, jnp.transpose(proj_down, (0, 2, 1)), jnp.transpose(fc2_down, (0, 2, 1)))
    flows = {}

    def cross_to(value, turn):
        return lax.ppermute(value, plane, cross[turn])

    if ringed:
        z, b, c, d = [attn_own], [], [], []
        ff_own = pair_up(w_fc1, w_fc2)
        got = fence(
            hop(attn_own, "shard"),
            cross_to(attn_own, 0),
            cross_to(attn_own, 1),
            deliver(block_of(tokens, tensor), to_owner),
            hop(ff_own, "shard"),
            ff_own,
            cotangent,
            adapter_index,
            down_in,
            out_up,
            *ups,
        )
        z.append(got[0])
        b.append(got[1])
        c.append(got[2])
        x_own = got[3]
        own = [got[5], got[4]]
        cotangent, adapter_index, down_in, out_up = got[6:10]
        ups = got[10:]
        got = fence(
            hop(z[1], "shard"),
            cross_to(z[1], 0),
            cross_to(z[1], 1),
            cross_to(b[0], 1),
            cross_to(own[0], 0),
            x_own,
            own[1],
            adapter_index,
            *ups,
        )
        z.append(got[0])
        b.append(got[1])
        c.append(got[2])
        d.append(got[3])
        aside = [got[4]]
        x_own, own[1], adapter_index = got[5:8]
        ups = got[8:]
        got = fence(
            hop(z[2], "shard"),
            cross_to(z[2], 0),
            cross_to(z[2], 1),
            cross_to(b[1], 1),
            swap(x_own),
            x_own,
            own[1],
            aside[0],
        )
        z.append(got[0])
        b.append(got[1])
        c.append(got[2])
        d.append(got[3])
        x_other, x_own, own[1], aside[0] = got[4:]
        packs = up_packs(adapter_index, ups)
        own.append(hop(own[1], "shard"))
        got = fence(cross_to(z[3], 0), cross_to(z[3], 1), cross_to(b[2], 1), cotangent, packs[1])
        b.append(got[0])
        c.append(got[1])
        d.append(got[2])
        cotangent, packs[1] = got[3:]
        last = cross_to(b[3], 1)
        own_over, aside_over = [], []

        step_of = np.repeat(np.arange(shards), 4)
        near_0 = np.tile([0, 0, 1, 1], shards)
        far_0 = np.tile([0, 1, 0, 1], shards)
        near = jnp.where(core == 0, near_0, far_0)
        across = jnp.where(core == 0, far_0, near_0)
        row = (shard - step_of) % shards * contexts + (context - near) % contexts
        attn_place = jnp.stack([row, across]).astype(jnp.int32)
        attn_moves = [(k, 0, depth) for k in range(4 * shards)]
        ff_moves = [(k, which * depth, depth, which) for which in range(2) for k in range(4 * shards)]
        ff_place = jnp.concatenate([attn_place, attn_place], axis=1)

        def start(*values):
            got = fence(*values, last, own[0], aside[0], own[2])
            d.append(got[-4])
            own[0], aside[0], own[2] = got[-3:]
            aside.append(hop(aside[0], "shard"))
            own_over.append(cross_to(own[0], 1))
            aside_over.append(cross_to(aside[0], 1))
            return got[:-4]

        def advance(stage, *values):
            count = len(values)
            if stage == 0:
                got = fence(*values, own[2], aside[1], own_over[0], aside_over[0], cotangent)
                own[2], aside[1], own_over[0], aside_over[0], late_cotangent = got[count:]
                own.append(hop(own[2], "shard"))
                own_over.append(cross_to(own[1], 1))
                flows["gy"] = deliver(block_of(late_cotangent, tensor), to_owner)
            elif stage == 1:
                got = fence(*values, own[3], own[2], aside[1])
                own[3], own[2], aside[1] = got[count:]
                aside.append(hop(aside[1], "shard"))
                aside_over.append(cross_to(aside[1], 1))
                own_over.append(cross_to(own[2], 1))
            elif stage == 2:
                got = fence(
                    *values, aside[2], own_over[1], own_over[2], aside_over[1], own[3], flows["gy"]
                )
                aside[2], own_over[1], own_over[2], aside_over[1], own[3], flows["gy"] = got[count:]
                aside.append(hop(aside[2], "shard"))
                own_over.append(cross_to(own[3], 1))
                aside_over.append(cross_to(aside[2], 1))
            else:
                got = fence(*values, aside[3], own_over[3], aside_over[2])
                aside[3], own_over[3], aside_over[2] = got[count:]
                aside_over.append(cross_to(aside[3], 1))
            return got[:count]

    else:

        def gather_plain(value):
            whole = lax.all_gather(value, ("shard", "context"), axis=0, tiled=True)
            return around(whole, "tensor")

        attn_parts = gather_plain(attn_own)
        fc1_parts = gather_plain(w_fc1)
        fc2_parts = gather_plain(w_fc2)
        packs = up_packs(adapter_index, ups)
        x_own = deliver(block_of(tokens, tensor), to_owner)
        x_other = swap(x_own)
        flows["gy"] = deliver(block_of(cotangent, tensor), to_owner)
        attn_moves = [(k, 0, model) for k in range(sides)]
        attn_place = jnp.asarray([[0] * sides, list(range(sides))], jnp.int32)
        ff_moves = [(k, 0, model, k // sides) for k in range(2 * sides)]
        ff_place = jnp.concatenate([attn_place, attn_place], axis=1)

        def start(*values):
            return values

        def advance(stage, *values):
            return values

    mine = adapter_of(adapter_index, 0)
    down = block_of(down_in, mine)
    down_t = jnp.transpose(down, (0, 2, 1)).reshape(4 * rank, model)
    out_t = block_of(out_up, mine)

    x_all = pair_up(x_own, x_other).astype(F32)
    normed, unit_one, inverse_one = normalize(x_all, ln1_gain, ln1_bias)
    n1 = normed.astype(BF16)
    u = dot_nt(down_t[: 3 * rank], n1).astype(BF16)
    qkv_lift, fc1_lift, proj_t, fc2_t = lifts(packs, width, hidden)
    n1, u, qkv_lift = start(n1, u, qkv_lift)
    if ringed:
        attn_parts = [part for i in range(shards) for part in (z[i], b[i], c[i], d[i])]
    w_in, w_out, qkv = project(n1, u, qkv_lift, attn_parts, attn_moves, attn_place, width)
    (qkv,) = advance(0, qkv)

    steps = [[h * half + i for i in range(half)] for h in range(2)]
    per_side = width // PAIR
    pairs = per_side * sides
    near, group_count = (per_side, sides) if half == 1 else (1, pairs // half)

    def to_heads(array, thirds_each):
        if half == 1:
            return array
        cells = array.reshape(array.shape[0], sides, thirds_each, per_side, PAIR)
        cells = jnp.transpose(cells, (0, 1, 3, 2, 4)).reshape(array.shape[0], pairs, -1)
        moved = lax.all_to_all(cells, "context", 1, 0, axis_index_groups=steps, tiled=True)
        return moved.reshape(moved.shape[0], -1)

    def to_rows(array, thirds_each):
        if half == 1:
            return array
        cells = array.reshape(array.shape[0], pairs // half, -1)
        moved = lax.all_to_all(cells, "context", 0, 1, axis_index_groups=steps, tiled=True)
        moved = moved.reshape(moved.shape[0], sides, per_side, thirds_each, PAIR)
        return jnp.transpose(moved, (0, 1, 3, 2, 4)).reshape(moved.shape[0], -1)

    qkv_heads = to_heads(qkv, 3)
    o_heads = None
    logs = []
    for group in range(group_count):
        o_heads, lse = attend(qkv_heads, group, near, o_heads)
        logs.append(lse)
        if group == 0:
            o_heads, qkv_heads = advance(1, o_heads, qkv_heads)
    (o_heads,) = advance(2, o_heads)
    gy_own = flows["gy"]
    o = to_rows(o_heads, 1)
    attn_far = dot_nt(o[rows:], w_out)
    c_part = dot_nt(proj_t, o)
    attn_sum = swap(attn_far) + dot_nt(o[:rows], w_out)
    c_own = (c_part[:, :rows] + swap(c_part[:, rows:])).astype(BF16)
    h = x_all[:rows] + layer_scale[0] * (attn_sum + dot_tn(c_own, out_t[0]))
    normed, unit_two, inverse_two = normalize(h, ln2_gain, ln2_bias)
    n2_own = normed.astype(BF16)
    gb_own = (gy_own.astype(F32) * layer_scale[1]).astype(BF16)
    gb = pair_up(gb_own, swap(gb_own))
    n2_own, gb = advance(3, n2_own, gb)
    n2_far = swap(n2_own)
    if ringed:
        ff_parts = [
            part
            for i in range(shards)
            for part in (own[i], aside[i], own_over[i], aside_over[i])
        ]
    else:
        ff_parts = fc1_parts + fc2_parts
    branch_own, branch_far, gn2_own, gn2_far, rank_own, rank_far, g_fc1, g_fc2 = mlp(
        n2_own, n2_far, gb, down_t[3 * rank :], out_t[1], ff_parts, ff_moves, ff_place, fc1_lift, fc2_t
    )
    ranks = (rank_own + swap(rank_far)).astype(BF16)
    ranks, gn2_far, branch_far = fence(ranks, gn2_far, branch_far)
    m_own, gf_own = ranks[:rank], ranks[rank:]
    branch = branch_own + swap(branch_far).astype(F32) + dot_tn(m_own, out_t[1])
    result_own = (h + layer_scale[1] * branch).astype(BF16)
    gn2 = gn2_own + swap(gn2_far) + dot_tn(gf_own, down_t[3 * rank :])
    g_out1 = dot(m_own, gb[:rows])
    g_down3 = dot(gf_own, n2_own)

    cut = model // 2
    one = jnp.where(context % half == 0, mine, 0)
    mark = jnp.full((rank, 128), one).astype(BF16)

    def halves(shared):
        shared = jnp.stack(shared)
        away = lax.dynamic_slice_in_dim(shared, (1 - core) * cut, cut, 2)
        keep = lax.dynamic_slice_in_dim(shared, core * cut, cut, 2)
        both = keep + swap(away)
        return [both[j] for j in range(len(both))]

    def to_sides(slices, shared):
        packed = []
        for far in range(sides):
            pack = jnp.concatenate([part.astype(BF16) for part in slices[far] + shared] + [mark], axis=1)
            if far:
                send = [(i, (i - 2 * far) % tensors) for i in range(tensors)]
                pack = lax.ppermute(pack, "tensor", send)
            packed.append(pack)
        return jnp.stack(packed)

    opposite = [(i, (i + half) % contexts) for i in range(contexts)]

    def merge(block):
        if half == 1:
            return block
        total = lax.psum(block.astype(F32), "context", axis_index_groups=steps)
        return total.astype(BF16)

    def over(block):
        return lax.ppermute(block, "context", opposite)

    def columns(array, far, size):
        return array[:, far * size : (far + 1) * size]

    early = to_sides(
        [[columns(g_fc1, far, hidden), columns(g_fc2, far, hidden)] for far in range(sides)],
        halves([g_down3, g_out1]),
    )
    gh = gy_own.astype(F32) + norm_back(gn2, unit_two, inverse_two, ln2_gain)
    gattn_own = (layer_scale[0] * gh).astype(BF16)
    gattn_far, early = fence(swap(gattn_own), early)
    gattn = pair_up(gattn_own, gattn_far)
    early_line = [merge(early)]
    early_line.append(hop(early_line[0], "shard"))
    early_over = [over(early_line[0])]
    g_out0 = dot(c_own, gattn_own)
    gc = dot_nt(out_t[0], gattn).astype(BF16)
    g_proj = dot(gc, o)
    mid = to_sides([[columns(g_proj, far, width)] for far in range(sides)], halves([g_out0]))
    go = (dot(gattn, w_out) + dot_tn(gc, proj_t)).astype(BF16)
    early_line[1], early_over[0], mid, go, result_own = fence(
        early_line[1], early_over[0], mid, go, result_own
    )
    early_line.append(hop(early_line[1], "shard"))
    early_over.append(over(early_line[1]))
    mid = merge(mid)
    mid_over = over(mid)
    sent = send_first(result_own)
    go_heads = to_heads(go, 1)
    g_heads = None
    for group in range(group_count):
        g_heads = attend_back(qkv_heads, go_heads, o_heads, logs[group], group, near, g_heads)
        if group == 0:
            g_heads, mid_over, early_line[2], *sent = fence(
                g_heads, mid_over, early_line[2], *sent
            )
            early_over.append(over(early_line[2]))
            for _ in range(3, shards):
                early_line.append(hop(early_line[-1], "shard"))
            mid_line = [pair_up(mid, mid_over)]
            mid_line.append(hop(mid_line[0], "shard"))
            sent = send_second(result_own, sent)
    g_heads, mid_line[1], early_over[1], early_over[2], *early_line[3:] = fence(
        g_heads, mid_line[1], early_over[1], early_over[2], *early_line[3:]
    )
    early_over.extend([over(block) for block in early_line[3:]])
    mid_line.append(hop(mid_line[1], "shard"))
    g = to_rows(g_heads, 3)

    gu_part = dot_nt(qkv_lift, g)
    gu_own = (gu_part[:, :rows] + swap(gu_part[:, rows:])).astype(BF16)
    gn1_far = swap(dot_nt(g[rows:], w_in))
    g_up = dot(u, g)
    gn1 = dot_nt(g[:rows], w_in) + gn1_far + dot_tn(gu_own, down_t[: 3 * rank])
    g_down = dot(gu_own, n1[:rows])
    late_slices = [
        [
            g_up[j * rank : (j + 1) * rank, (far * 3 + j) * width : (far * 3 + j + 1) * width]
            for j in range(3)
        ]
        for far in range(sides)
    ]
    late = to_sides(late_slices, halves([g_down[j * rank : (j + 1) * rank] for j in range(3)]))
    input_own = gh + norm_back(gn1, unit_one[:rows], inverse_one[:rows], ln1_gain)
    input_own = input_own.astype(BF16)
    late_line = [merge(late)]
    late_line.append(hop(late_line[0], "shard"))
    late_over = [over(late_line[0])]
    last_over = early_over[3:]
    late_line[1], late_over[0], input_own, mid_line[2], *got = fence(
        late_line[1], late_over[0], input_own, mid_line[2], *last_over, *sent
    )
    early_over[3:], sent = got[: len(last_over)], got[len(last_over) :]

    order = np.tile(np.arange(sides), 2)
    flip = np.repeat([0, 1], sides)
    far = jnp.where((core ^ flip) == context, 1 - order, order) if ringed else order
    where = (2 * ((side - far) % sides) + (core ^ flip)).astype(jnp.int32)
    late_line.append(hop(late_line[1], "shard"))
    input_sent = send_first(input_own)
    for _ in range(3, shards):
        mid_line.append(hop(mid_line[-1], "shard"))
    sent = list(sent) + [swap(part) for part in sent]
    fc1_grad, fc2_grad, early_half = totals(
        early_line + early_over, (hidden, hidden, 2 * cut), adapters
    )
    late_line[1], late_line[2], early_half, *got = fence(
        late_line[1], late_line[2], early_half, *sent, *mid_line
    )
    sent, mid_line = got[: 2 * sides], got[2 * sides :]
    for _ in range(3, shards):
        late_line.append(hop(late_line[-1], "shard"))
    late_over.append(over(late_line[1]))
    early_twin = swap(early_half)
    result = settle(sent, where, 0, 1, BF16, images)
    proj_grad, mid_half = totals(mid_line, (width, cut), adapters)
    late_line[-1], late_over[1], early_half, early_twin, mid_half, result, *input_sent = fence(
        late_line[-1], late_over[1], early_half, early_twin, mid_half, result, *input_sent
    )
    late_over.extend([over(block) for block in late_line[2:]])
    first_twin = swap(input_sent[0])
    input_sent = send_second(input_own, input_sent)
    mid_twin = swap(mid_half)
    input_grad = settle([input_sent[0], first_twin], where, 0, sides, F32, images)
    out_grad = spread(
        core, [mid_half, mid_twin, early_half, early_twin], ((0, 0), (1, 1)), cut
    )
    late_line[0], input_grad, out_grad, *late_over = fence(
        late_line[0], input_grad, out_grad, *late_over
    )
    qkv_grad, late_half = totals(late_line + late_over, (3 * width, 3 * cut), adapters, 3)
    late_half, qkv_grad, *input_sent = fence(late_half, qkv_grad, *input_sent)
    late_twin = swap(late_half)
    last_twins = [swap(part) for part in input_sent[1:]]
    input_grad = settle(input_sent[1:] + last_twins, where, 1, sides, F32, images, input_grad)
    down_grad = spread(
        core,
        [late_half, late_twin, early_half, early_twin],
        ((0, 0), (0, 1), (0, 2), (1, 0)),
        cut,
    )
    return (
        result,
        input_grad,
        jnp.transpose(down_grad, (0, 1, 3, 2)),
        qkv_grad,
        fc1_grad,
        jnp.transpose(proj_grad, (0, 2, 1)),
        jnp.transpose(fc2_grad, (0, 2, 1)),
        out_grad,
    )


def solution(mesh):
    sizes = (mesh.shape["shard"], mesh.shape["context"], mesh.shape["tensor"])
    placed = (
        P("shard", "context", None),
        P("shard", "context", None),
        P("shard"),
        P(),
        P(),
        P(),
        P(),
        P(),
        P(("shard", "context"), None, "tensor"),
        P(("shard", "context"), "tensor"),
        P(("shard", "context"), "tensor"),
        P(("shard", "context"), "tensor"),
        P(),
        P(None, None, None, "tensor"),
        P(None, None, "tensor"),
        P(None, "tensor", None),
        P(None, "tensor", None),
        P(),
    )
    return jax.shard_map(
        functools.partial(per_device, sizes),
        mesh=mesh,
        in_specs=placed,
        out_specs=(
            P("shard", "context", None),
            P("shard", "context", None),
            P(),
            P(None, None, None, "tensor"),
            P(None, None, "tensor"),
            P(None, "tensor", None),
            P(None, "tensor", None),
            P(),
        ),
        check_vma=False,
    )
```

```python
import functools
import math

import jax
import jax.numpy as jnp
import numpy as np
from jax import lax
from jax.experimental import pallas as pl
from jax.experimental.pallas import tpu as pltpu
from jax.sharding import PartitionSpec as P

HEAD_DIM = 64
PAIR = 2 * HEAD_DIM
EPS = 1e-06
LOG2E = math.log2(math.e)
SCORE = 1.0 / math.sqrt(HEAD_DIM)
F32 = jnp.float32
BF16 = jnp.bfloat16
NT = (((1,), (1,)), ((), ()))
TN = (((0,), (0,)), ((), ()))
BRIEF = pl.CostEstimate(flops=1000, bytes_accessed=1000, transcendentals=0)


def dot(a, b):
    return jnp.dot(a, b, preferred_element_type=F32)


def dot_nt(a, b):
    return lax.dot_general(a, b, NT, preferred_element_type=F32)


def dot_tn(a, b):
    return lax.dot_general(a, b, TN, preferred_element_type=F32)


def head_masks(rows):
    lane = lax.broadcasted_iota(jnp.int32, (rows, PAIR), 1)
    return lane < HEAD_DIM


def attend_kernel(block, q_ref, k_ref, v_ref, _, o_ref, lse_ref):
    rows = q_ref.shape[0]
    keys = k_ref[...]
    values = jnp.concatenate([v_ref[...], jnp.ones((rows, PAIR), BF16)], axis=1)
    first = head_masks(block)

    def step(i, carry):
        at = pl.ds(pl.multiple_of(i * block, block), block)
        q = q_ref[at, :]
        outs = []
        logs = []
        for head in range(2):
            mine = first if head == 0 else jnp.logical_not(first)
            s = dot_nt(jnp.where(mine, q, jnp.zeros_like(q)), keys)
            peak = jnp.max(s, axis=1, keepdims=True)
            e = jnp.exp2((s - peak) * (SCORE * LOG2E))
            acc = dot(e.astype(BF16), values)
            total = acc[:, PAIR:]
            outs.append(acc[:, :PAIR] / total)
            logs.append(peak * (SCORE * LOG2E) + jnp.log2(total))
        o_ref[at, :] = jnp.where(first, outs[0], outs[1]).astype(BF16)
        lane = lax.broadcasted_iota(jnp.int32, (block, PAIR), 1)
        both = jnp.where(lane == 0, logs[0], logs[1])
        lse_ref[0, :, at] = jnp.transpose(both)[:8]
        return carry

    lax.fori_loop(0, rows // block, step, 0)


def thirds(rows, group, near):
    return [
        pl.BlockSpec((rows, PAIR), lambda p, j=j: (0, (group * 3 + j) * near + p))
        for j in range(3)
    ]


def attend(qkv, group, near, o):
    rows, width = qkv.shape
    pairs = width // (3 * PAIR)
    block = min(256, rows)
    anywhere = pl.BlockSpec(memory_space=pl.ANY)
    operands = [qkv, qkv, qkv, qkv if o is None else o]
    return pl.pallas_call(
        functools.partial(attend_kernel, block),
        grid=(near,),
        in_specs=thirds(rows, group, near) + [anywhere],
        out_specs=[
            pl.BlockSpec((rows, PAIR), lambda p: (0, group * near + p)),
            pl.BlockSpec((1, 8, rows), lambda p: (p, 0, 0)),
        ],
        out_shape=[
            jax.ShapeDtypeStruct((rows, pairs * PAIR), BF16),
            jax.ShapeDtypeStruct((near, 8, rows), F32),
        ],
        input_output_aliases={} if o is None else {3: 0},
        cost_estimate=BRIEF,
        name="attend",
    )(*operands)


def attend_back_kernel(
    block, near, q_ref, k_ref, v_ref, go_ref, o_ref, lse_ref, _, g_ref, gq_ref, d_ref
):
    rows = q_ref.shape[0]
    pair = pl.program_id(0)
    lanes = [pl.ds(pl.multiple_of((j * near + pair) * PAIR, PAIR), PAIR) for j in range(3)]
    first = head_masks(block)
    prod = o_ref[...].astype(F32) * go_ref[...].astype(F32)
    lane8 = lax.broadcasted_iota(jnp.int32, (8, PAIR), 1) // HEAD_DIM
    row8 = lax.broadcasted_iota(jnp.int32, (8, PAIR), 0)
    d_ref[...] = lax.dot_general(
        (lane8 == row8).astype(F32),
        prod,
        NT,
        preferred_element_type=F32,
        precision=lax.Precision.HIGHEST,
    )
    gq_ref[...] = jnp.zeros_like(gq_ref)

    def step(i, carry):
        at = pl.ds(pl.multiple_of(i * block, block), block)
        k = k_ref[at, :]
        v = v_ref[at, :]
        q = q_ref[...]
        go = go_ref[...]
        gks = []
        gvs = []
        gq = None
        for head in range(2):
            mine = first if head == 0 else jnp.logical_not(first)
            k_own = jnp.where(mine, k, jnp.zeros_like(k))
            v_own = jnp.where(mine, v, jnp.zeros_like(v))
            s = dot_nt(k_own, q)
            gp = dot_nt(v_own, go)
            p = jnp.exp2(s * (SCORE * LOG2E) - lse_ref[0, head : head + 1, :])
            gs = (p * (gp - d_ref[head : head + 1, :])).astype(BF16)
            gks.append(dot(gs, q))
            gvs.append(dot(p.astype(BF16), go))
            part = dot(jnp.transpose(k_own), gs)
            gq = part if gq is None else gq + part
        gq_ref[...] += gq
        g_ref[at, lanes[1]] = (jnp.where(first, gks[0], gks[1]) * SCORE).astype(BF16)
        g_ref[at, lanes[2]] = jnp.where(first, gvs[0], gvs[1]).astype(BF16)
        return carry

    lax.fori_loop(0, rows // block, step, 0)
    g_ref[:, lanes[0]] = (jnp.transpose(gq_ref[...]) * SCORE).astype(BF16)


def attend_back(qkv, go, o, lse, group, near, g):
    rows, width = qkv.shape
    block = min(256, rows)
    mine = pl.BlockSpec((rows, PAIR), lambda p: (0, group * near + p))
    anywhere = pl.BlockSpec(memory_space=pl.ANY)
    operands = [qkv, qkv, qkv, go, o, lse, qkv if g is None else g]
    return pl.pallas_call(
        functools.partial(attend_back_kernel, block, near),
        grid=(near,),
        in_specs=thirds(rows, group, near)
        + [mine, mine, pl.BlockSpec((1, 8, rows), lambda p: (p, 0, 0)), anywhere],
        out_specs=pl.BlockSpec((rows, 3 * near * PAIR), lambda p: (0, group)),
        out_shape=jax.ShapeDtypeStruct((rows, width), BF16),
        scratch_shapes=[pltpu.VMEM((PAIR, rows), F32), pltpu.VMEM((8, rows), F32)],
        input_output_aliases={} if g is None else {6: 0},
        cost_estimate=BRIEF,
        name="attend_back",
    )(*operands)


def mlp_kernel(
    block,
    own,
    moves,
    pieces,
    place_ref,
    gb_ref,
    down_ref,
    up_ref,
    u1_ref,
    d2_ref,
    n_own,
    n_far,
    *refs,
):
    parts = refs[:pieces]
    outs, scratch = refs[pieces : pieces + 8], refs[pieces + 8 :]
    branch_own, branch_far, gn_own, gn_far = outs[:4]
    rank_own, rank_far, gf1_out, gf2_out = outs[4:]
    w1_all, w2_all, n_ref, f_ref, gm_ref, branch_ref, gn_ref = scratch[:7]
    rank_ref, gf1_ref, gf2_ref, cast_ref, sems, row_sems, out_sems = scratch[7:]
    rank = f_ref.shape[0]
    rows = n_ref.shape[0]
    chunk = u1_ref.shape[1]
    at_chunk = pl.ds(pl.multiple_of(pl.program_id(0) * chunk, chunk), chunk)

    @pl.when(pl.program_id(0) == 0)
    def _():
        rows_in = [
            pltpu.make_async_copy(n_own, n_ref.at[:own, :], row_sems.at[0]),
            pltpu.make_async_copy(n_far, n_ref.at[own:, :], row_sems.at[1]),
        ]
        for copy in rows_in:
            copy.start()
        for split in range(parts[0].shape[1] // chunk):
            for k, (part, start, depth, which) in enumerate(moves):
                number = place_ref[1, k] * (parts[part].shape[1] // chunk) + split
                down = pl.ds(pl.multiple_of(place_ref[0, k] * depth, depth), depth)
                along = pl.ds(pl.multiple_of(number * chunk, chunk), chunk)
                pltpu.make_async_copy(
                    parts[part].at[pl.ds(start, depth), pl.ds(split * chunk, chunk)],
                    (w1_all, w2_all)[which].at[down, along],
                    sems.at[which, number],
                ).start()
        branch_ref[...] = jnp.zeros_like(branch_ref)
        gn_ref[...] = jnp.zeros_like(gn_ref)
        rank_ref[...] = jnp.zeros_like(rank_ref)
        gm_ref[...] = dot_nt(up_ref[...], gb_ref[...]).astype(BF16)
        for copy in rows_in:
            copy.wait()
        f_ref[...] = dot_nt(down_ref[...], n_ref[...]).astype(BF16)

    final = pl.program_id(0) == pl.num_programs(0) - 1

    def leave(i, at, to, home):
        branch = branch_ref.at[at, :] if home else cast_ref.at[to, :]
        target = branch_own if home else branch_far
        gn_target = gn_own if home else gn_far
        return [
            pltpu.make_async_copy(branch, target.at[to, :], out_sems.at[0, i]),
            pltpu.make_async_copy(gn_ref.at[at, :], gn_target.at[to, :], out_sems.at[1, i]),
        ]

    for which, target in enumerate((w1_all, w2_all)):
        area = target.at[:, at_chunk]
        pltpu.make_async_copy(area, area, sems.at[which, pl.program_id(0)]).wait()
    gf1_ref[...] = jnp.zeros_like(gf1_ref)
    gf2_ref[...] = jnp.zeros_like(gf2_ref)

    def step(i, carry):
        at = pl.ds(pl.multiple_of(i * block, block), block)
        w1 = w1_all[:, at_chunk]
        w2 = w2_all[:, at_chunk]
        u1 = u1_ref[...]
        d2 = d2_ref[...]
        z = dot(n_ref[at, :], w1) + dot_tn(f_ref[:, at], u1)
        cdf = 0.5 * (1.0 + lax.erf(z * (1.0 / math.sqrt(2.0))))
        a = (z * cdf).astype(BF16)
        slope = cdf + z * (jnp.exp2(z * z * (-0.5 * LOG2E)) * (1.0 / math.sqrt(2.0 * math.pi)))
        ga = dot(gb_ref[at, :], w2) + dot_tn(gm_ref[:, at], d2)
        gz = (ga * slope).astype(BF16)
        branch_ref[at, :] += dot_nt(a, w2)
        rank_ref[:rank, at] += dot_nt(d2, a)
        gn_ref[at, :] += dot_nt(gz, w1)
        rank_ref[rank:, at] += dot_nt(u1, gz)
        gf1_ref[...] += dot(f_ref[:, at], gz)
        gf2_ref[...] += dot(gm_ref[:, at], a)

        @pl.when(jnp.logical_and(final, i < own // block))
        def _():
            for copy in leave(i, at, at, True):
                copy.start()

        @pl.when(jnp.logical_and(final, i >= own // block))
        def _():
            to = pl.ds(pl.multiple_of(i * block - own, block), block)
            cast_ref[to, :] = branch_ref[at, :].astype(BF16)
            for copy in leave(i, at, to, False):
                copy.start()

        return carry

    lax.fori_loop(0, rows // block, step, 0)
    gf1_out[...] = gf1_ref[...].astype(BF16)
    gf2_out[...] = gf2_ref[...].astype(BF16)

    @pl.when(pl.program_id(0) == pl.num_programs(0) - 1)
    def _():
        rank_own[...] = rank_ref[:, :own]
        rank_far[...] = rank_ref[:, own:]
        for i in range(rows // block):
            home = i < own // block
            at = pl.ds(i * block, block)
            to = at if home else pl.ds(i * block - own, block)
            for copy in leave(i, at, to, home):
                copy.wait()


def mlp(n_own, n_far, gb, down, up, parts, moves, place, u1, d2):
    own, model = n_own.shape
    rows = gb.shape[0]
    hidden = u1.shape[1]
    rank = down.shape[0]
    chunk = min(1024, hidden)
    block = min(256, own)
    whole = lambda shape: pl.BlockSpec(shape, lambda j, place: (0, 0))
    part = lambda depth: pl.BlockSpec((depth, chunk), lambda j, place: (0, j))
    far = rows - own
    shapes = [
        ((own, model), F32),
        ((far, model), BF16),
        ((own, model), F32),
        ((far, model), F32),
        ((2 * rank, own), F32),
        ((2 * rank, far), F32),
    ]
    return pl.pallas_call(
        functools.partial(mlp_kernel, block, own, moves, len(parts)),
        grid_spec=pltpu.PrefetchScalarGridSpec(
            num_scalar_prefetch=1,
            grid=(hidden // chunk,),
            in_specs=[
                whole((rows, model)),
                whole((rank, model)),
                whole((rank, model)),
                part(rank),
                part(rank),
            ]
            + [pl.BlockSpec(memory_space=pl.ANY)] * (2 + len(parts)),
            out_specs=[pl.BlockSpec(memory_space=pl.ANY)] * 4
            + [whole(shape) for shape, _ in shapes[4:]]
            + [part(rank), part(rank)],
            scratch_shapes=[
                pltpu.VMEM((model, hidden), BF16),
                pltpu.VMEM((model, hidden), BF16),
                pltpu.VMEM((rows, model), BF16),
                pltpu.VMEM((rank, rows), BF16),
                pltpu.VMEM((rank, rows), BF16),
                pltpu.VMEM((rows, model), F32),
                pltpu.VMEM((rows, model), F32),
                pltpu.VMEM((2 * rank, rows), F32),
                pltpu.VMEM((rank, chunk), F32),
                pltpu.VMEM((rank, chunk), F32),
                pltpu.VMEM((far, model), BF16),
                pltpu.SemaphoreType.DMA((2, hidden // chunk)),
                pltpu.SemaphoreType.DMA((2,)),
                pltpu.SemaphoreType.DMA((2, rows // block)),
            ],
        ),
        out_shape=[jax.ShapeDtypeStruct(*shape) for shape in shapes]
        + [jax.ShapeDtypeStruct((rank, hidden), BF16)] * 2,
        cost_estimate=BRIEF,
        name="mlp",
    )(place, gb, down, up, u1, d2, n_own, n_far, *parts)


def project_kernel(moves, pieces, place_ref, n_ref, u_ref, lift_ref, *refs):
    parts, (w_in, w_out, qkv_ref, in_all, out_all, sems, back) = refs[:pieces], refs[pieces:]

    def copies():
        column = 0
        for j, target in enumerate((in_all, out_all)):
            width = target.shape[1] // 2
            for k, (part, start, depth) in enumerate(moves):
                down = pl.ds(pl.multiple_of(place_ref[0, k] * depth, depth), depth)
                along = pl.ds(pl.multiple_of(place_ref[1, k] * width, width), width)
                yield pltpu.make_async_copy(
                    parts[part].at[pl.ds(start, depth), pl.ds(column, width)],
                    target.at[down, along],
                    sems.at[j, k],
                )
            column += width

    backs = [
        pltpu.make_async_copy(in_all, w_in, back.at[0]),
        pltpu.make_async_copy(out_all, w_out, back.at[1]),
    ]

    @pl.when(pl.program_id(0) == 0)
    def _():
        pending = list(copies())
        for copy in pending:
            copy.start()
        for copy in pending:
            copy.wait()
        for copy in backs:
            copy.start()

    sums = dot(n_ref[...], in_all[...]) + dot_tn(u_ref[...], lift_ref[...])
    qkv_ref[...] = sums.astype(BF16)

    @pl.when(pl.program_id(0) == pl.num_programs(0) - 1)
    def _():
        for copy in backs:
            copy.wait()


def project(n, u, lift, parts, moves, place, width):
    rows, model = n.shape
    block = min(256, rows)
    anywhere = pl.BlockSpec(memory_space=pl.ANY)
    shapes = [(model, 6 * width), (model, 2 * width), (rows, 6 * width)]
    return pl.pallas_call(
        functools.partial(project_kernel, moves, len(parts)),
        grid_spec=pltpu.PrefetchScalarGridSpec(
            num_scalar_prefetch=1,
            grid=(rows // block,),
            in_specs=[
                pl.BlockSpec((block, model), lambda i, place: (i, 0)),
                pl.BlockSpec((u.shape[0], block), lambda i, place: (0, i)),
                pl.BlockSpec(lift.shape, lambda i, place: (0, 0)),
            ]
            + [anywhere] * len(parts),
            out_specs=[
                anywhere,
                anywhere,
                pl.BlockSpec((block, 6 * width), lambda i, place: (i, 0)),
            ],
            scratch_shapes=[
                pltpu.VMEM((model, 6 * width), BF16),
                pltpu.VMEM((model, 2 * width), BF16),
                pltpu.SemaphoreType.DMA((2, len(moves))),
                pltpu.SemaphoreType.DMA((2,)),
            ],
        ),
        out_shape=[jax.ShapeDtypeStruct(shape, BF16) for shape in shapes],
        cost_estimate=BRIEF,
        name="project",
    )(place, n, u, lift, *parts)


def pick_kernel(sides, _, *refs):
    sources, outs = refs[: 4 * sides], refs[4 * sides :]
    for far, out in enumerate(outs):
        up, fc1, proj, fc2 = sources[4 * far : 4 * far + 4]
        column = 0
        for piece in [up[0, 0], up[0, 1], up[0, 2], fc1[0], proj[0], fc2[0]]:
            out[:, column : column + piece.shape[1]] = piece
            column += piece.shape[1]


def pick(chosen, ups):
    rank = ups[1].shape[1]
    wide = sum(up.shape[-1] for up in ups) + 2 * ups[0].shape[-1]
    sides = chosen.shape[0]
    specs = [
        pl.BlockSpec(
            (1,) + up.shape[1:],
            lambda i, e, far=far, n=up.ndim: (e[far],) + (0,) * (n - 1),
        )
        for far in range(sides)
        for up in ups
    ]
    return pl.pallas_call(
        functools.partial(pick_kernel, sides),
        grid_spec=pltpu.PrefetchScalarGridSpec(
            num_scalar_prefetch=1,
            grid=(1,),
            in_specs=specs,
            out_specs=[pl.BlockSpec((rank, wide), lambda i, e: (0, 0))] * sides,
        ),
        out_shape=[jax.ShapeDtypeStruct((rank, wide), BF16)] * sides,
        name="pick",
    )(chosen, *(list(ups) * sides))


def lifts_kernel(sizes, *refs):
    packs, (qkv_ref, fc1_ref, proj_ref, fc2_ref) = refs[:-4], refs[-4:]
    rank = fc1_ref.shape[0]
    width, hidden = sizes
    qkv_ref[...] = jnp.zeros_like(qkv_ref)
    for far, pack in enumerate(packs):
        for j in range(3):
            column = (3 * far + j) * width
            qkv_ref[j * rank : (j + 1) * rank, column : column + width] = pack[
                :, j * width : (j + 1) * width
            ]
        start = 3 * width
        for ref, size in ((fc1_ref, hidden), (proj_ref, width), (fc2_ref, hidden)):
            ref[:, far * size : (far + 1) * size] = pack[:, start : start + size]
            start += size


def lifts(packs, width, hidden):
    rank = packs[0].shape[0]
    sides = len(packs)
    shapes = [(3 * rank, 3 * width), (rank, hidden), (rank, width), (rank, hidden)]
    return pl.pallas_call(
        functools.partial(lifts_kernel, (width, hidden)),
        out_shape=[jax.ShapeDtypeStruct((r, sides * c), BF16) for r, c in shapes],
        name="lifts",
    )(*packs)


def totals_kernel(blocks, widths, *refs):
    sources, outs = refs[:blocks], refs[blocks:]
    for out in outs:
        out[...] = jnp.zeros_like(out)
    total = sum(widths)
    for source in sources:
        for k in range(source.shape[0]):
            owner = jnp.max(source[k, :, total:].astype(F32)).astype(jnp.int32)
            column = 0
            for out, width in zip(outs, widths):
                split = out.shape[1] if len(out.shape) == 4 else 1
                for j in range(split):
                    part = source[k, :, column : column + width // split].astype(F32)
                    if split > 1:
                        out[owner, j] += part
                    else:
                        out[owner] += part
                    column += width // split


def totals(blocks, widths, adapters, split=1):
    rank = blocks[0].shape[1]
    return pl.pallas_call(
        functools.partial(totals_kernel, len(blocks), widths),
        out_shape=[
            jax.ShapeDtypeStruct(
                (adapters, split, rank, width // split)
                if split > 1 and k == 0
                else (adapters, rank, width),
                F32,
            )
            for k, width in enumerate(widths)
        ],
        name="totals",
    )(*blocks)


def spread_kernel(order, core_ref, *refs):
    halves, target = refs[:-1], refs[-1]
    cut = target.shape[3] // 2
    first = core_ref[0] == 0
    for j, (pair, k) in enumerate(order):
        own = halves[2 * pair][:, :, k * cut : (k + 1) * cut]
        other = halves[2 * pair + 1][:, :, k * cut : (k + 1) * cut]
        target[:, j, :, :cut] = jnp.where(first, own, other)
        target[:, j, :, cut:] = jnp.where(first, other, own)


def spread(core, halves, order, cut):
    adapters, rank, _ = halves[0].shape
    return pl.pallas_call(
        functools.partial(spread_kernel, order),
        in_specs=[pl.BlockSpec(memory_space=pltpu.SMEM)]
        + [pl.BlockSpec(memory_space=pltpu.VMEM)] * len(halves),
        out_shape=jax.ShapeDtypeStruct((adapters, len(order), rank, 2 * cut), F32),
        name="spread",
    )(jnp.reshape(core, (1,)), *halves)


def settle_kernel(count, where_ref, *refs):
    parts, out = refs[:count], refs[-1]
    for k, part in enumerate(parts):

        @pl.when(pl.program_id(0) == k)
        def _():
            out[0] = part[...].astype(out.dtype)


def settle(parts, where, first, stride, kind, images, base=None):
    rows, model = parts[0].shape
    extra = [] if base is None else [base]
    return pl.pallas_call(
        functools.partial(settle_kernel, len(parts)),
        grid_spec=pltpu.PrefetchScalarGridSpec(
            num_scalar_prefetch=1,
            grid=(len(parts),),
            in_specs=[pl.BlockSpec((rows, model), lambda k, where: (0, 0))] * len(parts)
            + [pl.BlockSpec(memory_space=pl.ANY)] * len(extra),
            out_specs=pl.BlockSpec((1, rows, model), lambda k, where: (where[first + stride * k], 0, 0)),
        ),
        out_shape=jax.ShapeDtypeStruct((images, rows, model), kind),
        input_output_aliases={1 + len(parts): 0} if extra else {},
        name="settle",
    )(where, *parts, *extra)


def normalize(values, gain, shift):
    centre = values - jnp.mean(values, axis=-1, keepdims=True)
    inverse = lax.rsqrt(jnp.mean(centre * centre, axis=-1, keepdims=True) + EPS)
    unit = centre * inverse
    return unit * gain + shift, unit, inverse


def norm_back(grad, unit, inverse, gain):
    scaled = grad * gain
    centred = scaled - jnp.mean(scaled, axis=-1, keepdims=True)
    return inverse * (centred - unit * jnp.mean(scaled * unit, axis=-1, keepdims=True))


def per_device(
    sizes,
    tokens,
    cotangent,
    adapter_index,
    ln1_gain,
    ln1_bias,
    ln2_gain,
    ln2_bias,
    layer_scale,
    w_qkv,
    w_proj,
    w_fc1,
    w_fc2,
    down_in,
    qkv_up,
    fc1_up,
    proj_down,
    fc2_down,
    out_up,
):
    shards, contexts, tensors = sizes
    half = contexts // 2
    sides = tensors // 2
    images, rows, model = tokens.shape
    rank = down_in.shape[-1]
    depth = w_fc1.shape[0]
    width = w_proj.shape[1]
    hidden = w_fc1.shape[1]
    pairs = width // PAIR
    adapters = down_in.shape[0]
    shard = lax.axis_index("shard")
    context = lax.axis_index("context")
    tensor = lax.axis_index("tensor")
    side, core = tensor // 2, tensor % 2
    high = context // half

    ring = {
        "shard": [(i, (i + 1) % shards) for i in range(shards)],
        "context": [(i, (i + 1) % contexts) for i in range(contexts)],
        "tensor": [(i, (i + 2) % tensors) for i in range(tensors)],
    }
    count = {"shard": shards, "context": contexts, "tensor": sides}
    twin = [(i, i ^ 1) for i in range(tensors)]
    plane = ("context", "tensor")

    def hop(value, axis):
        return lax.ppermute(value, axis, ring[axis])

    def swap(value):
        return lax.ppermute(value, "tensor", twin)

    def around(value, axis):
        out = [value]
        for _ in range(count[axis] - 1):
            out.append(hop(out[-1], axis))
        return out

    def fence(*values):
        return lax.optimization_barrier(values)

    to_owner = []
    to_home = {far: [] for far in range(sides)}
    for c in range(contexts):
        for s in range(sides):
            for k in range(2):
                here = c * tensors + 2 * s + k
                source = 2 * (c % half) + k
                to_owner.append((source * tensors + 2 * s + c // half, here))
                for far in range(sides):
                    there = (s + far) % sides
                    to_home[far].append((here, source * tensors + 2 * there + c // half))

    ringed = contexts == 2 and sides == 2 and shards == 4
    cross = {0: [], 1: []}
    if ringed:
        for c in range(2):
            for s in range(2):
                for k in range(2):
                    here = c * tensors + 2 * s + k
                    along = c * tensors + 2 * (1 - s) + k
                    aside = (1 - c) * tensors + 2 * s + k
                    cross[0].append((here, along if k == 0 else aside))
                    cross[1].append((here, aside if k == 0 else along))

    def block_of(array, index):
        return lax.dynamic_index_in_dim(array, index, 0, keepdims=False)

    def deliver(value, pairs):
        stay = np.zeros(contexts * tensors, np.int32)
        for a, b in pairs:
            stay[a] = a == b
        got = lax.ppermute(value, plane, [(a, b) for a, b in pairs if a != b])
        if not stay.any():
            return got
        return jnp.where(jnp.asarray(stay)[context * tensors + tensor] == 1, value, got)

    def stays(value, other):
        return jnp.where(core == context, value, other)

    relay = [[], []]
    for c in range(2 if ringed else 0):
        for s in range(2):
            for k in range(2):
                here = c * tensors + 2 * s + k
                along = c * tensors + 2 * (1 - s) + k
                relay[0].append((here, along if k == c else (1 - c) * tensors + 2 * s + 1 - k))
                if k != c:
                    relay[1].append((here, along))

    def send_first(value):
        if ringed:
            return [lax.ppermute(value, plane, relay[0])]
        return [deliver(value, to_home[far]) for far in range(sides)]

    def send_second(value, got):
        if ringed:
            return [got[0], stays(value, lax.ppermute(got[0], plane, relay[1]))]
        return got

    def pair_up(a, b):
        return jnp.concatenate([a, b], axis=0)

    def adapter_of(index, far):
        return block_of(index, 2 * ((side + far) % sides) + high)

    def up_packs(index, ups):
        chosen = jnp.stack([adapter_of(index, far) for far in range(sides)])
        packs = list(pick(chosen, ups))
        for far in range(1, sides):
            send = [(i, (i + 2 * far) % tensors) for i in range(tensors)]
            packs[far] = lax.ppermute(packs[far], "tensor", send)
        return packs

    attn_own = jnp.concatenate([w_qkv[:, j] for j in range(3)] + [w_proj], axis=1)
    ups = (qkv_up, fc1_up, jnp.transpose(proj_down, (0, 2, 1)), jnp.transpose(fc2_down, (0, 2, 1)))
    flows = {}

    def cross_to(value, turn):
        return lax.ppermute(value, plane, cross[turn])

    if ringed:
        z, b, c, d = [attn_own], [], [], []
        ff_own = pair_up(w_fc1, w_fc2)
        got = fence(
            hop(attn_own, "shard"),
            cross_to(attn_own, 0),
            cross_to(attn_own, 1),
            deliver(block_of(tokens, tensor), to_owner),
            hop(ff_own, "shard"),
            ff_own,
            cotangent,
            adapter_index,
            down_in,
            out_up,
            *ups,
        )
        z.append(got[0])
        b.append(got[1])
        c.append(got[2])
        x_own = got[3]
        own = [got[5], got[4]]
        cotangent, adapter_index, down_in, out_up = got[6:10]
        ups = got[10:]
        got = fence(
            hop(z[1], "shard"),
            cross_to(z[1], 0),
            cross_to(z[1], 1),
            cross_to(b[0], 1),
            cross_to(own[0], 0),
            x_own,
            own[1],
            adapter_index,
            *ups,
        )
        z.append(got[0])
        b.append(got[1])
        c.append(got[2])
        d.append(got[3])
        aside = [got[4]]
        x_own, own[1], adapter_index = got[5:8]
        ups = got[8:]
        got = fence(
            hop(z[2], "shard"),
            cross_to(z[2], 0),
            cross_to(z[2], 1),
            cross_to(b[1], 1),
            swap(x_own),
            x_own,
            own[1],
            aside[0],
        )
        z.append(got[0])
        b.append(got[1])
        c.append(got[2])
        d.append(got[3])
        x_other, x_own, own[1], aside[0] = got[4:]
        packs = up_packs(adapter_index, ups)
        own.append(hop(own[1], "shard"))
        got = fence(cross_to(z[3], 0), cross_to(z[3], 1), cross_to(b[2], 1), cotangent, packs[1])
        b.append(got[0])
        c.append(got[1])
        d.append(got[2])
        cotangent, packs[1] = got[3:]
        last = cross_to(b[3], 1)
        own_over, aside_over = [], []

        step_of = np.repeat(np.arange(shards), 4)
        near_0 = np.tile([0, 0, 1, 1], shards)
        far_0 = np.tile([0, 1, 0, 1], shards)
        near = jnp.where(core == 0, near_0, far_0)
        across = jnp.where(core == 0, far_0, near_0)
        row = (shard - step_of) % shards * contexts + (context - near) % contexts
        attn_place = jnp.stack([row, across]).astype(jnp.int32)
        attn_moves = [(k, 0, depth) for k in range(4 * shards)]
        ff_moves = [(k, which * depth, depth, which) for which in range(2) for k in range(4 * shards)]
        ff_place = jnp.concatenate([attn_place, attn_place], axis=1)

        def start(*values):
            got = fence(*values, last, own[0], aside[0], own[2])
            d.append(got[-4])
            own[0], aside[0], own[2] = got[-3:]
            aside.append(hop(aside[0], "shard"))
            own_over.append(cross_to(own[0], 1))
            aside_over.append(cross_to(aside[0], 1))
            return got[:-4]

        def advance(stage, *values):
            count = len(values)
            if stage == 0:
                got = fence(*values, own[2], aside[1], own_over[0], aside_over[0], cotangent)
                own[2], aside[1], own_over[0], aside_over[0], late_cotangent = got[count:]
                own.append(hop(own[2], "shard"))
                own_over.append(cross_to(own[1], 1))
                flows["gy"] = deliver(block_of(late_cotangent, tensor), to_owner)
            elif stage == 1:
                got = fence(*values, own[3], own[2], aside[1])
                own[3], own[2], aside[1] = got[count:]
                aside.append(hop(aside[1], "shard"))
                aside_over.append(cross_to(aside[1], 1))
                own_over.append(cross_to(own[2], 1))
            elif stage == 2:
                got = fence(
                    *values, aside[2], own_over[1], own_over[2], aside_over[1], own[3], flows["gy"]
                )
                aside[2], own_over[1], own_over[2], aside_over[1], own[3], flows["gy"] = got[count:]
                aside.append(hop(aside[2], "shard"))
                own_over.append(cross_to(own[3], 1))
                aside_over.append(cross_to(aside[2], 1))
            else:
                got = fence(*values, aside[3], own_over[3], aside_over[2])
                aside[3], own_over[3], aside_over[2] = got[count:]
                aside_over.append(cross_to(aside[3], 1))
            return got[:count]

    else:

        def gather_plain(value):
            whole = lax.all_gather(value, ("shard", "context"), axis=0, tiled=True)
            return around(whole, "tensor")

        attn_parts = gather_plain(attn_own)
        fc1_parts = gather_plain(w_fc1)
        fc2_parts = gather_plain(w_fc2)
        packs = up_packs(adapter_index, ups)
        x_own = deliver(block_of(tokens, tensor), to_owner)
        x_other = swap(x_own)
        flows["gy"] = deliver(block_of(cotangent, tensor), to_owner)
        attn_moves = [(k, 0, model) for k in range(sides)]
        attn_place = jnp.asarray([[0] * sides, list(range(sides))], jnp.int32)
        ff_moves = [(k, 0, model, k // sides) for k in range(2 * sides)]
        ff_place = jnp.concatenate([attn_place, attn_place], axis=1)

        def start(*values):
            return values

        def advance(stage, *values):
            return values

    mine = adapter_of(adapter_index, 0)
    down = block_of(down_in, mine)
    down_t = jnp.transpose(down, (0, 2, 1)).reshape(4 * rank, model)
    out_t = block_of(out_up, mine)

    x_all = pair_up(x_own, x_other).astype(F32)
    normed, unit_one, inverse_one = normalize(x_all, ln1_gain, ln1_bias)
    n1 = normed.astype(BF16)
    u = dot_nt(down_t[: 3 * rank], n1).astype(BF16)
    qkv_lift, fc1_lift, proj_t, fc2_t = lifts(packs, width, hidden)
    n1, u, qkv_lift = start(n1, u, qkv_lift)
    if ringed:
        attn_parts = [part for i in range(shards) for part in (z[i], b[i], c[i], d[i])]
    w_in, w_out, qkv = project(n1, u, qkv_lift, attn_parts, attn_moves, attn_place, width)
    (qkv,) = advance(0, qkv)

    steps = [[h * half + i for i in range(half)] for h in range(2)]
    per_side = width // PAIR
    pairs = per_side * sides
    near, group_count = (per_side, sides) if half == 1 else (1, pairs // half)

    def to_heads(array, thirds_each):
        if half == 1:
            return array
        cells = array.reshape(array.shape[0], sides, thirds_each, per_side, PAIR)
        cells = jnp.transpose(cells, (0, 1, 3, 2, 4)).reshape(array.shape[0], pairs, -1)
        moved = lax.all_to_all(cells, "context", 1, 0, axis_index_groups=steps, tiled=True)
        return moved.reshape(moved.shape[0], -1)

    def to_rows(array, thirds_each):
        if half == 1:
            return array
        cells = array.reshape(array.shape[0], pairs // half, -1)
        moved = lax.all_to_all(cells, "context", 0, 1, axis_index_groups=steps, tiled=True)
        moved = moved.reshape(moved.shape[0], sides, per_side, thirds_each, PAIR)
        return jnp.transpose(moved, (0, 1, 3, 2, 4)).reshape(moved.shape[0], -1)

    qkv_heads = to_heads(qkv, 3)
    o_heads = None
    logs = []
    for group in range(group_count):
        o_heads, lse = attend(qkv_heads, group, near, o_heads)
        logs.append(lse)
        if group == 0:
            o_heads, qkv_heads = advance(1, o_heads, qkv_heads)
    (o_heads,) = advance(2, o_heads)
    gy_own = flows["gy"]
    o = to_rows(o_heads, 1)
    attn_far = dot_nt(o[rows:], w_out)
    c_part = dot_nt(proj_t, o)
    attn_sum = swap(attn_far) + dot_nt(o[:rows], w_out)
    c_own = (c_part[:, :rows] + swap(c_part[:, rows:])).astype(BF16)
    h = x_all[:rows] + layer_scale[0] * (attn_sum + dot_tn(c_own, out_t[0]))
    normed, unit_two, inverse_two = normalize(h, ln2_gain, ln2_bias)
    n2_own = normed.astype(BF16)
    gb_own = (gy_own.astype(F32) * layer_scale[1]).astype(BF16)
    gb = pair_up(gb_own, swap(gb_own))
    n2_own, gb = advance(3, n2_own, gb)
    n2_far = swap(n2_own)
    if ringed:
        ff_parts = [
            part
            for i in range(shards)
            for part in (own[i], aside[i], own_over[i], aside_over[i])
        ]
    else:
        ff_parts = fc1_parts + fc2_parts
    branch_own, branch_far, gn2_own, gn2_far, rank_own, rank_far, g_fc1, g_fc2 = mlp(
        n2_own, n2_far, gb, down_t[3 * rank :], out_t[1], ff_parts, ff_moves, ff_place, fc1_lift, fc2_t
    )
    ranks = (rank_own + swap(rank_far)).astype(BF16)
    ranks, gn2_far, branch_far = fence(ranks, gn2_far, branch_far)
    m_own, gf_own = ranks[:rank], ranks[rank:]
    branch = branch_own + swap(branch_far).astype(F32) + dot_tn(m_own, out_t[1])
    result_own = (h + layer_scale[1] * branch).astype(BF16)
    gn2 = gn2_own + swap(gn2_far) + dot_tn(gf_own, down_t[3 * rank :])
    g_out1 = dot(m_own, gb[:rows])
    g_down3 = dot(gf_own, n2_own)

    cut = model // 2
    one = jnp.where(context % half == 0, mine, 0)
    mark = jnp.full((rank, 128), one).astype(BF16)

    def halves(shared):
        shared = jnp.stack(shared)
        away = lax.dynamic_slice_in_dim(shared, (1 - core) * cut, cut, 2)
        keep = lax.dynamic_slice_in_dim(shared, core * cut, cut, 2)
        both = keep + swap(away)
        return [both[j] for j in range(len(both))]

    def to_sides(slices, shared):
        packed = []
        for far in range(sides):
            pack = jnp.concatenate([part.astype(BF16) for part in slices[far] + shared] + [mark], axis=1)
            if far:
                send = [(i, (i - 2 * far) % tensors) for i in range(tensors)]
                pack = lax.ppermute(pack, "tensor", send)
            packed.append(pack)
        return jnp.stack(packed)

    opposite = [(i, (i + half) % contexts) for i in range(contexts)]

    def merge(block):
        if half == 1:
            return block
        total = lax.psum(block.astype(F32), "context", axis_index_groups=steps)
        return total.astype(BF16)

    def over(block):
        return lax.ppermute(block, "context", opposite)

    def columns(array, far, size):
        return array[:, far * size : (far + 1) * size]

    early = to_sides(
        [[columns(g_fc1, far, hidden), columns(g_fc2, far, hidden)] for far in range(sides)],
        halves([g_down3, g_out1]),
    )
    gh = gy_own.astype(F32) + norm_back(gn2, unit_two, inverse_two, ln2_gain)
    gattn_own = (layer_scale[0] * gh).astype(BF16)
    gattn_far, early = fence(swap(gattn_own), early)
    gattn = pair_up(gattn_own, gattn_far)
    early_line = [merge(early)]
    early_line.append(hop(early_line[0], "shard"))
    early_over = [over(early_line[0])]
    g_out0 = dot(c_own, gattn_own)
    gc = dot_nt(out_t[0], gattn).astype(BF16)
    g_proj = dot(gc, o)
    mid = to_sides([[columns(g_proj, far, width)] for far in range(sides)], halves([g_out0]))
    go = (dot(gattn, w_out) + dot_tn(gc, proj_t)).astype(BF16)
    early_line[1], early_over[0], mid, go, result_own = fence(
        early_line[1], early_over[0], mid, go, result_own
    )
    early_line.append(hop(early_line[1], "shard"))
    early_over.append(over(early_line[1]))
    mid = merge(mid)
    mid_over = over(mid)
    sent = send_first(result_own)
    go_heads = to_heads(go, 1)
    g_heads = None
    for group in range(group_count):
        g_heads = attend_back(qkv_heads, go_heads, o_heads, logs[group], group, near, g_heads)
        if group == 0:
            g_heads, mid_over, early_line[2], *sent = fence(
                g_heads, mid_over, early_line[2], *sent
            )
            early_over.append(over(early_line[2]))
            for _ in range(3, shards):
                early_line.append(hop(early_line[-1], "shard"))
            mid_line = [pair_up(mid, mid_over)]
            mid_line.append(hop(mid_line[0], "shard"))
            sent = send_second(result_own, sent)
    g_heads, mid_line[1], early_over[1], early_over[2], *early_line[3:] = fence(
        g_heads, mid_line[1], early_over[1], early_over[2], *early_line[3:]
    )
    early_over.extend([over(block) for block in early_line[3:]])
    mid_line.append(hop(mid_line[1], "shard"))
    g = to_rows(g_heads, 3)

    gu_part = dot_nt(qkv_lift, g)
    gu_own = (gu_part[:, :rows] + swap(gu_part[:, rows:])).astype(BF16)
    gn1_far = swap(dot_nt(g[rows:], w_in))
    g_up = dot(u, g)
    gn1 = dot_nt(g[:rows], w_in) + gn1_far + dot_tn(gu_own, down_t[: 3 * rank])
    g_down = dot(gu_own, n1[:rows])
    late_slices = [
        [
            g_up[j * rank : (j + 1) * rank, (far * 3 + j) * width : (far * 3 + j + 1) * width]
            for j in range(3)
        ]
        for far in range(sides)
    ]
    late = to_sides(late_slices, halves([g_down[j * rank : (j + 1) * rank] for j in range(3)]))
    input_own = gh + norm_back(gn1, unit_one[:rows], inverse_one[:rows], ln1_gain)
    input_own = input_own.astype(BF16)
    late_line = [merge(late)]
    late_line.append(hop(late_line[0], "shard"))
    late_over = [over(late_line[0])]
    last_over = early_over[3:]
    late_line[1], late_over[0], input_own, mid_line[2], *got = fence(
        late_line[1], late_over[0], input_own, mid_line[2], *last_over, *sent
    )
    early_over[3:], sent = got[: len(last_over)], got[len(last_over) :]

    order = np.tile(np.arange(sides), 2)
    flip = np.repeat([0, 1], sides)
    far = jnp.where((core ^ flip) == context, 1 - order, order) if ringed else order
    where = (2 * ((side - far) % sides) + (core ^ flip)).astype(jnp.int32)
    late_line.append(hop(late_line[1], "shard"))
    input_sent = send_first(input_own)
    for _ in range(3, shards):
        mid_line.append(hop(mid_line[-1], "shard"))
    sent = list(sent) + [swap(part) for part in sent]
    fc1_grad, fc2_grad, early_half = totals(
        early_line + early_over, (hidden, hidden, 2 * cut), adapters
    )
    late_line[1], late_line[2], early_half, *got = fence(
        late_line[1], late_line[2], early_half, *sent, *mid_line
    )
    sent, mid_line = got[: 2 * sides], got[2 * sides :]
    for _ in range(3, shards):
        late_line.append(hop(late_line[-1], "shard"))
    late_over.append(over(late_line[1]))
    early_twin = swap(early_half)
    result = settle(sent, where, 0, 1, BF16, images)
    proj_grad, mid_half = totals(mid_line, (width, cut), adapters)
    late_line[-1], late_over[1], early_half, early_twin, mid_half, result, *input_sent = fence(
        late_line[-1], late_over[1], early_half, early_twin, mid_half, result, *input_sent
    )
    late_over.extend([over(block) for block in late_line[2:]])
    first_twin = swap(input_sent[0])
    input_sent = send_second(input_own, input_sent)
    mid_twin = swap(mid_half)
    input_grad = settle([input_sent[0], first_twin], where, 0, sides, F32, images)
    out_grad = spread(
        core, [mid_half, mid_twin, early_half, early_twin], ((0, 0), (1, 1)), cut
    )
    late_line[0], input_grad, out_grad, *late_over = fence(
        late_line[0], input_grad, out_grad, *late_over
    )
    qkv_grad, late_half = totals(late_line + late_over, (3 * width, 3 * cut), adapters, 3)
    late_half, qkv_grad, *input_sent = fence(late_half, qkv_grad, *input_sent)
    late_twin = swap(late_half)
    last_twins = [swap(part) for part in input_sent[1:]]
    input_grad = settle(input_sent[1:] + last_twins, where, 1, sides, F32, images, input_grad)
    down_grad = spread(
        core,
        [late_half, late_twin, early_half, early_twin],
        ((0, 0), (0, 1), (0, 2), (1, 0)),
        cut,
    )
    return (
        result,
        input_grad,
        jnp.transpose(down_grad, (0, 1, 3, 2)),
        qkv_grad,
        fc1_grad,
        jnp.transpose(proj_grad, (0, 2, 1)),
        jnp.transpose(fc2_grad, (0, 2, 1)),
        out_grad,
    )


def solution(mesh):
    sizes = (mesh.shape["shard"], mesh.shape["context"], mesh.shape["tensor"])
    placed = (
        P("shard", "context", None),
        P("shard", "context", None),
        P("shard"),
        P(),
        P(),
        P(),
        P(),
        P(),
        P(("shard", "context"), None, "tensor"),
        P(("shard", "context"), "tensor"),
        P(("shard", "context"), "tensor"),
        P(("shard", "context"), "tensor"),
        P(),
        P(None, None, None, "tensor"),
        P(None, None, "tensor"),
        P(None, "tensor", None),
        P(None, "tensor", None),
        P(),
    )
    return jax.shard_map(
        functools.partial(per_device, sizes),
        mesh=mesh,
        in_specs=placed,
        out_specs=(
            P("shard", "context", None),
            P("shard", "context", None),
            P(),
            P(None, None, None, "tensor"),
            P(None, None, "tensor"),
            P(None, "tensor", None),
            P(None, "tensor", None),
            P(),
        ),
        check_vma=False,
    )
```
